128 devices in a mesh: dp: 8 (over y_hi, z), tm: 16 (over y_lo, x, core).
Axes of the slice: x: 4, y: 4 (y_hi: 2, y_lo: 2; y = y_hi * 2 + y_lo), z: 4, core: 2. Of those that a mesh axis runs over, the one named last changes fastest.
Arguments:
- frames: bfloat16 [8, 4096, 1536], P('dp', 'tm'), may hold values from -6 to 6
- cotangent: bfloat16 [8, 4096, 1536], P('dp', 'tm'), may hold values from -6 to 6
- layer_norm_gain: float32 [1536], replicated, may hold values from 0.1 to 1.9
- w_query: bfloat16 [1536, 768], P('dp'), may hold values from -0.12757759 to 0.12757759
- w_key: bfloat16 [1536, 768], P('dp'), may hold values from -0.12757759 to 0.12757759
- w_value: bfloat16 [1536, 768], P('dp'), may hold values from -0.15625 to 0.15625
- w_out: bfloat16 [768, 1536], P('dp'), may hold values from -0.21875 to 0.21875
- lengths: int32 [8], P('dp'), may hold values from 2048 to 4096
- win_lo: int32 [8, 4096], P('dp', 'tm'), may hold values from 0 to 4095, as said below
- win_hi: int32 [8, 4096], P('dp', 'tm'), may hold values from 1 to 4096, as said below
Outputs:
- frames_out: bfloat16 [8, 4096, 1536], P('dp', 'tm')
- grad_frames: bfloat16 [8, 4096, 1536], P('dp', 'tm')
- grad_w_query: float32 [1536, 768], P(('dp', 'tm'))
- grad_w_key: float32 [1536, 768], P(('dp', 'tm'))
- grad_w_value: float32 [1536, 768], P(('dp', 'tm'))
- grad_w_out: float32 [768, 1536], P(('dp', 'tm'))
- grad_gain: float32 [1536], P(('dp', 'tm'))
The draws below stay inside these ranges and needn't reach their ends.
Inputs may be any that keep to these rules, and one draw needn't show every extreme that they name: win_lo[b, t] lies between t - 128 and t, and equals t - 128 at some frames of every utterance. win_hi[b, t] lies between t + 1 and t + 129, and equals t + 129 at some frames of every utterance. frames from lengths[b] on are padding.
All inputs are finite; a program needn't handle non-finite values.
Results may differ from the reference program's by a relative error of at most 0.035.
The reference program's roundings to bfloat16 on the way count: a program that leaves them out, or rounds other values in their place, can miss the bound.
Values may be sent and summed in bfloat16 or wider, within the bound.
A program may use at most 128 MiB of HBM per device.

```python
import jax
import jax.numpy as jnp
from jax import lax

D = 1536
HEADS = 12
HEAD_DIM = 64
REACH = 128
T_DEV = 256
HD = 768
FRAMES = 4096
BATCH = 8


def window_reach(key, which):
    sub = jax.random.fold_in(key, 7001 + which)
    reach = jax.random.randint(sub, (BATCH, FRAMES), 0, REACH + 1)
    position = jnp.arange(FRAMES, dtype=jnp.int32)[None, :]
    widest = position % 16 == which * 8
    return (jnp.where(widest, REACH, reach).astype(jnp.int32), position)


def draw_win_lo(key, part):
    reach, position = window_reach(key, 0)
    return jnp.maximum(position - reach, 0).astype(jnp.int32)


def draw_win_hi(key, part):
    reach, position = window_reach(key, 1)
    return jnp.minimum(position + 1 + reach, FRAMES).astype(jnp.int32)


def projection_draw(key, which):
    base = jax.random.truncated_normal(jax.random.fold_in(key, which), -4.0, 4.0, (D, HD), jnp.float32)
    base = base * D ** (-0.5)
    return base.astype(jnp.bfloat16)


def draw_w_query(key, part):
    return projection_draw(key, 31)


def draw_w_key(key, part):
    return projection_draw(key, 32)


def draw_frames(key, part):
    noise = jax.random.truncated_normal(jax.random.fold_in(key, 41), -6.0, 6.0, (BATCH, FRAMES, D), jnp.float32)
    result = noise
    return result.astype(jnp.bfloat16)


def with_ends(entries, rng, least, high):
    longest = entries.shape.index(max(entries.shape))
    spots = []
    for shift in (0, 1):
        where = [jax.random.randint(jax.random.fold_in(rng, axis), (), 0, length) for axis, length in enumerate(entries.shape)]
        where[longest] = (where[longest] + shift) % entries.shape[longest]
        spots.append(tuple(where))
    return entries.at[spots[0]].set(least).at[spots[1]].set(high)


def with_spikes(array, rng, source, target, blocks, factor):
    def block_of(axis_at):
        return (jnp.arange(array.shape[axis_at]) // (array.shape[axis_at] // blocks)).reshape((-1,) + (1,) * (array.ndim - 1 - axis_at))

    one_side = jax.random.permutation(rng, blocks)[block_of(target)]
    far = (block_of(target) + blocks // 2) % blocks
    return jnp.where((block_of(source) == one_side) | (block_of(source) == far), factor * array, array)


def block_levels(own_key, shape, cuts, smallest, top_value):
    factor_of, own = 1.0, jax.random.fold_in(own_key, 6)
    for dim, shards_of in cuts:
        draws = jnp.exp(jax.random.uniform(jax.random.fold_in(own, dim), (shards_of,), jnp.float32, smallest / len(cuts), top_value / len(cuts)))
        factor_of = factor_of * jnp.repeat(draws, shape[dim] // shards_of).reshape([-1 if axis == dim else 1 for axis in range(len(shape))])
    return factor_of


def gaussian(own_key, extent, deviation, most, cuts=(), held_as=jnp.bfloat16):
    drawn = deviation * jax.random.normal(own_key, extent, jnp.float32)
    if cuts:
        drawn = drawn * block_levels(own_key, extent, cuts, -0.22, 0.18)
    return jnp.clip(drawn, -most, most).astype(held_as)


def bell_draw_with(key, shape, scale, most, pieces, heavy, held_as=jnp.bfloat16):
    array = scale * jax.random.normal(key, shape, jnp.float32)
    if pieces:
        array = array * block_levels(key, shape, pieces, -0.22, 0.18)
    return jnp.clip(with_spikes(array, jax.random.fold_in(key, 3), *heavy), -most, most).astype(held_as)


def setup_inputs(seed: int = 0) -> dict:
    keys = jax.random.split(jax.random.key(seed), 11)
    return {
        "frames": draw_frames(jax.random.fold_in(keys[10], 71), 0),
        "cotangent": bell_draw_with(keys[1], (BATCH, FRAMES, D), 1.0, 6.0, ((0, 8), (1, 16)), (1, 2, 16, 2.0)),
        "layer_norm_gain": jnp.clip(1.0 + 0.18 * jax.random.normal(keys[2], (D,), jnp.float32), 0.1, 1.9),
        "w_query": draw_w_query(jax.random.fold_in(keys[10], 71), 0),
        "w_key": draw_w_key(jax.random.fold_in(keys[10], 71), 0),
        "w_value": gaussian(keys[5], (D, HD), D ** -0.5, 0.15625, ((0, 8),)),
        "w_out": gaussian(keys[6], (HD, D), HD ** -0.5, 0.21875, ((0, 8),)),
        "lengths": with_ends(jax.random.randint(keys[7], (BATCH,), FRAMES // 2, FRAMES + 1), jax.random.fold_in(keys[7], 1), FRAMES // 2, FRAMES).astype(jnp.int32),
        "win_lo": draw_win_lo(jax.random.fold_in(keys[10], 71), 0),
        "win_hi": draw_win_hi(jax.random.fold_in(keys[10], 71), 0),
    }


def layer_normalize(input_rows, norm_gain):
    xf = input_rows.astype(jnp.float32)
    feature_mean = lax.optimization_barrier(jnp.mean(xf, -1, keepdims=True))
    centered_input = xf - feature_mean
    var = lax.optimization_barrier(jnp.mean(centered_input * centered_input, -1, keepdims=True))
    inverse_deviation = lax.rsqrt(var + 1e-05)
    standardized_input = centered_input * inverse_deviation
    return ((standardized_input * norm_gain).astype(jnp.bfloat16), standardized_input, inverse_deviation)

def layer_normalize_backward(normalized_gradient, standardized_input, inverse_deviation, norm_gain):
    scaled_output = normalized_gradient * norm_gain
    gain_gradient = lax.optimization_barrier(jnp.sum(normalized_gradient * standardized_input, 0))
    first_term = lax.optimization_barrier(jnp.mean(scaled_output, -1, keepdims=True))
    second_term = lax.optimization_barrier(jnp.mean(scaled_output * standardized_input, -1, keepdims=True))
    return (inverse_deviation * (scaled_output - first_term - standardized_input * second_term), gain_gradient)

def window_mask(lo, hi, length, qpos, kpos):
    kp = kpos[None, :]
    inside = (kp >= lo[:, None]) & (kp < hi[:, None]) & (kp < length)
    return inside | (kp == qpos[:, None])

def split_heads(a):
    return a.reshape(a.shape[0], HEADS, HEAD_DIM).astype(jnp.float32)

def attend(query, key, value, mask):
    scale = HEAD_DIM ** (-0.5)
    scores = jnp.einsum('qhe,khe->hqk', split_heads(query), split_heads(key)) * scale
    scores = jnp.where(mask[None], scores, -1e+30)
    expo = jnp.exp(scores - lax.optimization_barrier(jnp.max(scores, -1, keepdims=True)))
    probs = expo / lax.optimization_barrier(jnp.sum(expo, -1, keepdims=True))
    probs_low = probs.astype(jnp.bfloat16)
    context = jnp.einsum('hqk,khe->qhe', probs_low.astype(jnp.float32), split_heads(value))
    return (context.reshape(query.shape[0], HEADS * HEAD_DIM).astype(jnp.bfloat16), probs, probs_low)

def attend_back(query, key, value, probs, probs_low, grad_context):
    scale = HEAD_DIM ** (-0.5)
    grad_heads = split_heads(grad_context)
    grad_value = jnp.einsum('hqk,qhe->khe', probs_low.astype(jnp.float32), grad_heads)
    grad_probs = jnp.einsum('qhe,khe->hqk', grad_heads, split_heads(value))
    delta = lax.optimization_barrier(jnp.sum(probs * grad_probs, -1, keepdims=True))
    grad_scores = (probs * (grad_probs - delta)).astype(jnp.bfloat16).astype(jnp.float32)
    grad_query = jnp.einsum('hqk,khe->qhe', grad_scores, split_heads(key)) * scale
    grad_key = jnp.einsum('hqk,qhe->khe', grad_scores, split_heads(query)) * scale
    width = HEADS * HEAD_DIM
    return (grad_query.reshape(query.shape[0], width).astype(jnp.bfloat16), grad_key.reshape(key.shape[0], width), grad_value.reshape(key.shape[0], width))

def reference(frames, cotangent, layer_norm_gain, w_query, w_key, w_value, w_out, lengths, win_lo, win_hi):
    width = HEADS * HEAD_DIM
    blocks = FRAMES // T_DEV
    span = T_DEV + 2 * REACH
    grad_wq = jnp.zeros((D, width), jnp.float32)
    grad_wk = jnp.zeros((D, width), jnp.float32)
    grad_wv = jnp.zeros((D, width), jnp.float32)
    grad_wo = jnp.zeros((width, D), jnp.float32)
    grad_gain = jnp.zeros((D,), jnp.float32)
    outputs = []
    input_grads = []
    for utter in range(BATCH):
        input_rows = frames[utter]
        grad_y = cotangent[utter]
        length = lengths[utter]
        lo_row = win_lo[utter]
        hi_row = win_hi[utter]
        normalized_input, standardized_input, inverse_deviation = layer_normalize(input_rows, layer_norm_gain)
        query = jnp.dot(normalized_input, w_query, preferred_element_type=jnp.float32).astype(jnp.bfloat16)
        key = jnp.dot(normalized_input, w_key, preferred_element_type=jnp.float32).astype(jnp.bfloat16)
        value = jnp.dot(normalized_input, w_value, preferred_element_type=jnp.float32).astype(jnp.bfloat16)
        padded = jnp.pad(jnp.concatenate([key, value], 1), ((REACH, REACH), (0, 0)))

        def block_parts(index):
            start = (index * T_DEV).astype(jnp.int32)
            q_block = lax.dynamic_slice_in_dim(query, start, T_DEV, 0)
            kv_block = lax.dynamic_slice_in_dim(padded, start, span, 0)
            qpos = start + jnp.arange(T_DEV, dtype=jnp.int32)
            kpos = start - REACH + jnp.arange(span, dtype=jnp.int32)
            lo_block = lax.dynamic_slice_in_dim(lo_row, start, T_DEV, 0)
            hi_block = lax.dynamic_slice_in_dim(hi_row, start, T_DEV, 0)
            mask = window_mask(lo_block, hi_block, length, qpos, kpos)
            return (q_block, kv_block[:, :width], kv_block[:, width:], mask, start)

        def forward_block(index):
            q_block, k_block, v_block, mask, start = block_parts(index)
            return attend(q_block, k_block, v_block, mask)[0]
        indices = jnp.arange(blocks, dtype=jnp.int32)
        context = lax.map(forward_block, indices).reshape(FRAMES, width)
        attn = jnp.dot(context, w_out, preferred_element_type=jnp.float32)
        valid = jnp.arange(FRAMES, dtype=jnp.int32) < length
        outputs.append((input_rows.astype(jnp.float32) + jnp.where(valid[:, None], attn, 0.0)).astype(jnp.bfloat16))
        masked_grad = jnp.where(valid[:, None], grad_y, jnp.zeros_like(grad_y))
        grad_wo = grad_wo + jnp.dot(context.T, masked_grad, preferred_element_type=jnp.float32)
        grad_context = jnp.dot(masked_grad, w_out.T, preferred_element_type=jnp.float32).astype(jnp.bfloat16)

        def backward_block(carry, index):
            q_block, k_block, v_block, mask, start = block_parts(index)
            unused, probs, probs_low = attend(q_block, k_block, v_block, mask)
            grad_block = lax.dynamic_slice_in_dim(grad_context, start, T_DEV, 0)
            grad_q, grad_k, grad_v = attend_back(q_block, k_block, v_block, probs, probs_low, grad_block)
            old = lax.dynamic_slice_in_dim(carry, start, span, 0)
            carry = lax.dynamic_update_slice_in_dim(carry, old + jnp.concatenate([grad_k, grad_v], 1), start, 0)
            return (carry, grad_q)
        total, grad_blocks = lax.scan(backward_block, jnp.zeros((FRAMES + 2 * REACH, 2 * width), jnp.float32), indices)
        grad_query = grad_blocks.reshape(FRAMES, width)
        grad_kv = total[REACH:REACH + FRAMES].astype(jnp.bfloat16)
        grad_key = grad_kv[:, :width]
        grad_value = grad_kv[:, width:]
        grad_wq = grad_wq + jnp.dot(normalized_input.T, grad_query, preferred_element_type=jnp.float32)
        grad_wk = grad_wk + jnp.dot(normalized_input.T, grad_key, preferred_element_type=jnp.float32)
        grad_wv = grad_wv + jnp.dot(normalized_input.T, grad_value, preferred_element_type=jnp.float32)
        normalized_gradient = jnp.dot(grad_query, w_query.T, preferred_element_type=jnp.float32) + jnp.dot(grad_key, w_key.T, preferred_element_type=jnp.float32) + jnp.dot(grad_value, w_value.T, preferred_element_type=jnp.float32)
        layer_norm_gradient, gain_product = layer_normalize_backward(normalized_gradient, standardized_input, inverse_deviation, layer_norm_gain)
        grad_gain = grad_gain + gain_product
        input_grads.append((grad_y.astype(jnp.float32) + layer_norm_gradient).astype(jnp.bfloat16))
    return (jnp.stack(outputs, 0), jnp.stack(input_grads, 0), grad_wq, grad_wk, grad_wv, grad_wo, grad_gain)
```

```python
import jax
import jax.numpy as jnp
from jax import lax
from jax.experimental import pallas as pl
from jax.experimental.pallas import tpu as pltpu

from jax.sharding import PartitionSpec as P

MESH = pl.DeviceIdType.MESH
BF = jnp.bfloat16
F32 = jnp.float32


class Place:
    def __init__(self):
        dp, tm = lax.axis_index("dp"), lax.axis_index("tm")
        self.yh, self.z = dp // 4, lax.rem(dp, 4)
        self.yl, self.x, self.core = tm // 8, lax.rem(tm // 2, 4), lax.rem(tm, 2)
        self.y = self.yh * 2 + self.yl

    def at(self, axis):
        return {"x": self.x, "y": self.y, "z": self.z}[axis]

    def device(self, axis=None, j=None):
        y, z, x, core = self.y, self.z, self.x, self.core
        if axis == "x":
            x = j
        elif axis == "y":
            y = j
        elif axis == "z":
            z = j
        else:
            core = 1 - core
        return ((y // 2) * 4 + z, (lax.rem(y, 2) * 4 + x) * 2 + core)

    def right(self, axis):
        return lax.rem(self.at(axis) + 1, 4)

    def left(self, axis):
        return lax.rem(self.at(axis) + 3, 4)

    def over(self, axis):
        return lax.rem(self.at(axis) + 2, 4)


def greet(me):
    barrier = pltpu.get_barrier_semaphore()
    for axis in "xyz":
        for j in (me.left(axis), me.right(axis)):
            pl.semaphore_signal(barrier, inc=1, device_id=me.device(axis, j), device_id_type=MESH)
    pl.semaphore_signal(barrier, inc=1, device_id=me.device(), device_id_type=MESH)
    pl.semaphore_wait(barrier, 7)


def gather_regions(me, w, h):
    return (
        (
            ("y", lambda j, p: w.at[j // 2, me.z, h, 0, lax.rem(j, 2), pl.ds(2 * p, 2)]),
            ("z", lambda j, p: w.at[p, j, h, 0]),
        ),
        (
            ("z", lambda j, p: w.at[me.yh, j, h, 1, me.yl, pl.ds(2 * p, 2)]),
            ("y", lambda j, p: w.at[j // 2, pl.ds(2 * p, 2), h, 1, lax.rem(j, 2)]),
        ),
        (
            ("z", lambda j, p: w.at[me.yh, j, h, 2, me.yl, me.x, :, pl.ds(384 * p, 384)]),
            ("y", lambda j, p: w.at[j // 2, pl.ds(2 * p, 2), h, 2, lax.rem(j, 2), me.x]),
            ("x", lambda j, p: w.at[p, :, h, 2, :, j]),
        ),
    )


class GatherStage:
    def __init__(self, me, axis, region, other, send, recv, base):
        self.me, self.axis, self.region, self.other = me, axis, region, other
        self.send, self.recv, self.base = send, recv, base

    def hop(self, k, j, p, right):
        me, n = self.me, self.base + k
        to = me.right(self.axis) if right else me.left(self.axis)
        part = self.region(j, p)
        return pltpu.make_async_remote_copy(
            src_ref=part, dst_ref=part, send_sem=self.send.at[n], recv_sem=self.recv.at[n],
            device_id=me.device(self.axis, to), device_id_type=MESH)

    def share(self, k, j, p, region=None):
        n = self.base + 6 + k
        part = (region or self.region)(j, p)
        return pltpu.make_async_remote_copy(
            src_ref=part, dst_ref=part, send_sem=self.send.at[n], recv_sem=self.recv.at[n],
            device_id=self.me.device(), device_id_type=MESH)

    def start(self):
        i = self.me.at(self.axis)
        self.hop(0, i, 0, True).start()
        self.hop(1, i, 1, False).start()
        self.hop(2, i, 1, True).start()
        self.hop(3, i, 0, False).start()

    def relay(self):
        me = self.me
        l, r = me.left(self.axis), me.right(self.axis)
        self.hop(0, l, 0, True).wait_recv()
        self.hop(4, l, 0, True).start()
        self.share(0, l, 0).start()
        self.hop(1, r, 1, False).wait_recv()
        self.hop(5, r, 1, False).start()
        self.share(1, r, 1).start()

    def finish(self):
        me = self.me
        l, r, o = me.left(self.axis), me.right(self.axis), me.over(self.axis)
        self.hop(2, l, 1, True).wait_recv()
        self.share(2, l, 1).start()
        self.hop(3, r, 0, False).wait_recv()
        self.share(3, r, 0).start()
        self.hop(4, o, 0, True).wait_recv()
        self.share(4, o, 0).start()
        self.hop(5, o, 1, False).wait_recv()
        self.share(5, o, 1).start()

    def arrive(self):
        me = self.me
        l, r, o = me.left(self.axis), me.right(self.axis), me.over(self.axis)
        for k, (j, p) in enumerate(((l, 0), (r, 1), (l, 1), (r, 0), (o, 0), (o, 1))):
            self.share(k, j, p, self.other).wait_recv()

    def drain(self):
        me = self.me
        i, l, r, o = me.at(self.axis), me.left(self.axis), me.right(self.axis), me.over(self.axis)
        for k, (j, p, right) in enumerate(((i, 0, True), (i, 1, False), (i, 1, True), (i, 0, False), (l, 0, True), (r, 1, False))):
            self.hop(k, j, p, right).wait_send()
        for k, (j, p) in enumerate(((l, 0), (r, 1), (l, 1), (r, 0), (o, 0), (o, 1))):
            self.share(k, j, p).wait_send()


def gather_stages(me, w, send, recv):
    mine, theirs = gather_regions(me, w, me.core), gather_regions(me, w, 1 - me.core)
    stages, base = [], 0
    for colour, other in zip(mine, theirs):
        row = []
        for (axis, region), (_, other_region) in zip(colour, other):
            row.append(GatherStage(me, axis, region, other_region, send, recv, base))
            base += 12
        stages.append(row)
    return stages


GATHER_SEMS = 84


def run_gather(me, w_own, w, send, recv, local):
    own = (
        pltpu.make_async_copy(w_own.at[:, pl.ds(0, 2), me.yl], w.at[me.yh, me.z, :, pl.ds(0, 2), me.yl], local.at[0]),
        pltpu.make_async_copy(w_own.at[:, 2, me.yl, me.x], w.at[me.yh, me.z, :, 2, me.yl, me.x], local.at[1]),
    )
    for copy in own:
        copy.start()
    greet(me)
    for copy in own:
        copy.wait()
    a, b, c = gather_stages(me, w, send, recv)
    c[0].start()
    a[0].start()
    b[0].start()
    c[0].relay()
    c[0].finish()
    c[1].start()
    a[0].relay()
    b[0].relay()
    a[0].finish()
    a[1].start()
    b[0].finish()
    b[1].start()
    c[1].relay()
    c[1].finish()
    c[2].start()
    a[1].relay()
    b[1].relay()
    c[2].relay()
    a[1].finish()
    b[1].finish()
    c[2].finish()
    for row in (a, b, c):
        for stage in row:
            stage.arrive()
    for row in (a, b, c):
        for stage in row:
            stage.drain()


def gather_kernel(w_own, w, send, recv, local):
    run_gather(Place(), w_own, w, send, recv, local)


def gather_weights(own):
    return pl.pallas_call(
        gather_kernel,
        out_shape=jax.ShapeDtypeStruct((2, 4) + own.shape, BF),
        in_specs=[pl.BlockSpec(memory_space=pltpu.VMEM)],
        out_specs=pl.BlockSpec(memory_space=pltpu.VMEM),
        scratch_shapes=[
            pltpu.SemaphoreType.DMA((GATHER_SEMS,)),
            pltpu.SemaphoreType.DMA((GATHER_SEMS,)),
            pltpu.SemaphoreType.DMA((2,)),
        ],
        compiler_params=pltpu.CompilerParams(collective_id=0, has_side_effects=True, vmem_limit_bytes=40 << 20),
        name="gather_weights",
    )(own)


ORDERS = (("x", "y", "z"), ("y", "z", "x"), ("z", "x", "y"))
DIMS = {"y": 0, "z": 1, "x": 2}


class ReduceStage:
    def __init__(self, me, axis, load, count, out, bufs, sems, base):
        self.me, self.axis, self.load, self.count, self.out = me, axis, load, count, out
        self.sent, self.got = bufs
        self.send, self.recv = sems
        self.base = base

    def hop(self, k):
        me = self.me
        to = me.right(self.axis) if k % 2 == 0 else me.left(self.axis)
        return pltpu.make_async_remote_copy(
            src_ref=self.sent.at[k], dst_ref=self.got.at[k],
            send_sem=self.send.at[self.base + k], recv_sem=self.recv.at[self.base + k],
            device_id=me.device(self.axis, to), device_id_type=MESH)

    def each(self, body):
        if self.count == 1:
            body(0)
        else:
            @pl.loop(0, self.count)
            def _(m):
                body(m)

    def fill(self, k, j, p, extra=None):
        def body(m):
            v = self.load(j, p, m)
            if extra is not None:
                v = v + self.got[extra, m].astype(F32)
            self.sent[k, m] = v.astype(self.sent.dtype)
        self.each(body)
        self.hop(k).start()

    def start(self):
        me = self.me
        l, r, o = me.left(self.axis), me.right(self.axis), me.over(self.axis)
        self.fill(0, o, 0)
        self.fill(1, o, 1)
        self.fill(2, r, 1)
        self.fill(3, l, 0)

    def relay(self):
        me = self.me
        self.hop(0).wait_recv()
        self.fill(4, me.right(self.axis), 0, 0)
        self.hop(1).wait_recv()
        self.fill(5, me.left(self.axis), 1, 1)

    def finish(self):
        me = self.me
        i = me.at(self.axis)
        for k in (2, 3, 4, 5):
            self.hop(k).wait_recv()

        for p, a, b in ((0, 4, 3), (1, 2, 5)):
            def body(m, p=p, a=a, b=b):
                v = self.load(i, p, m) + self.got[a, m].astype(F32) + self.got[b, m].astype(F32)
                self.out(p, m, v)
            self.each(body)

    def drain(self):
        for k in range(6):
            self.hop(k).wait_send()


class GainSum:
    STEPS = (None, "x1", "x3", "y1", "y3", "z1", "z3")

    def __init__(self, me, total, got, send, recv):
        self.me, self.total, self.got, self.send, self.recv = me, total, got, send, recv

    def hop(self, s):
        me, step = self.me, self.STEPS[s]
        if step is None:
            device = me.device()
        else:
            i = me.at(step[0])
            j = 3 - i if step[1] == "3" else i + 1 - 2 * lax.rem(i, 2)
            device = me.device(step[0], j)
        return pltpu.make_async_remote_copy(
            src_ref=self.total.at[s], dst_ref=self.got.at[s], send_sem=self.send.at[s], recv_sem=self.recv.at[s],
            device_id=device, device_id_type=MESH)

    def start(self, s):
        self.hop(s).start()

    def finish(self, s):
        self.hop(s).wait_recv()
        self.total[s + 1] = self.total[s] + self.got[s]

    def drain(self):
        for s in range(7):
            self.hop(s).wait_send()


def reduce_scratch():
    sem = pltpu.SemaphoreType.DMA
    return [
        pltpu.VMEM((3, 4, 4, 4, 96, 128), BF),
        pltpu.VMEM((3, 6, 8, 96, 128), BF), pltpu.VMEM((3, 6, 8, 96, 128), BF),
        pltpu.VMEM((3, 6, 2, 96, 128), BF), pltpu.VMEM((3, 6, 2, 96, 128), BF),
        pltpu.VMEM((3, 6, 1, 48, 128), F32), pltpu.VMEM((3, 6, 1, 48, 128), F32),
        pltpu.VMEM((3, 4, 4, 96, 128), F32),
        pltpu.VMEM((3, 4, 96, 128), F32),
        pltpu.VMEM((2, 3, 96, 128), F32),
        pltpu.VMEM((8, 16, 128), F32), pltpu.VMEM((7, 16, 128), F32),
        sem((54,)), sem((54,)), sem((3,)), sem((3,)), sem((8,)), sem((8,)),
    ]


def reduce_stages(me, g_at, scratch):
    (r0, s1, d1, s2, d2, s3, d3, t1, t2, fin, gt, gg, send, recv, csend, crecv, gsend, grecv) = scratch

    def load1(c):
        axis = ORDERS[c][0]

        def load(j, p, m):
            a, b = 2 * p + m // 4, lax.rem(m, 4)
            at = {"x": (a, b, j), "y": (j, a, b), "z": (a, j, b)}[axis]
            return g_at(c, at) + r0[(c,) + at].astype(F32)
        return load

    def out1(c):
        def out(p, m, v):
            t1[c, 2 * p + m // 4, lax.rem(m, 4)] = v
        return out

    def load2(c):
        def load(j, p, m):
            return t1[c, 2 * p + m, j] if c == 2 else t1[c, j, 2 * p + m]
        return load

    def out2(c):
        def out(p, m, v):
            t2[c, 2 * p + m] = v
        return out

    def load3(c):
        def load(j, p, m):
            return t2[c, j, pl.ds(48 * p, 48)]
        return load

    def out3(c):
        def out(p, m, v):
            fin[me.core, c, pl.ds(48 * p, 48)] = v
        return out

    stages, base = [], 0
    for c in range(3):
        row = []
        for n, (load, out, bufs, count) in enumerate(
            ((load1, out1, (s1, d1), 8), (load2, out2, (s2, d2), 2), (load3, out3, (s3, d3), 1))
        ):
            row.append(ReduceStage(me, ORDERS[c][n], load(c), count, out(c), (bufs[0].at[c], bufs[1].at[c]), (send, recv), base))
            base += 6
        stages.append(row)
    return stages


def core_hop(me, g, scratch, c):
    r0, csend, crecv = scratch[0], scratch[14], scratch[15]
    return pltpu.make_async_remote_copy(
        src_ref=g.at[1 - me.core, c], dst_ref=r0.at[c], send_sem=csend.at[c], recv_sem=crecv.at[c],
        device_id=me.device(), device_id_type=MESH)


def run_reduce(me, g_at, hop0, scratch):
    fin, gt, gg, gsend, grecv = scratch[9], scratch[10], scratch[11], scratch[16], scratch[17]
    stages = reduce_stages(me, g_at, scratch)
    gain = GainSum(me, gt, gg, gsend, grecv)
    gain.start(0)
    for c in range(3):
        hop0(c).wait_recv()
        stages[c][0].start()
    gain.finish(0)
    gain.start(1)
    for c in range(3):
        stages[c][0].relay()
    gain.finish(1)
    gain.start(2)
    for n in range(3):
        for c in range(3):
            stages[c][n].finish()
            if n < 2:
                stages[c][n + 1].start()
        gain.finish(2 * n + 2)
        if n < 2:
            gain.start(2 * n + 3)
            for c in range(3):
                stages[c][n + 1].relay()
            gain.finish(2 * n + 3)
            gain.start(2 * n + 4)
    last = pltpu.make_async_remote_copy(
        src_ref=fin.at[me.core], dst_ref=fin.at[me.core], send_sem=gsend.at[7], recv_sem=grecv.at[7],
        device_id=me.device(), device_id_type=MESH)
    last.start()
    arrived = pltpu.make_async_remote_copy(
        src_ref=fin.at[1 - me.core], dst_ref=fin.at[1 - me.core], send_sem=gsend.at[7], recv_sem=grecv.at[7],
        device_id=me.device(), device_id_type=MESH)
    for c in range(3):
        hop0(c).wait_send()
        for n in range(3):
            stages[c][n].drain()
    gain.drain()
    last.wait_send()
    arrived.wait_recv()


def reduce_kernel(g, gain, out, gain_out, *scratch):
    me = Place()
    scratch[10][0] = gain[...]
    greet(me)

    def hop0(c):
        return core_hop(me, g, scratch, c)

    for c in range(3):
        hop0(c).start()
    run_reduce(me, lambda c, at: g[(me.core, c) + at].astype(F32), hop0, scratch)
    out[...] = scratch[9][...]
    gain_out[...] = scratch[10][7]


def reduce_grads(g, gain):
    vm = pl.BlockSpec(memory_space=pltpu.VMEM)
    return pl.pallas_call(
        reduce_kernel,
        out_shape=(jax.ShapeDtypeStruct((2, 3, 96, 128), F32), jax.ShapeDtypeStruct((16, 128), F32)),
        in_specs=[vm, vm],
        out_specs=(vm, vm),
        scratch_shapes=reduce_scratch(),
        compiler_params=pltpu.CompilerParams(collective_id=1, has_side_effects=True, vmem_limit_bytes=56 << 20),
        name="reduce_grads",
    )(g, gain)


def chunks(a, rows):
    a = a.reshape(2, 4, 2, 4, rows, 2, 3, a.shape[1] // 768 * 128)
    return a.transpose(5, 6, 0, 2, 1, 3, 4, 7).reshape(2, 3, 4, 4, 4, rows, -1)


def pack_grads(gq, gk, gv, go):
    o = chunks(go, 12).reshape(2, 3, 4, 4, 4, 12, 2, 128).swapaxes(5, 6).reshape(2, 3, 4, 4, 4, 24, 128)
    return jnp.concatenate([chunks(gq, 24), chunks(gk, 24), chunks(gv, 24), o], 5).astype(BF)


def unpack_grads(total):
    core = lax.rem(lax.axis_index("tm"), 2)
    parts = []
    for n in range(3):
        t = lax.dynamic_slice_in_dim(total[:, :, 24 * n: 24 * n + 24], 12 * core, 12, 2)
        parts.append(t.transpose(2, 0, 1, 3).reshape(12, 768))
    o = total[:, :, 72:].reshape(2, 3, 2, 12, 128)
    o = lax.dynamic_slice_in_dim(o, 6 * core, 6, 3)
    parts.append(o.transpose(3, 0, 1, 2, 4).reshape(6, 1536))
    return parts


HEADS = 12
HEAD_DIM = 64
REACH = 128


def extended_2(value, sides, width):
    for axis, dim in sides:
        devices, length = (lax.axis_size(axis), value.shape[dim])
        up = [(i, (i + 1) % devices) for i in range(devices - 1)]
        down = [(j, i) for i, j in up]
        last = lax.slice_in_dim(value, length - width, length, axis=dim)
        first = lax.slice_in_dim(value, 0, width, axis=dim)
        before = lax.ppermute(last, axis, up)
        after = lax.ppermute(first, axis, down)
        value = jnp.concatenate([before, value, after], axis=dim)
    return value


def shifted(value, axis, by):
    devices = lax.axis_size(axis)
    pairs = [(i, i + by) for i in range(devices) if 0 <= i + by < devices]
    return lax.ppermute(value, axis, pairs)


def layer_normalize(input_rows, norm_gain):
    xf = input_rows.astype(jnp.float32)
    feature_mean = jnp.mean(xf, -1, keepdims=True)
    centered_input = xf - feature_mean
    var = jnp.mean(centered_input * centered_input, -1, keepdims=True)
    inverse_deviation = lax.rsqrt(var + 1e-05)
    standardized_input = centered_input * inverse_deviation
    return (
        (standardized_input * norm_gain).astype(jnp.bfloat16),
        standardized_input,
        inverse_deviation,
    )


def layer_normalize_backward(normalized_gradient, standardized_input, inverse_deviation, norm_gain):
    scaled_output = normalized_gradient * norm_gain
    gain_gradient = jnp.sum(normalized_gradient * standardized_input, 0)
    first_term = jnp.mean(scaled_output, -1, keepdims=True)
    second_term = jnp.mean(scaled_output * standardized_input, -1, keepdims=True)
    return (
        inverse_deviation * (scaled_output - first_term - standardized_input * second_term),
        gain_gradient,
    )


def window_mask(lo, hi, length, qpos, kpos):
    kp = kpos[None, :]
    inside = (kp >= lo[:, None]) & (kp < hi[:, None]) & (kp < length)
    return inside | (kp == qpos[:, None])


def split_heads(a):
    return a.reshape(a.shape[0], HEADS, HEAD_DIM)


def attend(query, key, value, mask):
    scale = HEAD_DIM ** (-0.5)
    scores = (
        jnp.einsum(
            "qhe,khe->hqk", split_heads(query), split_heads(key), preferred_element_type=jnp.float32
        )
        * scale
    )
    scores = jnp.where(mask[None], scores, -1e30)
    expo = jnp.exp(scores - jnp.max(scores, -1, keepdims=True))
    probs = expo / jnp.sum(expo, -1, keepdims=True)
    probs_low = probs.astype(jnp.bfloat16)
    context = jnp.einsum(
        "hqk,khe->qhe", probs_low, split_heads(value), preferred_element_type=jnp.float32
    )
    return (
        context.reshape(query.shape[0], HEADS * HEAD_DIM).astype(jnp.bfloat16),
        probs,
        probs_low,
    )


def attend_back(query, key, value, probs, probs_low, grad_context):
    scale = HEAD_DIM ** (-0.5)
    grad_heads = split_heads(grad_context)
    grad_value = jnp.einsum(
        "hqk,qhe->khe", probs_low, grad_heads, preferred_element_type=jnp.float32
    )
    grad_probs = jnp.einsum(
        "qhe,khe->hqk", grad_heads, split_heads(value), preferred_element_type=jnp.float32
    )
    delta = jnp.sum(probs * grad_probs, -1, keepdims=True)
    grad_scores = (probs * (grad_probs - delta)).astype(jnp.bfloat16)
    grad_query = (
        jnp.einsum(
            "hqk,khe->qhe", grad_scores, split_heads(key), preferred_element_type=jnp.float32
        )
        * scale
    )
    grad_key = (
        jnp.einsum(
            "hqk,qhe->khe", grad_scores, split_heads(query), preferred_element_type=jnp.float32
        )
        * scale
    )
    width = HEADS * HEAD_DIM
    return (
        grad_query.reshape(query.shape[0], width).astype(jnp.bfloat16),
        grad_key.reshape(key.shape[0], width),
        grad_value.reshape(key.shape[0], width),
    )


def per_device(
    frames, cotangent, layer_norm_gain, w_query, w_key, w_value, w_out, lengths, win_lo, win_hi
):
    input_rows = frames[0]
    grad_y = cotangent[0]
    length = lengths[0]
    rows = input_rows.shape[0]
    width = HEADS * HEAD_DIM
    base = lax.axis_index("tm") * rows
    normalized_input, standardized_input, inverse_deviation = layer_normalize(
        input_rows, layer_norm_gain
    )
    own = jnp.concatenate([w_query, w_key, w_value, w_out[:, :768], w_out[:, 768:]], 0)
    gathered = gather_weights(own.reshape(2, 3, 2, 4, 16, 768)).reshape(8, 48, 16, 768)
    full_q, full_k, full_v = (gathered[:, 12 * n: 12 * n + 12].reshape(1536, 768) for n in range(3))
    full_o = jnp.concatenate([gathered[:, 36:42].reshape(768, 768), gathered[:, 42:].reshape(768, 768)], 1)
    query = jnp.dot(normalized_input, full_q, preferred_element_type=jnp.float32).astype(
        jnp.bfloat16
    )
    key = jnp.dot(normalized_input, full_k, preferred_element_type=jnp.float32).astype(jnp.bfloat16)
    value = jnp.dot(normalized_input, full_v, preferred_element_type=jnp.float32).astype(
        jnp.bfloat16
    )
    extended = extended_2(jnp.concatenate([key, value], 1), (("tm", 0),), REACH)
    key_ext = extended[:, :width]
    value_ext = extended[:, width:]
    qpos = base + jnp.arange(rows, dtype=jnp.int32)
    kpos = base - REACH + jnp.arange(rows + 2 * REACH, dtype=jnp.int32)
    mask = window_mask(win_lo[0], win_hi[0], length, qpos, kpos)
    context, probs, probs_low = attend(query, key_ext, value_ext, mask)
    attn = jnp.dot(context, full_o, preferred_element_type=jnp.float32)
    valid = qpos < length
    frames_out = (input_rows.astype(jnp.float32) + jnp.where(valid[:, None], attn, 0.0)).astype(
        jnp.bfloat16
    )
    masked_grad = jnp.where(valid[:, None], grad_y, jnp.zeros_like(grad_y))
    grad_wo = jnp.einsum("th,td->hd", context, masked_grad, preferred_element_type=jnp.float32)
    grad_context = jnp.einsum(
        "td,hd->th", masked_grad, full_o, preferred_element_type=jnp.float32
    ).astype(jnp.bfloat16)
    grad_query, grad_key_ext, grad_value_ext = attend_back(
        query, key_ext, value_ext, probs, probs_low, grad_context
    )
    grad_kv_ext = jnp.concatenate([grad_key_ext, grad_value_ext], 1)
    lower_rim = grad_kv_ext[:REACH]
    upper_rim = grad_kv_ext[REACH + rows :]
    from_next = shifted(lower_rim.astype(jnp.bfloat16), "tm", -1).astype(lower_rim.dtype)
    from_prev = shifted(upper_rim.astype(jnp.bfloat16), "tm", 1).astype(upper_rim.dtype)
    center = grad_kv_ext[REACH : REACH + rows]
    center = center.at[:REACH].add(from_prev)
    center = center.at[rows - REACH :].add(from_next)
    grad_kv = center.astype(jnp.bfloat16)
    grad_key = grad_kv[:, :width]
    grad_value = grad_kv[:, width:]
    grad_wq = jnp.einsum(
        "td,th->dh", normalized_input, grad_query, preferred_element_type=jnp.float32
    )
    grad_wk = jnp.einsum(
        "td,th->dh", normalized_input, grad_key, preferred_element_type=jnp.float32
    )
    grad_wv = jnp.einsum(
        "td,th->dh", normalized_input, grad_value, preferred_element_type=jnp.float32
    )
    normalized_gradient = (
        jnp.einsum("th,dh->td", grad_query, full_q, preferred_element_type=jnp.float32)
        + jnp.einsum("th,dh->td", grad_key, full_k, preferred_element_type=jnp.float32)
        + jnp.einsum("th,dh->td", grad_value, full_v, preferred_element_type=jnp.float32)
    )
    layer_norm_gradient, gain_product = layer_normalize_backward(
        normalized_gradient, standardized_input, inverse_deviation, layer_norm_gain
    )
    grad_frames = (grad_y.astype(jnp.float32) + layer_norm_gradient).astype(jnp.bfloat16)
    total, gain_total = reduce_grads(
        pack_grads(grad_wq, grad_wk, grad_wv, grad_wo),
        jnp.pad(gain_product.reshape(12, 128), ((0, 4), (0, 0))),
    )
    owner = lax.axis_index("dp") * 16 + lax.axis_index("tm")
    gain_own = lax.dynamic_slice_in_dim(gain_total.reshape(2048), owner * 12, 12)
    owned = unpack_grads(total) + [gain_own]
    return (frames_out[None], grad_frames[None], owned[0], owned[1], owned[2], owned[3], owned[4])


def solution(mesh):
    in_specs = (
        P("dp", "tm", None),
        P("dp", "tm", None),
        P(),
        P("dp", None),
        P("dp", None),
        P("dp", None),
        P("dp", None),
        P("dp"),
        P("dp", "tm"),
        P("dp", "tm"),
    )
    out_specs = (
        P("dp", "tm", None),
        P("dp", "tm", None),
        P(("dp", "tm"), None),
        P(("dp", "tm"), None),
        P(("dp", "tm"), None),
        P(("dp", "tm"), None),
        P(("dp", "tm")),
    )
    return jax.shard_map(
        per_device, mesh=mesh, in_specs=in_specs, out_specs=out_specs, check_vma=False
    )
```

```python
import jax
import jax.numpy as jnp
from jax import lax
from jax.experimental import pallas as pl
from jax.experimental.pallas import tpu as pltpu

from jax.sharding import PartitionSpec as P

MESH = pl.DeviceIdType.MESH
BF = jnp.bfloat16
F32 = jnp.float32


class Place:
    def __init__(self):
        dp, tm = lax.axis_index("dp"), lax.axis_index("tm")
        self.yh, self.z = dp // 4, lax.rem(dp, 4)
        self.yl, self.x, self.core = tm // 8, lax.rem(tm // 2, 4), lax.rem(tm, 2)
        self.y = self.yh * 2 + self.yl

    def at(self, axis):
        return {"x": self.x, "y": self.y, "z": self.z}[axis]

    def device(self, axis=None, j=None):
        y, z, x, core = self.y, self.z, self.x, self.core
        if axis == "x":
            x = j
        elif axis == "y":
            y = j
        elif axis == "z":
            z = j
        else:
            core = 1 - core
        return ((y // 2) * 4 + z, (lax.rem(y, 2) * 4 + x) * 2 + core)

    def right(self, axis):
        return lax.rem(self.at(axis) + 1, 4)

    def left(self, axis):
        return lax.rem(self.at(axis) + 3, 4)

    def over(self, axis):
        return lax.rem(self.at(axis) + 2, 4)


def greet(me, far=False):
    barrier = pltpu.get_barrier_semaphore()
    for axis in "xyz":
        for j in (me.left(axis), me.right(axis)) + ((me.over(axis),) if far else ()):
            pl.semaphore_signal(barrier, inc=1, device_id=me.device(axis, j), device_id_type=MESH)
    pl.semaphore_signal(barrier, inc=1, device_id=me.device(), device_id_type=MESH)
    pl.semaphore_wait(barrier, 10 if far else 7)


def gather_regions(me, w, h):
    return (
        (
            ("y", lambda j, p: w.at[j // 2, me.z, h, 0, lax.rem(j, 2), pl.ds(2 * p, 2)]),
            ("z", lambda j, p: w.at[p, j, h, 0]),
        ),
        (
            ("z", lambda j, p: w.at[me.yh, j, h, 1, me.yl, pl.ds(2 * p, 2)]),
            ("y", lambda j, p: w.at[j // 2, pl.ds(2 * p, 2), h, 1, lax.rem(j, 2)]),
        ),
        (
            ("z", lambda j, p: w.at[me.yh, j, h, 2, me.yl, me.x, :, pl.ds(384 * p, 384)]),
            ("y", lambda j, p: w.at[j // 2, pl.ds(2 * p, 2), h, 2, lax.rem(j, 2), me.x]),
            ("x", lambda j, p: w.at[p, :, h, 2, :, j]),
        ),
    )


class GatherStage:
    def __init__(self, me, axis, region, other, send, recv, base):
        self.me, self.axis, self.region, self.other = me, axis, region, other
        self.send, self.recv, self.base = send, recv, base

    def hop(self, k, j, p, right):
        me, n = self.me, self.base + k
        to = me.right(self.axis) if right else me.left(self.axis)
        part = self.region(j, p)
        return pltpu.make_async_remote_copy(
            src_ref=part, dst_ref=part, send_sem=self.send.at[n], recv_sem=self.recv.at[n],
            device_id=me.device(self.axis, to), device_id_type=MESH)

    def share(self, k, j, p, region=None):
        n = self.base + 6 + k
        part = (region or self.region)(j, p)
        return pltpu.make_async_remote_copy(
            src_ref=part, dst_ref=part, send_sem=self.send.at[n], recv_sem=self.recv.at[n],
            device_id=self.me.device(), device_id_type=MESH)

    def start(self):
        i = self.me.at(self.axis)
        self.hop(0, i, 0, True).start()
        self.hop(1, i, 1, False).start()
        self.hop(2, i, 1, True).start()
        self.hop(3, i, 0, False).start()

    def relay(self):
        me = self.me
        l, r = me.left(self.axis), me.right(self.axis)
        self.hop(0, l, 0, True).wait_recv()
        self.hop(4, l, 0, True).start()
        self.share(0, l, 0).start()
        self.hop(1, r, 1, False).wait_recv()
        self.hop(5, r, 1, False).start()
        self.share(1, r, 1).start()

    def finish(self):
        me = self.me
        l, r, o = me.left(self.axis), me.right(self.axis), me.over(self.axis)
        self.hop(2, l, 1, True).wait_recv()
        self.share(2, l, 1).start()
        self.hop(3, r, 0, False).wait_recv()
        self.share(3, r, 0).start()
        self.hop(4, o, 0, True).wait_recv()
        self.share(4, o, 0).start()
        self.hop(5, o, 1, False).wait_recv()
        self.share(5, o, 1).start()

    def arrive(self):
        me = self.me
        l, r, o = me.left(self.axis), me.right(self.axis), me.over(self.axis)
        for k, (j, p) in enumerate(((l, 0), (r, 1), (l, 1), (r, 0), (o, 0), (o, 1))):
            self.share(k, j, p, self.other).wait_recv()

    def drain(self):
        me = self.me
        i, l, r, o = me.at(self.axis), me.left(self.axis), me.right(self.axis), me.over(self.axis)
        for k, (j, p, right) in enumerate(((i, 0, True), (i, 1, False), (i, 1, True), (i, 0, False), (l, 0, True), (r, 1, False))):
            self.hop(k, j, p, right).wait_send()
        for k, (j, p) in enumerate(((l, 0), (r, 1), (l, 1), (r, 0), (o, 0), (o, 1))):
            self.share(k, j, p).wait_send()


def gather_stages(me, w, send, recv):
    mine, theirs = gather_regions(me, w, me.core), gather_regions(me, w, 1 - me.core)
    stages, base = [], 0
    for colour, other in zip(mine, theirs):
        row = []
        for (axis, region), (_, other_region) in zip(colour, other):
            row.append(GatherStage(me, axis, region, other_region, send, recv, base))
            base += 12
        stages.append(row)
    return stages


GATHER_SEMS = 84


def run_gather(me, shards, held, w, send, recv, local):
    wq, wk, wv, wo = shards
    loads = [pltpu.make_async_copy(part, held.at[pl.ds(12 * n, 12)], local.at[n]) for n, part in enumerate((wq, wk, wv))]
    for n in range(2):
        loads.append(pltpu.make_async_copy(wo.at[:, :, pl.ds(768 * n, 768)], held.at[pl.ds(36 + 6 * n, 6)], local.at[3 + n]))
    for copy in loads:
        copy.start()
    greet(me)
    for copy in loads:
        copy.wait()
    own = []
    for h in range(2):
        for c in range(2):
            own.append((held.at[pl.ds(24 * h + 8 * c + 4 * me.yl, 4)], w.at[me.yh, me.z, h, c, me.yl]))
        own.append((held.at[24 * h + 16 + 4 * me.yl + me.x], w.at[me.yh, me.z, h, 2, me.yl, me.x]))
    own = [pltpu.make_async_copy(src, dst, local.at[n]) for n, (src, dst) in enumerate(own)]
    for copy in own:
        copy.start()
    for copy in own:
        copy.wait()
    a, b, c = gather_stages(me, w, send, recv)
    c[0].start()
    a[0].start()
    b[0].start()
    c[0].relay()
    c[0].finish()
    c[1].start()
    a[0].relay()
    b[0].relay()
    a[0].finish()
    a[1].start()
    b[0].finish()
    b[1].start()
    c[1].relay()
    c[1].finish()
    c[2].start()
    a[1].relay()
    b[1].relay()
    c[2].relay()
    a[1].finish()
    b[1].finish()
    c[2].finish()
    for row in (a, b, c):
        for stage in row:
            stage.arrive()
    for row in (a, b, c):
        for stage in row:
            stage.drain()


def gather_kernel(wq, wk, wv, wo, w, held, send, recv, local):
    run_gather(Place(), (wq, wk, wv, wo), held, w, send, recv, local)


def gather_weights(wq, wk, wv, wo):
    return pl.pallas_call(
        gather_kernel,
        out_shape=jax.ShapeDtypeStruct((2, 4, 2, 3, 2, 4, 16, 768), BF),
        in_specs=[pl.BlockSpec(memory_space=pl.ANY)] * 4,
        out_specs=pl.BlockSpec(memory_space=pltpu.VMEM),
        scratch_shapes=[
            pltpu.VMEM((48, 16, 768), BF),
            pltpu.SemaphoreType.DMA((GATHER_SEMS,)),
            pltpu.SemaphoreType.DMA((GATHER_SEMS,)),
            pltpu.SemaphoreType.DMA((6,)),
        ],
        compiler_params=pltpu.CompilerParams(collective_id=0, has_side_effects=True, vmem_limit_bytes=40 << 20),
        name="gather_weights",
    )(wq.reshape(12, 16, 768), wk.reshape(12, 16, 768), wv.reshape(12, 16, 768), wo.reshape(6, 16, 1536))


ORDERS = (("x", "y", "z"), ("y", "z", "x"), ("z", "x", "y"))
DIMS = {"y": 0, "z": 1, "x": 2}


class ReduceStage:
    def __init__(self, me, axis, load, count, out, bufs, sems, base):
        self.me, self.axis, self.load, self.count, self.out = me, axis, load, count, out
        self.sent, self.got = bufs
        self.send, self.recv = sems
        self.base = base

    def hop(self, k):
        me = self.me
        to = me.right(self.axis) if k % 2 == 0 else me.left(self.axis)
        return pltpu.make_async_remote_copy(
            src_ref=self.sent.at[k], dst_ref=self.got.at[k],
            send_sem=self.send.at[self.base + k], recv_sem=self.recv.at[self.base + k],
            device_id=me.device(self.axis, to), device_id_type=MESH)

    def each(self, body):
        if self.count == 1:
            body(0)
        else:
            @pl.loop(0, self.count)
            def _(m):
                body(m)

    def fill(self, k, j, p, extra=None):
        def body(m):
            v = self.load(j, p, m)
            if extra is not None:
                v = v + self.got[extra, m].astype(F32)
            self.sent[k, m] = v.astype(self.sent.dtype)
        self.each(body)
        self.hop(k).start()

    def start(self):
        me = self.me
        l, r, o = me.left(self.axis), me.right(self.axis), me.over(self.axis)
        self.fill(0, o, 0)
        self.fill(1, o, 1)
        self.fill(2, r, 1)
        self.fill(3, l, 0)

    def relay(self):
        me = self.me
        self.hop(0).wait_recv()
        self.fill(4, me.right(self.axis), 0, 0)
        self.hop(1).wait_recv()
        self.fill(5, me.left(self.axis), 1, 1)

    def finish(self):
        me = self.me
        i = me.at(self.axis)
        for k in (2, 3, 4, 5):
            self.hop(k).wait_recv()

        for p, a, b in ((0, 4, 3), (1, 2, 5)):
            def body(m, p=p, a=a, b=b):
                v = self.load(i, p, m) + self.got[a, m].astype(F32) + self.got[b, m].astype(F32)
                self.out(p, m, v)
            self.each(body)

    def drain(self):
        for k in range(6):
            self.hop(k).wait_send()


class GainSum:
    def __init__(self, me, total, got, send, recv):
        self.me, self.total, self.got, self.send, self.recv = me, total, got, send, recv

    def hops(self, s):
        me = self.me
        if s == 3:
            devices = (me.device(),)
        else:
            axis = "xyz"[s]
            devices = tuple(me.device(axis, j) for j in (me.right(axis), me.left(axis), me.over(axis)))
        return [
            pltpu.make_async_remote_copy(
                src_ref=self.total.at[s], dst_ref=self.got.at[3 * s + n], send_sem=self.send.at[3 * s + n],
                recv_sem=self.recv.at[3 * s + n], device_id=device, device_id_type=MESH)
            for n, device in enumerate(devices)
        ]

    def start(self, s):
        for hop in self.hops(s):
            hop.start()

    def finish(self, s):
        v = self.total[s]
        for n, hop in enumerate(self.hops(s)):
            hop.wait_recv()
            v = v + self.got[3 * s + n]
        self.total[s + 1] = v

    def drain(self):
        for s in range(4):
            for hop in self.hops(s):
                hop.wait_send()


def reduce_scratch():
    sem = pltpu.SemaphoreType.DMA
    return [
        pltpu.VMEM((3, 4, 4, 4, 96, 128), BF),
        pltpu.VMEM((3, 6, 8, 96, 128), BF), pltpu.VMEM((3, 6, 8, 96, 128), BF),
        pltpu.VMEM((3, 6, 2, 96, 128), BF), pltpu.VMEM((3, 6, 2, 96, 128), BF),
        pltpu.VMEM((3, 6, 1, 48, 128), F32), pltpu.VMEM((3, 6, 1, 48, 128), F32),
        pltpu.VMEM((3, 4, 4, 96, 128), F32),
        pltpu.VMEM((3, 4, 96, 128), F32),
        pltpu.VMEM((2, 3, 96, 128), F32),
        pltpu.VMEM((5, 16, 128), F32), pltpu.VMEM((10, 16, 128), F32),
        sem((54,)), sem((54,)), sem((3,)), sem((3,)), sem((11,)), sem((11,)),
        pltpu.VMEM((3, 4, 4, 4, 96, 128), BF),
        pltpu.VMEM((3, 4, 4, 4, 96, 128), F32),
        pltpu.VMEM((1536, 256), BF), pltpu.VMEM((768, 256), BF),
        pltpu.VMEM((1536, 384), F32), pltpu.VMEM((768, 256), F32),
        pltpu.VMEM((256, 1536), F32), pltpu.VMEM((256, 1536), F32),
    ]


def reduce_stages(me, half, scratch):
    (r0, s1, d1, s2, d2, s3, d3, t1, t2, fin, gt, gg, send, recv, csend, crecv, gsend, grecv) = scratch[:18]

    def load1(c):
        axis = ORDERS[c][0]

        def load(j, p, m):
            a, b = 2 * p + m // 4, lax.rem(m, 4)
            at = {"x": (a, b, j), "y": (j, a, b), "z": (a, j, b)}[axis]
            return half[(c,) + at]
        return load

    def out1(c):
        def out(p, m, v):
            t1[c, 2 * p + m // 4, lax.rem(m, 4)] = v
        return out

    def load2(c):
        def load(j, p, m):
            return t1[c, 2 * p + m, j] if c == 2 else t1[c, j, 2 * p + m]
        return load

    def out2(c):
        def out(p, m, v):
            t2[c, 2 * p + m] = v
        return out

    def load3(c):
        def load(j, p, m):
            return t2[c, j, pl.ds(48 * p, 48)]
        return load

    def out3(c):
        def out(p, m, v):
            fin[me.core, c, pl.ds(48 * p, 48)] = v
        return out

    stages, base = [], 0
    for c in range(3):
        row = []
        for n, (load, out, bufs, count) in enumerate(
            ((load1, out1, (s1, d1), 8), (load2, out2, (s2, d2), 2), (load3, out3, (s3, d3), 1))
        ):
            row.append(ReduceStage(me, ORDERS[c][n], load(c), count, out(c), (bufs[0].at[c], bufs[1].at[c]), (send, recv), base))
            base += 6
        stages.append(row)
    return stages


def core_hop(me, scratch, c):
    r0, csend, crecv, g = scratch[0], scratch[14], scratch[15], scratch[18]
    return pltpu.make_async_remote_copy(
        src_ref=g.at[c], dst_ref=r0.at[c], send_sem=csend.at[c], recv_sem=crecv.at[c],
        device_id=me.device(), device_id_type=MESH)


def weight_terms(refs, scratch, h, c, put):
    gq, gk, gv, masked = refs
    nt, ct, prod, prod_o = scratch[20:24]
    columns = pl.ds(pl.multiple_of(h * 384 + c * 128, 128), 128)
    rhs = jnp.concatenate([gq[:, columns], gk[:, columns], gv[:, columns]], 1)
    prod[...] = jnp.dot(nt[...], rhs, preferred_element_type=F32)
    columns = pl.ds(pl.multiple_of(h * 768 + c * 256, 128), 256)
    prod_o[...] = jnp.dot(ct[...], masked[:, columns], preferred_element_type=F32)

    @pl.loop(0, 32)
    def _(pair):
        upper = lax.broadcasted_iota(jnp.int32, (8, 128), 0) < 4
        at = pl.multiple_of(pair * 24, 8)
        tiles = [[prod_o[pl.ds(at + 8 * n, 8), pl.ds(128 * b, 128)] for b in range(2)] for n in range(3)]
        mixed = (
            jnp.where(upper, tiles[1][0], pltpu.roll(tiles[1][1], 4, 0)),
            jnp.where(upper, pltpu.roll(tiles[1][0], 4, 0), tiles[1][1]),
        )
        yh, z, yl, xh = pair // 16, lax.rem(pair // 4, 4), lax.rem(pair // 2, 2), lax.rem(pair, 2)
        for odd in range(2):
            rows = pl.ds(pl.multiple_of(pair * 48 + 24 * odd, 8), 24)
            parts = [prod[rows, pl.ds(128 * n, 128)] for n in range(3)]
            parts += [tiles[2 * odd][0], tiles[2 * odd][1], mixed[odd]]
            put((yh * 2 + yl, z, xh * 2 + odd), jnp.concatenate(parts, 0))


def norm(frames):
    xf = frames.astype(F32)
    mean = jnp.mean(xf, -1, keepdims=True)
    centered = xf - mean
    var = jnp.mean(centered * centered, -1, keepdims=True)
    inverse = lax.rsqrt(var + 1e-05)
    return centered * inverse, inverse


def grad_normed(w, gq, gk, gv, out):
    for s in range(4):
        total = None
        for n, g in enumerate((gq, gk, gv)):
            rows = w[2 * s: 2 * s + 2, 12 * n: 12 * n + 12].reshape(384, 768)
            term = lax.dot_general(g[...], rows, (((1,), (1,)), ((), ())), preferred_element_type=F32)
            total = term if total is None else total + term
        out[:, 384 * s: 384 * s + 384] = total


def norm_backward(frames, cotangent, gain, gn, gx, grad_frames, gain_total):
    @pl.loop(0, 8)
    def _(n):
        rows = pl.ds(pl.multiple_of(n * 32, 32), 32)
        xhat, inverse = norm(frames[rows])
        grad = gn[rows]
        gx[rows] = grad * xhat
        g = grad * gain[...]
        first = jnp.mean(g, -1, keepdims=True)
        second = jnp.mean(g * xhat, -1, keepdims=True)
        back = inverse * (g - first - xhat * second)
        grad_frames[rows] = (cotangent[rows].astype(F32) + back).astype(BF)

    gain_total[0] = jnp.zeros((16, 128), F32)
    for b in range(12):
        gain_total[0, b:b + 1] = jnp.sum(gx[:, 128 * b: 128 * b + 128], 0, keepdims=True)


def reduce_kernel(
    normed, gq, gk, gv, context, masked, w, frames, cotangent, gain,
    out_q, out_k, out_v, out_o, gain_out, grad_frames, *scratch
):
    me = Place()
    r0, fin, gt, gg, gsend, grecv = scratch[0], scratch[9], scratch[10], scratch[11], scratch[16], scratch[17]
    for_other, half, nt, ct = scratch[18:22]
    gn, gx = scratch[24:26]
    nt[...] = normed[...].T
    ct[...] = context[...].T
    refs = (gq, gk, gv, masked)
    greet(me, far=True)
    for c in range(3):
        def put(at, v, c=c):
            for_other[(c,) + at] = v.astype(BF)
        weight_terms(refs, scratch, 1 - me.core, c, put)
        core_hop(me, scratch, c).start()
    stages = reduce_stages(me, half, scratch)
    sum_gain = GainSum(me, gt, gg, gsend, grecv)
    for c in range(3):
        core_hop(me, scratch, c).wait_recv()

        def put(at, v, c=c):
            half[(c,) + at] = v + r0[(c,) + at].astype(F32)
        weight_terms(refs, scratch, me.core, c, put)
        stages[c][0].start()
    grad_normed(w, gq, gk, gv, gn)
    for c in range(3):
        stages[c][0].relay()
    norm_backward(frames, cotangent, gain, gn, gx, grad_frames, gt)
    sum_gain.start(0)
    for n in range(3):
        for c in range(3):
            stages[c][n].finish()
            if n < 2:
                stages[c][n + 1].start()
        sum_gain.finish(n)
        sum_gain.start(n + 1)
        if n < 2:
            for c in range(3):
                stages[c][n + 1].relay()

    def last(core):
        return pltpu.make_async_remote_copy(
            src_ref=fin.at[core], dst_ref=fin.at[core], send_sem=gsend.at[10], recv_sem=grecv.at[10],
            device_id=me.device(), device_id_type=MESH)

    last(me.core).start()
    sum_gain.finish(3)
    gain_out[...] = gt[4]
    for c in range(3):
        core_hop(me, scratch, c).wait_send()
        for n in range(3):
            stages[c][n].drain()
    sum_gain.drain()
    last(me.core).wait_send()
    last(1 - me.core).wait_recv()
    odd = lax.rem(me.x, 2)
    for h in range(2):
        for c in range(3):
            lanes = pl.ds(384 * h + 128 * c, 128)
            for n, out in enumerate((out_q, out_k, out_v)):
                t = fin[h, c, pl.ds(24 * n, 24)]
                out[:, lanes] = jnp.where(me.core == 0, t[:12], t[12:])
            for b in range(2):
                lanes = pl.ds(768 * h + 256 * c + 128 * b, 128)
                for r in range(6):
                    even0, even1 = 8 * b + r, 8 * b + 6 + r if r < 2 else 14 + 4 * b + r
                    odd0, odd1 = 16 + 4 * b + r if r < 4 else 8 * b + r - 4, 8 * b + 2 + r
                    row = 72 + jnp.where(
                        odd == 0, jnp.where(me.core == 0, even0, even1), jnp.where(me.core == 0, odd0, odd1))
                    out_o[r:r + 1, lanes] = fin[h, c, pl.ds(row, 1)]


def reduce_grads(*args):
    vm = pl.BlockSpec(memory_space=pltpu.VMEM)
    sds = jax.ShapeDtypeStruct
    return pl.pallas_call(
        reduce_kernel,
        out_shape=(sds((12, 768), F32),) * 3 + (sds((6, 1536), F32), sds((16, 128), F32), sds((256, 1536), BF)),
        in_specs=[vm] * 10,
        out_specs=(vm,) * 6,
        scratch_shapes=reduce_scratch(),
        compiler_params=pltpu.CompilerParams(collective_id=1, has_side_effects=True, vmem_limit_bytes=62 << 20),
        name="reduce_grads",
    )(*args)


HEADS = 12
HEAD_DIM = 64
REACH = 128


def extended_2(value, sides, width):
    for axis, dim in sides:
        devices, length = (lax.axis_size(axis), value.shape[dim])
        up = [(i, (i + 1) % devices) for i in range(devices - 1)]
        down = [(j, i) for i, j in up]
        last = lax.slice_in_dim(value, length - width, length, axis=dim)
        first = lax.slice_in_dim(value, 0, width, axis=dim)
        before = lax.ppermute(last, axis, up)
        after = lax.ppermute(first, axis, down)
        value = jnp.concatenate([before, value, after], axis=dim)
    return value


def shifted(value, axis, by):
    devices = lax.axis_size(axis)
    pairs = [(i, i + by) for i in range(devices) if 0 <= i + by < devices]
    return lax.ppermute(value, axis, pairs)


def layer_normalize(input_rows, norm_gain):
    xf = input_rows.astype(jnp.float32)
    feature_mean = jnp.mean(xf, -1, keepdims=True)
    centered_input = xf - feature_mean
    var = jnp.mean(centered_input * centered_input, -1, keepdims=True)
    inverse_deviation = lax.rsqrt(var + 1e-05)
    standardized_input = centered_input * inverse_deviation
    return (
        (standardized_input * norm_gain).astype(jnp.bfloat16),
        standardized_input,
        inverse_deviation,
    )


def window_mask(lo, hi, length, qpos, kpos):
    kp = kpos[None, :]
    inside = (kp >= lo[:, None]) & (kp < hi[:, None]) & (kp < length)
    return inside | (kp == qpos[:, None])


def split_heads(a):
    return a.reshape(a.shape[0], HEADS, HEAD_DIM)


def attend(query, key, value, mask):
    scale = HEAD_DIM ** (-0.5)
    scores = (
        jnp.einsum(
            "qhe,khe->hqk", split_heads(query), split_heads(key), preferred_element_type=jnp.float32
        )
        * scale
    )
    scores = jnp.where(mask[None], scores, -1e30)
    expo = jnp.exp(scores - jnp.max(scores, -1, keepdims=True))
    probs = expo / jnp.sum(expo, -1, keepdims=True)
    probs_low = probs.astype(jnp.bfloat16)
    context = jnp.einsum(
        "hqk,khe->qhe", probs_low, split_heads(value), preferred_element_type=jnp.float32
    )
    return (
        context.reshape(query.shape[0], HEADS * HEAD_DIM).astype(jnp.bfloat16),
        probs,
        probs_low,
    )


def attend_back(query, key, value, probs, probs_low, grad_context):
    scale = HEAD_DIM ** (-0.5)
    grad_heads = split_heads(grad_context)
    grad_value = jnp.einsum(
        "hqk,qhe->khe", probs_low, grad_heads, preferred_element_type=jnp.float32
    )
    grad_probs = jnp.einsum(
        "qhe,khe->hqk", grad_heads, split_heads(value), preferred_element_type=jnp.float32
    )
    delta = jnp.sum(probs * grad_probs, -1, keepdims=True)
    grad_scores = (probs * (grad_probs - delta)).astype(jnp.bfloat16)
    grad_query = (
        jnp.einsum(
            "hqk,khe->qhe", grad_scores, split_heads(key), preferred_element_type=jnp.float32
        )
        * scale
    )
    grad_key = (
        jnp.einsum(
            "hqk,qhe->khe", grad_scores, split_heads(query), preferred_element_type=jnp.float32
        )
        * scale
    )
    width = HEADS * HEAD_DIM
    return (
        grad_query.reshape(query.shape[0], width).astype(jnp.bfloat16),
        grad_key.reshape(key.shape[0], width),
        grad_value.reshape(key.shape[0], width),
    )


def per_device(
    frames, cotangent, layer_norm_gain, w_query, w_key, w_value, w_out, lengths, win_lo, win_hi
):
    input_rows = frames[0]
    grad_y = cotangent[0]
    length = lengths[0]
    rows = input_rows.shape[0]
    width = HEADS * HEAD_DIM
    base = lax.axis_index("tm") * rows
    normalized_input, standardized_input, inverse_deviation = layer_normalize(
        input_rows, layer_norm_gain
    )
    gathered = gather_weights(w_query, w_key, w_value, w_out).reshape(8, 48, 16, 768)
    full_q, full_k, full_v = (gathered[:, 12 * n: 12 * n + 12].reshape(1536, 768) for n in range(3))
    full_o = jnp.concatenate([gathered[:, 36:42].reshape(768, 768), gathered[:, 42:].reshape(768, 768)], 1)
    query = jnp.dot(normalized_input, full_q, preferred_element_type=jnp.float32).astype(
        jnp.bfloat16
    )
    key = jnp.dot(normalized_input, full_k, preferred_element_type=jnp.float32).astype(jnp.bfloat16)
    value = jnp.dot(normalized_input, full_v, preferred_element_type=jnp.float32).astype(
        jnp.bfloat16
    )
    extended = extended_2(jnp.concatenate([key, value], 1), (("tm", 0),), REACH)
    key_ext = extended[:, :width]
    value_ext = extended[:, width:]
    qpos = base + jnp.arange(rows, dtype=jnp.int32)
    kpos = base - REACH + jnp.arange(rows + 2 * REACH, dtype=jnp.int32)
    mask = window_mask(win_lo[0], win_hi[0], length, qpos, kpos)
    context, probs, probs_low = attend(query, key_ext, value_ext, mask)
    attn = jnp.dot(context, full_o, preferred_element_type=jnp.float32)
    valid = qpos < length
    frames_out = (input_rows.astype(jnp.float32) + jnp.where(valid[:, None], attn, 0.0)).astype(
        jnp.bfloat16
    )
    masked_grad = jnp.where(valid[:, None], grad_y, jnp.zeros_like(grad_y))
    grad_context = jnp.einsum(
        "td,hd->th", masked_grad, full_o, preferred_element_type=jnp.float32
    ).astype(jnp.bfloat16)
    grad_query, grad_key_ext, grad_value_ext = attend_back(
        query, key_ext, value_ext, probs, probs_low, grad_context
    )
    grad_kv_ext = jnp.concatenate([grad_key_ext, grad_value_ext], 1)
    lower_rim = grad_kv_ext[:REACH]
    upper_rim = grad_kv_ext[REACH + rows :]
    from_next = shifted(lower_rim.astype(jnp.bfloat16), "tm", -1).astype(lower_rim.dtype)
    from_prev = shifted(upper_rim.astype(jnp.bfloat16), "tm", 1).astype(upper_rim.dtype)
    center = grad_kv_ext[REACH : REACH + rows]
    center = center.at[:REACH].add(from_prev)
    center = center.at[rows - REACH :].add(from_next)
    grad_kv = center.astype(jnp.bfloat16)
    grad_key = grad_kv[:, :width]
    grad_value = grad_kv[:, width:]
    *owned, gain_total, grad_frames = reduce_grads(
        normalized_input, grad_query, grad_key, grad_value, context, masked_grad, gathered,
        input_rows, grad_y, layer_norm_gain[None],
    )
    owner = lax.axis_index("dp") * 16 + lax.axis_index("tm")
    owned.append(lax.dynamic_slice_in_dim(gain_total.reshape(2048), owner * 12, 12))
    return (frames_out[None], grad_frames[None], owned[0], owned[1], owned[2], owned[3], owned[4])


def solution(mesh):
    in_specs = (
        P("dp", "tm", None),
        P("dp", "tm", None),
        P(),
        P("dp", None),
        P("dp", None),
        P("dp", None),
        P("dp", None),
        P("dp"),
        P("dp", "tm"),
        P("dp", "tm"),
    )
    out_specs = (
        P("dp", "tm", None),
        P("dp", "tm", None),
        P(("dp", "tm"), None),
        P(("dp", "tm"), None),
        P(("dp", "tm"), None),
        P(("dp", "tm"), None),
        P(("dp", "tm")),
    )
    return jax.shard_map(
        per_device, mesh=mesh, in_specs=in_specs, out_specs=out_specs, check_vma=False
    )
```

```python
import jax
import jax.numpy as jnp
from jax import lax
from jax.experimental import pallas as pl
from jax.experimental.pallas import tpu as pltpu

from jax.sharding import PartitionSpec as P

MESH = pl.DeviceIdType.MESH
BF = jnp.bfloat16
F32 = jnp.float32


class Place:
    def __init__(self):
        dp, tm = lax.axis_index("dp"), lax.axis_index("tm")
        self.yh, self.z = dp // 4, lax.rem(dp, 4)
        self.yl, self.x, self.core = tm // 8, lax.rem(tm // 2, 4), lax.rem(tm, 2)
        self.y = self.yh * 2 + self.yl

    def at(self, axis):
        return {"x": self.x, "y": self.y, "z": self.z}[axis]

    def device(self, axis=None, j=None):
        y, z, x, core = self.y, self.z, self.x, self.core
        if axis == "x":
            x = j
        elif axis == "y":
            y = j
        elif axis == "z":
            z = j
        else:
            core = 1 - core
        return ((y // 2) * 4 + z, (lax.rem(y, 2) * 4 + x) * 2 + core)

    def along(self, by):
        return (lax.axis_index("dp"), lax.rem(lax.axis_index("tm") + by, 16))

    def right(self, axis):
        return lax.rem(self.at(axis) + 1, 4)

    def left(self, axis):
        return lax.rem(self.at(axis) + 3, 4)

    def over(self, axis):
        return lax.rem(self.at(axis) + 2, 4)


def greet(me, far=False, ring=False):
    barrier = pltpu.get_barrier_semaphore()
    for axis in "xyz":
        for j in (me.left(axis), me.right(axis)) + ((me.over(axis),) if far else ()):
            pl.semaphore_signal(barrier, inc=1, device_id=me.device(axis, j), device_id_type=MESH)
    pl.semaphore_signal(barrier, inc=1, device_id=me.device(), device_id_type=MESH)
    if ring:
        for by in (1, 15):
            pl.semaphore_signal(barrier, inc=1, device_id=me.along(by), device_id_type=MESH)
    pl.semaphore_wait(barrier, 7 + 3 * far + 2 * ring)


def gather_regions(me, w, h):
    return (
        (
            ("y", lambda j, p: w.at[j // 2, me.z, h, 0, lax.rem(j, 2), pl.ds(2 * p, 2)]),
            ("z", lambda j, p: w.at[p, j, h, 0]),
        ),
        (
            ("z", lambda j, p: w.at[me.yh, j, h, 1, me.yl, pl.ds(2 * p, 2)]),
            ("y", lambda j, p: w.at[j // 2, pl.ds(2 * p, 2), h, 1, lax.rem(j, 2)]),
        ),
        (
            ("z", lambda j, p: w.at[me.yh, j, h, 2, me.yl, me.x, :, pl.ds(384 * p, 384)]),
            ("y", lambda j, p: w.at[j // 2, pl.ds(2 * p, 2), h, 2, lax.rem(j, 2), me.x]),
            ("x", lambda j, p: w.at[p, :, h, 2, :, j]),
        ),
    )


class GatherStage:
    def __init__(self, me, axis, region, other, send, recv, base):
        self.me, self.axis, self.region, self.other = me, axis, region, other
        self.send, self.recv, self.base = send, recv, base

    def hop(self, k, j, p, right):
        me, n = self.me, self.base + k
        to = me.right(self.axis) if right else me.left(self.axis)
        part = self.region(j, p)
        return pltpu.make_async_remote_copy(
            src_ref=part, dst_ref=part, send_sem=self.send.at[n], recv_sem=self.recv.at[n],
            device_id=me.device(self.axis, to), device_id_type=MESH)

    def share(self, k, j, p, region=None):
        n = self.base + 6 + k
        part = (region or self.region)(j, p)
        return pltpu.make_async_remote_copy(
            src_ref=part, dst_ref=part, send_sem=self.send.at[n], recv_sem=self.recv.at[n],
            device_id=self.me.device(), device_id_type=MESH)

    def start(self):
        i = self.me.at(self.axis)
        self.hop(0, i, 0, True).start()
        self.hop(1, i, 1, False).start()
        self.hop(2, i, 1, True).start()
        self.hop(3, i, 0, False).start()

    def relay(self):
        me = self.me
        l, r = me.left(self.axis), me.right(self.axis)
        self.hop(0, l, 0, True).wait_recv()
        self.hop(4, l, 0, True).start()
        self.share(0, l, 0).start()
        self.hop(1, r, 1, False).wait_recv()
        self.hop(5, r, 1, False).start()
        self.share(1, r, 1).start()

    def finish(self):
        me = self.me
        l, r, o = me.left(self.axis), me.right(self.axis), me.over(self.axis)
        self.hop(2, l, 1, True).wait_recv()
        self.share(2, l, 1).start()
        self.hop(3, r, 0, False).wait_recv()
        self.share(3, r, 0).start()
        self.hop(4, o, 0, True).wait_recv()
        self.share(4, o, 0).start()
        self.hop(5, o, 1, False).wait_recv()
        self.share(5, o, 1).start()

    def arrive(self):
        me = self.me
        l, r, o = me.left(self.axis), me.right(self.axis), me.over(self.axis)
        for k, (j, p) in enumerate(((l, 0), (r, 1), (l, 1), (r, 0), (o, 0), (o, 1))):
            self.share(k, j, p, self.other).wait_recv()

    def drain(self):
        me = self.me
        i, l, r, o = me.at(self.axis), me.left(self.axis), me.right(self.axis), me.over(self.axis)
        for k, (j, p, right) in enumerate(((i, 0, True), (i, 1, False), (i, 1, True), (i, 0, False), (l, 0, True), (r, 1, False))):
            self.hop(k, j, p, right).wait_send()
        for k, (j, p) in enumerate(((l, 0), (r, 1), (l, 1), (r, 0), (o, 0), (o, 1))):
            self.share(k, j, p).wait_send()


def gather_stages(me, w, send, recv):
    mine, theirs = gather_regions(me, w, me.core), gather_regions(me, w, 1 - me.core)
    stages, base = [], 0
    for colour, other in zip(mine, theirs):
        row = []
        for (axis, region), (_, other_region) in zip(colour, other):
            row.append(GatherStage(me, axis, region, other_region, send, recv, base))
            base += 12
        stages.append(row)
    return stages


GATHER_SEMS = 84


def start_gather(me, shards, held, w, send, recv, local):
    wq, wk, wv, wo = shards
    loads = [pltpu.make_async_copy(part, held.at[pl.ds(12 * n, 12)], local.at[n]) for n, part in enumerate((wq, wk, wv))]
    for n in range(2):
        loads.append(pltpu.make_async_copy(wo.at[:, :, pl.ds(768 * n, 768)], held.at[pl.ds(36 + 6 * n, 6)], local.at[3 + n]))
    for copy in loads:
        copy.start()
    greet(me, ring=True)
    for copy in loads:
        copy.wait()
    own = []
    for h in range(2):
        for c in range(2):
            own.append((held.at[pl.ds(24 * h + 8 * c + 4 * me.yl, 4)], w.at[me.yh, me.z, h, c, me.yl]))
        own.append((held.at[24 * h + 16 + 4 * me.yl + me.x], w.at[me.yh, me.z, h, 2, me.yl, me.x]))
    own = [pltpu.make_async_copy(src, dst, local.at[n]) for n, (src, dst) in enumerate(own)]
    for copy in own:
        copy.start()
    for copy in own:
        copy.wait()
    rows = gather_stages(me, w, send, recv)
    for row in (rows[2], rows[0], rows[1]):
        row[0].start()
    return rows


def finish_gather(rows, under):
    a, b, c = rows
    c[0].relay()
    c[0].finish()
    c[1].start()
    a[0].relay()
    b[0].relay()
    a[0].finish()
    a[1].start()
    b[0].finish()
    b[1].start()
    c[1].relay()
    c[1].finish()
    c[2].start()
    under()
    a[1].relay()
    b[1].relay()
    c[2].relay()
    a[1].finish()
    b[1].finish()
    c[2].finish()
    for row in rows:
        for stage in row:
            stage.arrive()


def weight_rows(w, s, n):
    parts = []
    for k in range(3 * n, 3 * n + 3):
        parts.append(w[s // 4, s % 4, k // 6, k % 6 // 2, k % 2].reshape(64, 768))
    return jnp.concatenate(parts, 0)


def pair_rows(w, i, n):
    return jnp.concatenate([weight_rows(w, 2 * i, n), weight_rows(w, 2 * i + 1, n)], 0)


def out_rows(w, yh, b):
    parts = []
    for z in range(4):
        parts.append(w[yh, z, 1, 2, b].reshape(64, 768) if b else w[yh, z, 1, 1, 1].reshape(64, 768))
        middle = w[yh, z, 1, 2, 0, 2 * b:2 * b + 2].reshape(32, 768)
        parts.insert(len(parts) - 1 if b else len(parts), middle)
    return jnp.concatenate(parts, 0)


def norm(frames):
    xf = frames.astype(F32)
    mean = jnp.mean(xf, -1, keepdims=True)
    centered = xf - mean
    var = jnp.mean(centered * centered, -1, keepdims=True)
    inverse = lax.rsqrt(var + 1e-05)
    return centered * inverse, inverse


ROWS, COLS = (((1,), (1,)), ((), ())), (((1,), (0,)), ((), ()))


def dot(a, b, dims=COLS):
    return lax.dot_general(a, b, dims, preferred_element_type=F32)


def forward_kernel(
    wq, wk, wv, wo, frames, cotangent, gain, lengths, lo, hi,
    w_out, nt, ct, ctx, gq, gk, gv, masked,
    held, w, nm, q6, gc6, kv, center, bias, rim_s, rim_r, send, recv, local, ring_send, ring_recv
):
    me = Place()
    length = lengths[0]
    base = lax.axis_index("tm") * 256
    rows = start_gather(me, (wq, wk, wv, wo), held, w, send, recv, local)

    @pl.loop(0, 8)
    def _(n):
        at = pl.ds(pl.multiple_of(n * 32, 32), 32)
        xhat, _ = norm(frames[at])
        nm[at] = (xhat * gain[...]).astype(BF)

    def under():
        nt[...] = nm[...].T

        @pl.loop(0, 8)
        def _(n):
            at = pl.ds(pl.multiple_of(n * 32, 32), 32)
            frame = base + n * 32 + lax.broadcasted_iota(jnp.int32, (32, 1536), 0)
            masked[at] = jnp.where(frame < length, cotangent[at].astype(F32), 0.0).astype(BF)

        for b in range(2):
            kp = base + 128 * (b - 1) + lax.broadcasted_iota(jnp.int32, (384, 128), 0)
            qp = base + 128 * b + lax.broadcasted_iota(jnp.int32, (384, 128), 1)
            cols = pl.ds(128 * b, 128)
            seen = (kp >= lo[:, cols]) & (kp < hi[:, cols]) & (kp < length)
            bias[b] = jnp.where(seen | (kp == qp), 0.0, -1e30)

    finish_gather(rows, under)
    spread = pltpu.make_async_copy(w, w_out, local.at[6])
    spread.start()

    def project(n):
        total = None
        for i in range(4):
            term = dot(nm[:, 384 * i:384 * i + 384], pair_rows(w, i, n))
            total = term if total is None else total + term
        return total.astype(BF)

    def halo(p, right):
        src, dst, by = (256, 0, 1) if right else (128, 384, 15)
        n = 2 * p + right
        return pltpu.make_async_remote_copy(
            src_ref=kv.at[p, :, pl.ds(src, 128)], dst_ref=kv.at[p, :, pl.ds(dst, 128)],
            send_sem=ring_send.at[n], recv_sem=ring_recv.at[n], device_id=me.along(by), device_id_type=MESH)

    def rim(p, right):
        n = 12 + 2 * p + right
        return pltpu.make_async_remote_copy(
            src_ref=rim_s.at[p, right], dst_ref=rim_r.at[p, right],
            send_sem=ring_send.at[n], recv_sem=ring_recv.at[n], device_id=me.along(1 if right else 15), device_id_type=MESH)

    for m in range(2):
        k = project(1 + m)
        for p in range(6):
            kv[p, m, 128:384] = k[:, 128 * p:128 * p + 128]
    for p in range(6):
        for right in range(2):
            halo(p, right).start()
    q = project(0)
    for p in range(6):
        q6[p] = q[:, 128 * p:128 * p + 128]
    for yh in range(2):
        g = (dot(masked[:, :768], out_rows(w, yh, 0), ROWS) + dot(masked[:, 768:], out_rows(w, yh, 1), ROWS)).astype(BF)
        for n in range(3):
            gc6[3 * yh + n] = g[:, 128 * n:128 * n + 128]

    @pl.loop(0, 6)
    def _(p):
        for right in range(2):
            halo(p, right).wait_recv()
        first = (lax.broadcasted_iota(jnp.int32, (128, 128), 1) < 64).astype(F32)
        even, odd = first.astype(BF), (1.0 - first).astype(BF)
        lanes = pl.ds(pl.multiple_of(128 * p, 128), 128)
        grads = []
        for b in range(2):
            at = pl.ds(128 * b, 128)
            q = q6[p, at]
            g = gc6[p, at]
            qm = jnp.concatenate([q * even, q * odd], 0)
            gm = jnp.concatenate([g * even, g * odd], 0)
            key = kv[p, 0, pl.ds(128 * b, 384)]
            value = kv[p, 1, pl.ds(128 * b, 384)]
            s = dot(key, qm, ROWS) * 0.125 + jnp.concatenate([bias[b], bias[b]], 1)
            e = jnp.exp(s - jnp.max(s, 0, keepdims=True))
            probs = e * (1.0 / jnp.sum(e, 0, keepdims=True))
            low = probs.astype(BF)
            grad = dot(value, gm, ROWS)
            delta = jnp.sum(probs * grad, 0, keepdims=True)
            ds = (probs * (grad - delta)).astype(BF)
            c = dot(value.T, low)
            c = jnp.concatenate([c[:64, :128], c[64:, 128:]], 0)
            ct[lanes, at] = c.astype(BF)
            ctx[at, lanes] = c.T.astype(BF)
            d = dot(key.T, ds)
            d = jnp.concatenate([d[:64, :128], d[64:, 128:]], 0) * 0.125
            gq[at, lanes] = d.T.astype(BF)
            grads.append((dot(ds, qm) * 0.125, dot(low, gm)))
        for m in range(2):
            here, there = grads[0][m], grads[1][m]
            rim_s[p, 0, m] = here[:128].astype(BF)
            rim_s[p, 1, m] = there[256:].astype(BF)
            center[p, m] = here[128:] + there[:256]
        for right in range(2):
            rim(p, right).start()

    for p in range(6):
        for right in range(2):
            rim(p, right).wait_recv()
        for m, out in enumerate((gk, gv)):
            lanes = pl.ds(128 * p, 128)
            out[:128, lanes] = (center[p, m, :128] + rim_r[p, 1, m].astype(F32)).astype(BF)
            out[128:, lanes] = (center[p, m, 128:] + rim_r[p, 0, m].astype(F32)).astype(BF)
    for p in range(6):
        for right in range(2):
            halo(p, right).wait_send()
            rim(p, right).wait_send()
    for row in rows:
        for stage in row:
            stage.drain()
    spread.wait()


def forward(wq, wk, wv, wo, frames, cotangent, gain, lengths, lo, hi):
    vm, hbm = pl.BlockSpec(memory_space=pltpu.VMEM), pl.BlockSpec(memory_space=pltpu.HBM)
    sds, sem = jax.ShapeDtypeStruct, pltpu.SemaphoreType.DMA
    return pl.pallas_call(
        forward_kernel,
        out_shape=(
            sds((2, 4, 2, 3, 2, 4, 16, 768), BF), sds((1536, 256), BF), sds((768, 256), BF),
            sds((256, 768), BF), sds((256, 768), BF), sds((256, 768), BF), sds((256, 768), BF), sds((256, 1536), BF),
        ),
        in_specs=[hbm] * 4 + [vm] * 3 + [pl.BlockSpec(memory_space=pltpu.SMEM)] + [vm] * 2,
        out_specs=(hbm,) + (vm,) * 7,
        scratch_shapes=[
            pltpu.VMEM((48, 16, 768), BF),
            pltpu.VMEM((2, 4, 2, 3, 2, 4, 16, 768), BF),
            pltpu.VMEM((256, 1536), BF),
            pltpu.VMEM((6, 256, 128), BF), pltpu.VMEM((6, 256, 128), BF),
            pltpu.VMEM((6, 2, 512, 128), BF),
            pltpu.VMEM((6, 2, 256, 128), F32),
            pltpu.VMEM((2, 384, 128), F32),
            pltpu.VMEM((6, 2, 2, 128, 128), BF), pltpu.VMEM((6, 2, 2, 128, 128), BF),
            sem((GATHER_SEMS,)), sem((GATHER_SEMS,)), sem((7,)), sem((24,)), sem((24,)),
        ],
        compiler_params=pltpu.CompilerParams(collective_id=0, has_side_effects=True, vmem_limit_bytes=48 << 20),
        name="forward",
    )(wq.reshape(12, 16, 768), wk.reshape(12, 16, 768), wv.reshape(12, 16, 768), wo.reshape(6, 16, 1536),
      frames, cotangent, gain, lengths, lo, hi)


ORDERS = (("x", "y", "z"), ("y", "z", "x"), ("z", "x", "y"))
DIMS = {"y": 0, "z": 1, "x": 2}


class ReduceStage:
    def __init__(self, me, axis, load, count, out, bufs, sems, base):
        self.me, self.axis, self.load, self.count, self.out = me, axis, load, count, out
        self.sent, self.got = bufs
        self.send, self.recv = sems
        self.base = base

    def hop(self, k):
        me = self.me
        to = me.right(self.axis) if k % 2 == 0 else me.left(self.axis)
        return pltpu.make_async_remote_copy(
            src_ref=self.sent.at[k], dst_ref=self.got.at[k],
            send_sem=self.send.at[self.base + k], recv_sem=self.recv.at[self.base + k],
            device_id=me.device(self.axis, to), device_id_type=MESH)

    def each(self, body):
        if self.count == 1:
            body(0)
        else:
            @pl.loop(0, self.count)
            def _(m):
                body(m)

    def fill(self, k, j, p, extra=None):
        def body(m):
            v = self.load(j, p, m)
            if extra is not None:
                v = v + self.got[extra, m].astype(F32)
            self.sent[k, m] = v.astype(self.sent.dtype)
        self.each(body)
        self.hop(k).start()

    def start(self):
        me = self.me
        l, r, o = me.left(self.axis), me.right(self.axis), me.over(self.axis)
        self.fill(0, o, 0)
        self.fill(1, o, 1)
        self.fill(2, r, 1)
        self.fill(3, l, 0)

    def relay(self):
        me = self.me
        self.hop(0).wait_recv()
        self.fill(4, me.right(self.axis), 0, 0)
        self.hop(1).wait_recv()
        self.fill(5, me.left(self.axis), 1, 1)

    def finish(self):
        me = self.me
        i = me.at(self.axis)
        for k in (2, 3, 4, 5):
            self.hop(k).wait_recv()

        for p, a, b in ((0, 4, 3), (1, 2, 5)):
            def body(m, p=p, a=a, b=b):
                v = self.load(i, p, m) + self.got[a, m].astype(F32) + self.got[b, m].astype(F32)
                self.out(p, m, v)
            self.each(body)

    def drain(self):
        for k in range(6):
            self.hop(k).wait_send()


class GainSum:
    def __init__(self, me, total, got, send, recv):
        self.me, self.total, self.got, self.send, self.recv = me, total, got, send, recv

    def hops(self, s):
        me = self.me
        if s == 3:
            devices = (me.device(),)
        else:
            axis = "xyz"[s]
            devices = tuple(me.device(axis, j) for j in (me.right(axis), me.left(axis), me.over(axis)))
        return [
            pltpu.make_async_remote_copy(
                src_ref=self.total.at[s], dst_ref=self.got.at[3 * s + n], send_sem=self.send.at[3 * s + n],
                recv_sem=self.recv.at[3 * s + n], device_id=device, device_id_type=MESH)
            for n, device in enumerate(devices)
        ]

    def start(self, s):
        for hop in self.hops(s):
            hop.start()

    def finish(self, s):
        v = self.total[s]
        for n, hop in enumerate(self.hops(s)):
            hop.wait_recv()
            v = v + self.got[3 * s + n]
        self.total[s + 1] = v

    def drain(self):
        for s in range(4):
            for hop in self.hops(s):
                hop.wait_send()


def reduce_scratch():
    sem = pltpu.SemaphoreType.DMA
    return [
        pltpu.VMEM((3, 4, 4, 4, 96, 128), BF),
        pltpu.VMEM((3, 6, 8, 96, 128), BF), pltpu.VMEM((3, 6, 8, 96, 128), BF),
        pltpu.VMEM((3, 6, 2, 96, 128), BF), pltpu.VMEM((3, 6, 2, 96, 128), BF),
        pltpu.VMEM((3, 6, 1, 48, 128), F32), pltpu.VMEM((3, 6, 1, 48, 128), F32),
        pltpu.VMEM((3, 4, 4, 96, 128), F32),
        pltpu.VMEM((3, 4, 96, 128), F32),
        pltpu.VMEM((2, 3, 96, 128), F32),
        pltpu.VMEM((5, 16, 128), F32), pltpu.VMEM((10, 16, 128), F32),
        sem((54,)), sem((54,)), sem((3,)), sem((3,)), sem((11,)), sem((11,)),
        pltpu.VMEM((3, 4, 4, 4, 96, 128), BF),
        pltpu.VMEM((3, 4, 4, 4, 96, 128), F32),
        pltpu.VMEM((1536, 384), F32), pltpu.VMEM((768, 256), F32),
        pltpu.VMEM((256, 1536), F32),
        pltpu.VMEM((2, 4, 2, 3, 2, 4, 16, 768), BF), sem,
    ]


def reduce_stages(me, half, scratch):
    (r0, s1, d1, s2, d2, s3, d3, t1, t2, fin, gt, gg, send, recv, csend, crecv, gsend, grecv) = scratch[:18]

    def load1(c):
        axis = ORDERS[c][0]

        def load(j, p, m):
            a, b = 2 * p + m // 4, lax.rem(m, 4)
            at = {"x": (a, b, j), "y": (j, a, b), "z": (a, j, b)}[axis]
            return half[(c,) + at]
        return load

    def out1(c):
        def out(p, m, v):
            t1[c, 2 * p + m // 4, lax.rem(m, 4)] = v
        return out

    def load2(c):
        def load(j, p, m):
            return t1[c, 2 * p + m, j] if c == 2 else t1[c, j, 2 * p + m]
        return load

    def out2(c):
        def out(p, m, v):
            t2[c, 2 * p + m] = v
        return out

    def load3(c):
        def load(j, p, m):
            return t2[c, j, pl.ds(48 * p, 48)]
        return load

    def out3(c):
        def out(p, m, v):
            fin[me.core, c, pl.ds(48 * p, 48)] = v
        return out

    stages, base = [], 0
    for c in range(3):
        row = []
        for n, (load, out, bufs, count) in enumerate(
            ((load1, out1, (s1, d1), 8), (load2, out2, (s2, d2), 2), (load3, out3, (s3, d3), 1))
        ):
            row.append(ReduceStage(me, ORDERS[c][n], load(c), count, out(c), (bufs[0].at[c], bufs[1].at[c]), (send, recv), base))
            base += 6
        stages.append(row)
    return stages


def core_hop(me, scratch, c):
    r0, csend, crecv, g = scratch[0], scratch[14], scratch[15], scratch[18]
    return pltpu.make_async_remote_copy(
        src_ref=g.at[c], dst_ref=r0.at[c], send_sem=csend.at[c], recv_sem=crecv.at[c],
        device_id=me.device(), device_id_type=MESH)


def weight_terms(refs, scratch, h, c, put):
    nt, ct, gq, gk, gv, masked = refs
    prod, prod_o = scratch[20:22]
    columns = pl.ds(pl.multiple_of(h * 384 + c * 128, 128), 128)
    rhs = jnp.concatenate([gq[:, columns], gk[:, columns], gv[:, columns]], 1)
    prod[...] = jnp.dot(nt[...], rhs, preferred_element_type=F32)
    columns = pl.ds(pl.multiple_of(h * 768 + c * 256, 128), 256)
    prod_o[...] = jnp.dot(ct[...], masked[:, columns], preferred_element_type=F32)

    @pl.loop(0, 32)
    def _(pair):
        upper = lax.broadcasted_iota(jnp.int32, (8, 128), 0) < 4
        at = pl.multiple_of(pair * 24, 8)
        tiles = [[prod_o[pl.ds(at + 8 * n, 8), pl.ds(128 * b, 128)] for b in range(2)] for n in range(3)]
        mixed = (
            jnp.where(upper, tiles[1][0], pltpu.roll(tiles[1][1], 4, 0)),
            jnp.where(upper, pltpu.roll(tiles[1][0], 4, 0), tiles[1][1]),
        )
        yh, z, yl, xh = pair // 16, lax.rem(pair // 4, 4), lax.rem(pair // 2, 2), lax.rem(pair, 2)
        for odd in range(2):
            rows = pl.ds(pl.multiple_of(pair * 48 + 24 * odd, 8), 24)
            parts = [prod[rows, pl.ds(128 * n, 128)] for n in range(3)]
            parts += [tiles[2 * odd][0], tiles[2 * odd][1], mixed[odd]]
            put((yh * 2 + yl, z, xh * 2 + odd), jnp.concatenate(parts, 0))


def grad_normed(w, gq, gk, gv, out):
    for s in range(4):
        total = None
        for n, g in enumerate((gq, gk, gv)):
            term = dot(g[...], pair_rows(w, s, n), ROWS)
            total = term if total is None else total + term
        out[:, 384 * s: 384 * s + 384] = total


def norm_backward(frames, cotangent, gain, gn, grad_frames, gain_total):
    gain_total[0] = jnp.zeros((16, 128), F32)

    @pl.loop(0, 8)
    def _(n):
        rows = pl.ds(pl.multiple_of(n * 32, 32), 32)
        xhat, inverse = norm(frames[rows])
        grad = gn[rows]
        gx = grad * xhat
        for b in range(12):
            gain_total[0, b:b + 1] += jnp.sum(gx[:, 128 * b: 128 * b + 128], 0, keepdims=True)
        g = grad * gain[...]
        first = jnp.mean(g, -1, keepdims=True)
        second = jnp.mean(gx * gain[...], -1, keepdims=True)
        back = inverse * (g - first - xhat * second)
        grad_frames[rows] = (cotangent[rows].astype(F32) + back).astype(BF)


def project_out(w, ctx, frames, length, out):
    base = lax.axis_index("tm") * 256
    for b in range(2):
        attn = dot(ctx[:, :384], out_rows(w, 0, b)) + dot(ctx[:, 384:], out_rows(w, 1, b))
        lanes = pl.ds(768 * b, 768)
        frame = base + lax.broadcasted_iota(jnp.int32, (256, 768), 0)
        out[:, lanes] = (frames[:, lanes].astype(F32) + jnp.where(frame < length, attn, 0.0)).astype(BF)


def reduce_kernel(
    nt, gq, gk, gv, ct, ctx, masked, w_hbm, frames, cotangent, gain, lengths,
    total, gain_out, grad_frames, frames_out, *scratch
):
    me = Place()
    r0, fin, gt, gg, gsend, grecv = scratch[0], scratch[9], scratch[10], scratch[11], scratch[16], scratch[17]
    for_other, half = scratch[18:20]
    gn, w = scratch[22:24]
    load = pltpu.make_async_copy(w_hbm, w, scratch[24])
    load.start()
    refs = (nt, ct, gq, gk, gv, masked)
    greet(me, far=True)
    for c in range(3):
        def put(at, v, c=c):
            for_other[(c,) + at] = v.astype(BF)
        weight_terms(refs, scratch, 1 - me.core, c, put)
        core_hop(me, scratch, c).start()
    stages = reduce_stages(me, half, scratch)
    sum_gain = GainSum(me, gt, gg, gsend, grecv)
    for c in range(3):
        core_hop(me, scratch, c).wait_recv()

        def put(at, v, c=c):
            half[(c,) + at] = v + r0[(c,) + at].astype(F32)
        weight_terms(refs, scratch, me.core, c, put)
        stages[c][0].start()
    load.wait()
    grad_normed(w, gq, gk, gv, gn)
    for c in range(3):
        stages[c][0].relay()
    norm_backward(frames, cotangent, gain, gn, grad_frames, gt)
    sum_gain.start(0)
    project_out(w, ctx, frames, lengths[0], frames_out)
    for n in range(3):
        for c in range(3):
            stages[c][n].finish()
            if n < 2:
                stages[c][n + 1].start()
        sum_gain.finish(n)
        sum_gain.start(n + 1)
        if n < 2:
            for c in range(3):
                stages[c][n + 1].relay()

    def last(core):
        return pltpu.make_async_remote_copy(
            src_ref=fin.at[core], dst_ref=fin.at[core], send_sem=gsend.at[10], recv_sem=grecv.at[10],
            device_id=me.device(), device_id_type=MESH)

    last(me.core).start()
    sum_gain.finish(3)
    gain_out[...] = gt[4]
    for c in range(3):
        core_hop(me, scratch, c).wait_send()
        for n in range(3):
            stages[c][n].drain()
    sum_gain.drain()
    last(me.core).wait_send()
    last(1 - me.core).wait_recv()
    total[...] = fin[...]


def reduce_grads(*args):
    vm, hbm = pl.BlockSpec(memory_space=pltpu.VMEM), pl.BlockSpec(memory_space=pltpu.HBM)
    sds = jax.ShapeDtypeStruct
    return pl.pallas_call(
        reduce_kernel,
        out_shape=(sds((2, 3, 96, 128), F32), sds((16, 128), F32), sds((256, 1536), BF), sds((256, 1536), BF)),
        in_specs=[vm] * 7 + [hbm] + [vm] * 3 + [pl.BlockSpec(memory_space=pltpu.SMEM)],
        out_specs=(vm,) * 4,
        scratch_shapes=reduce_scratch(),
        compiler_params=pltpu.CompilerParams(collective_id=1, has_side_effects=True, vmem_limit_bytes=62 << 20),
        name="reduce_grads",
    )(*args)


def outputs_kernel(total, gain, grad_in, frames_in, out_q, out_k, out_v, out_o, out_gain, grad_frames, frames_out):
    me = Place()
    frames_out[...] = frames_in[...]
    grad_frames[...] = grad_in[...]
    odd = lax.rem(me.x, 2)
    for h in range(2):
        for c in range(3):
            lanes = pl.ds(384 * h + 128 * c, 128)
            for n, out in enumerate((out_q, out_k, out_v)):
                t = total[h, c, pl.ds(24 * n, 24)]
                out[:, lanes] = jnp.where(me.core == 0, t[:12], t[12:])
            for b in range(2):
                lanes = pl.ds(768 * h + 256 * c + 128 * b, 128)
                for r in range(6):
                    even0, even1 = 8 * b + r, 8 * b + 6 + r if r < 2 else 14 + 4 * b + r
                    odd0, odd1 = 16 + 4 * b + r if r < 4 else 8 * b + r - 4, 8 * b + 2 + r
                    row = 72 + jnp.where(
                        odd == 0, jnp.where(me.core == 0, even0, even1), jnp.where(me.core == 0, odd0, odd1))
                    out_o[r:r + 1, lanes] = total[h, c, pl.ds(row, 1)]
    at = (lax.axis_index("dp") * 16 + lax.axis_index("tm")) * 12
    row, lane = at // 128, lax.rem(at, 128)
    both = jnp.concatenate([gain[pl.ds(row, 1)], gain[pl.ds(row + 1, 1)]], 1)
    both = jnp.broadcast_to(both, (8, 256))
    out_gain[...] = pltpu.roll(both, lax.rem(256 - lane, 256), 1)[:1, :12]


def write_outputs(*args):
    vm = pl.BlockSpec(memory_space=pltpu.VMEM)
    sds = jax.ShapeDtypeStruct
    return pl.pallas_call(
        outputs_kernel,
        out_shape=(sds((12, 768), F32),) * 3 + (
            sds((6, 1536), F32), sds((1, 12), F32), sds((256, 1536), BF), sds((256, 1536), BF)),
        in_specs=[vm] * 4,
        out_specs=(vm,) * 7,
        name="write_outputs",
    )(*args)


def per_device(
    frames, cotangent, layer_norm_gain, w_query, w_key, w_value, w_out, lengths, win_lo, win_hi
):
    gain = layer_norm_gain[None]
    weights, nt, ct, ctx, gq, gk, gv, masked = forward(
        w_query, w_key, w_value, w_out, frames[0], cotangent[0], gain, lengths, win_lo, win_hi)
    sums = reduce_grads(nt, gq, gk, gv, ct, ctx, masked, weights, frames[0], cotangent[0], gain, lengths)
    grad_wq, grad_wk, grad_wv, grad_wo, grad_gain, grad_frames, frames_out = write_outputs(*sums)
    return (frames_out[None], grad_frames[None], grad_wq, grad_wk, grad_wv, grad_wo, grad_gain.reshape(12))


def solution(mesh):
    in_specs = (
        P("dp", "tm", None),
        P("dp", "tm", None),
        P(),
        P("dp", None),
        P("dp", None),
        P("dp", None),
        P("dp", None),
        P("dp"),
        P("dp", "tm"),
        P("dp", "tm"),
    )
    out_specs = (
        P("dp", "tm", None),
        P("dp", "tm", None),
        P(("dp", "tm"), None),
        P(("dp", "tm"), None),
        P(("dp", "tm"), None),
        P(("dp", "tm"), None),
        P(("dp", "tm")),
    )
    return jax.shard_map(
        per_device, mesh=mesh, in_specs=in_specs, out_specs=out_specs, check_vma=False
    )
```

```python
import jax
import jax.numpy as jnp
from jax import lax
from jax.experimental import pallas as pl
from jax.experimental.pallas import tpu as pltpu

from jax.sharding import PartitionSpec as P

MESH = pl.DeviceIdType.MESH
BF = jnp.bfloat16
F32 = jnp.float32


class Place:
    def __init__(self):
        dp, tm = lax.axis_index("dp"), lax.axis_index("tm")
        self.yh, self.z = dp // 4, lax.rem(dp, 4)
        self.yl, self.x, self.core = tm // 8, lax.rem(tm // 2, 4), lax.rem(tm, 2)
        self.y = self.yh * 2 + self.yl

    def at(self, axis):
        return {"x": self.x, "y": self.y, "z": self.z}[axis]

    def device(self, axis=None, j=None):
        y, z, x, core = self.y, self.z, self.x, self.core
        if axis == "x":
            x = j
        elif axis == "y":
            y = j
        elif axis == "z":
            z = j
        else:
            core = 1 - core
        return ((y // 2) * 4 + z, (lax.rem(y, 2) * 4 + x) * 2 + core)

    def along(self, by):
        return (lax.axis_index("dp"), lax.rem(lax.axis_index("tm") + by, 16))

    def right(self, axis):
        return lax.rem(self.at(axis) + 1, 4)

    def left(self, axis):
        return lax.rem(self.at(axis) + 3, 4)

    def over(self, axis):
        return lax.rem(self.at(axis) + 2, 4)


def greet(me, far=False, ring=False):
    barrier = pltpu.get_barrier_semaphore()
    for axis in "xyz":
        for j in (me.left(axis), me.right(axis)) + ((me.over(axis),) if far else ()):
            pl.semaphore_signal(barrier, inc=1, device_id=me.device(axis, j), device_id_type=MESH)
    pl.semaphore_signal(barrier, inc=1, device_id=me.device(), device_id_type=MESH)
    if ring:
        for by in (1, 15):
            pl.semaphore_signal(barrier, inc=1, device_id=me.along(by), device_id_type=MESH)
    pl.semaphore_wait(barrier, 7 + 3 * far + 2 * ring)


def gather_regions(me, w, h):
    return (
        (
            ("y", lambda j, p: w.at[j // 2, me.z, h, 0, lax.rem(j, 2), pl.ds(2 * p, 2)]),
            ("z", lambda j, p: w.at[p, j, h, 0]),
        ),
        (
            ("z", lambda j, p: w.at[me.yh, j, h, 1, me.yl, pl.ds(2 * p, 2)]),
            ("y", lambda j, p: w.at[j // 2, pl.ds(2 * p, 2), h, 1, lax.rem(j, 2)]),
        ),
        (
            ("z", lambda j, p: w.at[me.yh, j, h, 2, me.yl, me.x, :, pl.ds(384 * p, 384)]),
            ("y", lambda j, p: w.at[j // 2, pl.ds(2 * p, 2), h, 2, lax.rem(j, 2), me.x]),
            ("x", lambda j, p: w.at[p, :, h, 2, :, j]),
        ),
    )


class GatherStage:
    def __init__(self, me, axis, region, other, send, recv, base):
        self.me, self.axis, self.region, self.other = me, axis, region, other
        self.send, self.recv, self.base = send, recv, base

    def hop(self, k, j, p, right):
        me, n = self.me, self.base + k
        to = me.right(self.axis) if right else me.left(self.axis)
        part = self.region(j, p)
        return pltpu.make_async_remote_copy(
            src_ref=part, dst_ref=part, send_sem=self.send.at[n], recv_sem=self.recv.at[n],
            device_id=me.device(self.axis, to), device_id_type=MESH)

    def share(self, k, j, p, region=None):
        n = self.base + 6 + k
        part = (region or self.region)(j, p)
        return pltpu.make_async_remote_copy(
            src_ref=part, dst_ref=part, send_sem=self.send.at[n], recv_sem=self.recv.at[n],
            device_id=self.me.device(), device_id_type=MESH)

    def start(self):
        i = self.me.at(self.axis)
        self.hop(0, i, 0, True).start()
        self.hop(1, i, 1, False).start()
        self.hop(2, i, 1, True).start()
        self.hop(3, i, 0, False).start()

    def relay(self):
        me = self.me
        l, r = me.left(self.axis), me.right(self.axis)
        self.hop(0, l, 0, True).wait_recv()
        self.hop(4, l, 0, True).start()
        self.share(0, l, 0).start()
        self.hop(1, r, 1, False).wait_recv()
        self.hop(5, r, 1, False).start()
        self.share(1, r, 1).start()

    def finish(self):
        me = self.me
        l, r, o = me.left(self.axis), me.right(self.axis), me.over(self.axis)
        self.hop(2, l, 1, True).wait_recv()
        self.share(2, l, 1).start()
        self.hop(3, r, 0, False).wait_recv()
        self.share(3, r, 0).start()
        self.hop(4, o, 0, True).wait_recv()
        self.share(4, o, 0).start()
        self.hop(5, o, 1, False).wait_recv()
        self.share(5, o, 1).start()

    def arrive(self):
        me = self.me
        l, r, o = me.left(self.axis), me.right(self.axis), me.over(self.axis)
        for k, (j, p) in enumerate(((l, 0), (r, 1), (l, 1), (r, 0), (o, 0), (o, 1))):
            self.share(k, j, p, self.other).wait_recv()

    def drain(self):
        me = self.me
        i, l, r, o = me.at(self.axis), me.left(self.axis), me.right(self.axis), me.over(self.axis)
        for k, (j, p, right) in enumerate(((i, 0, True), (i, 1, False), (i, 1, True), (i, 0, False), (l, 0, True), (r, 1, False))):
            self.hop(k, j, p, right).wait_send()
        for k, (j, p) in enumerate(((l, 0), (r, 1), (l, 1), (r, 0), (o, 0), (o, 1))):
            self.share(k, j, p).wait_send()


def gather_stages(me, w, send, recv):
    mine, theirs = gather_regions(me, w, me.core), gather_regions(me, w, 1 - me.core)
    stages, base = [], 0
    for colour, other in zip(mine, theirs):
        row = []
        for (axis, region), (_, other_region) in zip(colour, other):
            row.append(GatherStage(me, axis, region, other_region, send, recv, base))
            base += 12
        stages.append(row)
    return stages


GATHER_SEMS = 84


def start_gather(me, shards, held, w, send, recv, local):
    wq, wk, wv, wo = shards
    loads = [pltpu.make_async_copy(part, held.at[pl.ds(12 * n, 12)], local.at[n]) for n, part in enumerate((wq, wk, wv))]
    for n in range(2):
        loads.append(pltpu.make_async_copy(wo.at[:, :, pl.ds(768 * n, 768)], held.at[pl.ds(36 + 6 * n, 6)], local.at[3 + n]))
    for copy in loads:
        copy.start()
    greet(me, far=True, ring=True)
    for copy in loads:
        copy.wait()
    own = []
    for h in range(2):
        for c in range(2):
            own.append((held.at[pl.ds(24 * h + 8 * c + 4 * me.yl, 4)], w.at[me.yh, me.z, h, c, me.yl]))
        own.append((held.at[24 * h + 16 + 4 * me.yl + me.x], w.at[me.yh, me.z, h, 2, me.yl, me.x]))
    own = [pltpu.make_async_copy(src, dst, local.at[n]) for n, (src, dst) in enumerate(own)]
    for copy in own:
        copy.start()
    for copy in own:
        copy.wait()
    rows = gather_stages(me, w, send, recv)
    for row in (rows[2], rows[0], rows[1]):
        row[0].start()
    return rows


def finish_gather(rows, under):
    a, b, c = rows
    c[0].relay()
    c[0].finish()
    c[1].start()
    a[0].relay()
    b[0].relay()
    a[0].finish()
    a[1].start()
    b[0].finish()
    b[1].start()
    c[1].relay()
    c[1].finish()
    c[2].start()
    under()
    a[1].relay()
    b[1].relay()
    c[2].relay()
    a[1].finish()
    b[1].finish()
    c[2].finish()
    for row in rows:
        for stage in row:
            stage.arrive()


def weight_rows(w, s, n):
    parts = []
    for k in range(3 * n, 3 * n + 3):
        parts.append(w[s // 4, s % 4, k // 6, k % 6 // 2, k % 2].reshape(64, 768))
    return jnp.concatenate(parts, 0)


def pair_rows(w, i, n):
    return jnp.concatenate([weight_rows(w, 2 * i, n), weight_rows(w, 2 * i + 1, n)], 0)


def out_rows(w, yh, b):
    parts = []
    for z in range(4):
        parts.append(w[yh, z, 1, 2, b].reshape(64, 768) if b else w[yh, z, 1, 1, 1].reshape(64, 768))
        middle = w[yh, z, 1, 2, 0, 2 * b:2 * b + 2].reshape(32, 768)
        parts.insert(len(parts) - 1 if b else len(parts), middle)
    return jnp.concatenate(parts, 0)


def norm(frames):
    xf = frames.astype(F32)
    mean = jnp.mean(xf, -1, keepdims=True)
    centered = xf - mean
    var = jnp.mean(centered * centered, -1, keepdims=True)
    inverse = lax.rsqrt(var + 1e-05)
    return centered * inverse, inverse


ROWS, COLS = (((1,), (1,)), ((), ())), (((1,), (0,)), ((), ()))


def dot(a, b, dims=COLS):
    return lax.dot_general(a, b, dims, preferred_element_type=F32)


ORDERS = (("x", "y", "z"), ("y", "z", "x"), ("z", "x", "y"))
DIMS = {"y": 0, "z": 1, "x": 2}


class ReduceStage:
    def __init__(self, me, axis, load, count, out, bufs, sems, base):
        self.me, self.axis, self.load, self.count, self.out = me, axis, load, count, out
        self.sent, self.got = bufs
        self.send, self.recv = sems
        self.base = base

    def hop(self, k):
        me = self.me
        to = me.right(self.axis) if k % 2 == 0 else me.left(self.axis)
        return pltpu.make_async_remote_copy(
            src_ref=self.sent.at[k], dst_ref=self.got.at[k],
            send_sem=self.send.at[self.base + k], recv_sem=self.recv.at[self.base + k],
            device_id=me.device(self.axis, to), device_id_type=MESH)

    def each(self, body):
        if self.count == 1:
            body(0)
        else:
            @pl.loop(0, self.count)
            def _(m):
                body(m)

    def fill(self, k, j, p, extra=None):
        def body(m):
            v = self.load(j, p, m)
            if extra is not None:
                v = v + self.got[extra, m].astype(F32)
            self.sent[k, m] = v.astype(self.sent.dtype)
        self.each(body)
        self.hop(k).start()

    def start(self):
        me = self.me
        l, r, o = me.left(self.axis), me.right(self.axis), me.over(self.axis)
        self.fill(0, o, 0)
        self.fill(1, o, 1)
        self.fill(2, r, 1)
        self.fill(3, l, 0)

    def relay(self):
        me = self.me
        self.hop(0).wait_recv()
        self.fill(4, me.right(self.axis), 0, 0)
        self.hop(1).wait_recv()
        self.fill(5, me.left(self.axis), 1, 1)

    def finish(self):
        me = self.me
        i = me.at(self.axis)
        for k in (2, 3, 4, 5):
            self.hop(k).wait_recv()

        for p, a, b in ((0, 4, 3), (1, 2, 5)):
            def body(m, p=p, a=a, b=b):
                v = self.load(i, p, m) + self.got[a, m].astype(F32) + self.got[b, m].astype(F32)
                self.out(p, m, v)
            self.each(body)

    def drain(self):
        for k in range(6):
            self.hop(k).wait_send()


class GainSum:
    def __init__(self, me, total, got, send, recv):
        self.me, self.total, self.got, self.send, self.recv = me, total, got, send, recv

    def hops(self, s):
        me = self.me
        if s == 3:
            devices = (me.device(),)
        else:
            axis = "xyz"[s]
            devices = tuple(me.device(axis, j) for j in (me.right(axis), me.left(axis), me.over(axis)))
        return [
            pltpu.make_async_remote_copy(
                src_ref=self.total.at[s], dst_ref=self.got.at[3 * s + n], send_sem=self.send.at[3 * s + n],
                recv_sem=self.recv.at[3 * s + n], device_id=device, device_id_type=MESH)
            for n, device in enumerate(devices)
        ]

    def start(self, s):
        for hop in self.hops(s):
            hop.start()

    def finish(self, s):
        v = self.total[s]
        for n, hop in enumerate(self.hops(s)):
            hop.wait_recv()
            v = v + self.got[3 * s + n]
        self.total[s + 1] = v

    def drain(self):
        for s in range(4):
            for hop in self.hops(s):
                hop.wait_send()


def reduce_scratch():
    sem = pltpu.SemaphoreType.DMA
    return [
        pltpu.VMEM((3, 4, 4, 4, 96, 128), BF),
        pltpu.VMEM((3, 6, 8, 96, 128), BF), pltpu.VMEM((3, 6, 8, 96, 128), BF),
        pltpu.VMEM((3, 6, 2, 96, 128), BF), pltpu.VMEM((3, 6, 2, 96, 128), BF),
        pltpu.VMEM((3, 6, 1, 48, 128), F32), pltpu.VMEM((3, 6, 1, 48, 128), F32),
        pltpu.VMEM((3, 4, 4, 96, 128), F32),
        pltpu.VMEM((3, 4, 96, 128), F32),
        pltpu.VMEM((2, 3, 96, 128), F32),
        pltpu.VMEM((5, 16, 128), F32), pltpu.VMEM((10, 16, 128), F32),
        sem((54,)), sem((54,)), sem((3,)), sem((3,)), sem((11,)), sem((11,)),
        pltpu.VMEM((3, 4, 4, 4, 96, 128), BF),
        pltpu.VMEM((3, 4, 4, 4, 96, 128), F32),
        pltpu.VMEM((1536, 384), F32), pltpu.VMEM((768, 256), F32),
    ]


def reduce_stages(me, half, scratch):
    (r0, s1, d1, s2, d2, s3, d3, t1, t2, fin, gt, gg, send, recv, csend, crecv, gsend, grecv) = scratch[:18]

    def load1(c):
        axis = ORDERS[c][0]

        def load(j, p, m):
            a, b = 2 * p + m // 4, lax.rem(m, 4)
            at = {"x": (a, b, j), "y": (j, a, b), "z": (a, j, b)}[axis]
            return half[(c,) + at]
        return load

    def out1(c):
        def out(p, m, v):
            t1[c, 2 * p + m // 4, lax.rem(m, 4)] = v
        return out

    def load2(c):
        def load(j, p, m):
            return t1[c, 2 * p + m, j] if c == 2 else t1[c, j, 2 * p + m]
        return load

    def out2(c):
        def out(p, m, v):
            t2[c, 2 * p + m] = v
        return out

    def load3(c):
        def load(j, p, m):
            return t2[c, j, pl.ds(48 * p, 48)]
        return load

    def out3(c):
        def out(p, m, v):
            fin[me.core, c, pl.ds(48 * p, 48)] = v
        return out

    stages, base = [], 0
    for c in range(3):
        row = []
        for n, (load, out, bufs, count) in enumerate(
            ((load1, out1, (s1, d1), 8), (load2, out2, (s2, d2), 2), (load3, out3, (s3, d3), 1))
        ):
            row.append(ReduceStage(me, ORDERS[c][n], load(c), count, out(c), (bufs[0].at[c], bufs[1].at[c]), (send, recv), base))
            base += 6
        stages.append(row)
    return stages


def core_hop(me, scratch, c):
    r0, csend, crecv, g = scratch[0], scratch[14], scratch[15], scratch[18]
    return pltpu.make_async_remote_copy(
        src_ref=g.at[c], dst_ref=r0.at[c], send_sem=csend.at[c], recv_sem=crecv.at[c],
        device_id=me.device(), device_id_type=MESH)


def weight_terms(refs, scratch, h, c, put):
    nt, ct, gq, gk, gv, masked = refs
    prod, prod_o = scratch[20:22]
    columns = pl.ds(pl.multiple_of(h * 384 + c * 128, 128), 128)
    rhs = jnp.concatenate([gq[:, columns], gk[:, columns], gv[:, columns]], 1)
    prod[...] = jnp.dot(nt[...], rhs, preferred_element_type=F32)
    columns = pl.ds(pl.multiple_of(h * 768 + c * 256, 128), 256)
    prod_o[...] = jnp.dot(ct[...], masked[:, columns], preferred_element_type=F32)

    @pl.loop(0, 32)
    def _(pair):
        upper = lax.broadcasted_iota(jnp.int32, (8, 128), 0) < 4
        at = pl.multiple_of(pair * 24, 8)
        tiles = [[prod_o[pl.ds(at + 8 * n, 8), pl.ds(128 * b, 128)] for b in range(2)] for n in range(3)]
        mixed = (
            jnp.where(upper, tiles[1][0], pltpu.roll(tiles[1][1], 4, 0)),
            jnp.where(upper, pltpu.roll(tiles[1][0], 4, 0), tiles[1][1]),
        )
        yh, z, yl, xh = pair // 16, lax.rem(pair // 4, 4), lax.rem(pair // 2, 2), lax.rem(pair, 2)
        for odd in range(2):
            rows = pl.ds(pl.multiple_of(pair * 48 + 24 * odd, 8), 24)
            parts = [prod[rows, pl.ds(128 * n, 128)] for n in range(3)]
            parts += [tiles[2 * odd][0], tiles[2 * odd][1], mixed[odd]]
            put((yh * 2 + yl, z, xh * 2 + odd), jnp.concatenate(parts, 0))


def grad_normed(w, gq, gk, gv, out):
    for s in range(4):
        total = None
        for n, g in enumerate((gq, gk, gv)):
            term = dot(g[...], pair_rows(w, s, n), ROWS)
            total = term if total is None else total + term
        for b in range(3 * s, 3 * s + 3):
            out[b // 2, b % 2] = total[:, 128 * (b - 3 * s):128 * (b - 3 * s) + 128]


def norm_backward(frames, cotangent, gain, gn, grad_frames, gain_total):
    gain_total[0] = jnp.zeros((16, 128), F32)

    @pl.loop(0, 8)
    def _(n):
        rows = pl.ds(pl.multiple_of(n * 32, 32), 32)
        xhat, inverse = norm(frames[rows])
        grad = jnp.concatenate([gn[b // 2, b % 2, rows] for b in range(12)], 1)
        gx = grad * xhat
        for b in range(12):
            gain_total[0, b:b + 1] += jnp.sum(gx[:, 128 * b: 128 * b + 128], 0, keepdims=True)
        g = grad * gain[...]
        first = jnp.mean(g, -1, keepdims=True)
        second = jnp.mean(gx * gain[...], -1, keepdims=True)
        back = inverse * (g - first - xhat * second)
        grad_frames[rows] = (cotangent[rows].astype(F32) + back).astype(BF)


def project_out(w, ctx, frames, length, out):
    base = lax.axis_index("tm") * 256
    for b in range(2):
        attn = dot(ctx[:, :384], out_rows(w, 0, b)) + dot(ctx[:, 384:], out_rows(w, 1, b))
        lanes = pl.ds(768 * b, 768)
        frame = base + lax.broadcasted_iota(jnp.int32, (256, 768), 0)
        out[:, lanes] = (frames[:, lanes].astype(F32) + jnp.where(frame < length, attn, 0.0)).astype(BF)


def block_kernel(
    wq, wk, wv, wo, frames_hbm, cotangent_hbm, gain_hbm, lengths, lo_hbm, hi_hbm,
    total, gain_out, grad_frames_hbm, frames_out_hbm,
    nt, ct, ctx, gq, gk, gv, masked, frames, cotangent, gain, lo, hi, grad_frames, frames_out,
    held, w, nm, q6, gc6, kv, center, bias, rim_s, rim_r, send, recv, local, ring_send, ring_recv, *scratch
):
    me = Place()
    length = lengths[0]
    base = lax.axis_index("tm") * 256
    loads = ((frames_hbm, frames), (gain_hbm, gain), (cotangent_hbm, cotangent), (lo_hbm, lo), (hi_hbm, hi))
    loads = [pltpu.make_async_copy(src, dst, local.at[6 + n]) for n, (src, dst) in enumerate(loads)]
    for copy in loads:
        copy.start()
    rows = start_gather(me, (wq, wk, wv, wo), held, w, send, recv, local)
    for copy in loads:
        copy.wait()

    @pl.loop(0, 8)
    def _(n):
        at = pl.ds(pl.multiple_of(n * 32, 32), 32)
        xhat, _ = norm(frames[at])
        nm[at] = (xhat * gain[...]).astype(BF)

    def under():
        nt[...] = nm[...].T

        @pl.loop(0, 8)
        def _(n):
            at = pl.ds(pl.multiple_of(n * 32, 32), 32)
            frame = base + n * 32 + lax.broadcasted_iota(jnp.int32, (32, 1536), 0)
            masked[at] = jnp.where(frame < length, cotangent[at].astype(F32), 0.0).astype(BF)

        for b in range(2):
            kp = base + 128 * (b - 1) + lax.broadcasted_iota(jnp.int32, (384, 128), 0)
            qp = base + 128 * b + lax.broadcasted_iota(jnp.int32, (384, 128), 1)
            cols = pl.ds(128 * b, 128)
            seen = (kp >= lo[:, cols]) & (kp < hi[:, cols]) & (kp < length)
            bias[b] = jnp.where(seen | (kp == qp), 0.0, -1e30)

    finish_gather(rows, under)

    def project(n):
        total = None
        for i in range(4):
            term = dot(nm[:, 384 * i:384 * i + 384], pair_rows(w, i, n))
            total = term if total is None else total + term
        return total.astype(BF)

    def halo(p, right):
        src, dst, by = (256, 0, 1) if right else (128, 384, 15)
        n = 2 * p + right
        return pltpu.make_async_remote_copy(
            src_ref=kv.at[p, :, pl.ds(src, 128)], dst_ref=kv.at[p, :, pl.ds(dst, 128)],
            send_sem=ring_send.at[n], recv_sem=ring_recv.at[n], device_id=me.along(by), device_id_type=MESH)

    def rim(p, right):
        n = 12 + 2 * p + right
        return pltpu.make_async_remote_copy(
            src_ref=rim_s.at[p, right], dst_ref=rim_r.at[p, right],
            send_sem=ring_send.at[n], recv_sem=ring_recv.at[n], device_id=me.along(1 if right else 15), device_id_type=MESH)

    for m in range(2):
        k = project(1 + m)
        for p in range(6):
            kv[p, m, 128:384] = k[:, 128 * p:128 * p + 128]
    for p in range(6):
        for right in range(2):
            halo(p, right).start()
    q = project(0)
    for p in range(6):
        q6[p] = q[:, 128 * p:128 * p + 128]
    for yh in range(2):
        g = (dot(masked[:, :768], out_rows(w, yh, 0), ROWS) + dot(masked[:, 768:], out_rows(w, yh, 1), ROWS)).astype(BF)
        for n in range(3):
            gc6[3 * yh + n] = g[:, 128 * n:128 * n + 128]

    @pl.loop(0, 6)
    def _(p):
        for right in range(2):
            halo(p, right).wait_recv()
        first = (lax.broadcasted_iota(jnp.int32, (128, 128), 1) < 64).astype(F32)
        even, odd = first.astype(BF), (1.0 - first).astype(BF)
        lanes = pl.ds(pl.multiple_of(128 * p, 128), 128)
        grads = []
        for b in range(2):
            at = pl.ds(128 * b, 128)
            q = q6[p, at]
            g = gc6[p, at]
            qm = jnp.concatenate([q * even, q * odd], 0)
            gm = jnp.concatenate([g * even, g * odd], 0)
            key = kv[p, 0, pl.ds(128 * b, 384)]
            value = kv[p, 1, pl.ds(128 * b, 384)]
            s = dot(key, qm, ROWS) * 0.125 + jnp.concatenate([bias[b], bias[b]], 1)
            e = jnp.exp(s - jnp.max(s, 0, keepdims=True))
            probs = e * (1.0 / jnp.sum(e, 0, keepdims=True))
            low = probs.astype(BF)
            grad = dot(value, gm, ROWS)
            delta = jnp.sum(probs * grad, 0, keepdims=True)
            ds = (probs * (grad - delta)).astype(BF)
            c = dot(value.T, low)
            c = jnp.concatenate([c[:64, :128], c[64:, 128:]], 0)
            ct[lanes, at] = c.astype(BF)
            ctx[at, lanes] = c.T.astype(BF)
            d = dot(key.T, ds)
            d = jnp.concatenate([d[:64, :128], d[64:, 128:]], 0) * 0.125
            gq[at, lanes] = d.T.astype(BF)
            grads.append((dot(ds, qm) * 0.125, dot(low, gm)))
        for m in range(2):
            here, there = grads[0][m], grads[1][m]
            rim_s[p, 0, m] = here[:128].astype(BF)
            rim_s[p, 1, m] = there[256:].astype(BF)
            center[p, m] = here[128:] + there[:256]
        for right in range(2):
            rim(p, right).start()

    for p in range(6):
        for right in range(2):
            rim(p, right).wait_recv()
        for m, out in enumerate((gk, gv)):
            lanes = pl.ds(128 * p, 128)
            out[:128, lanes] = (center[p, m, :128] + rim_r[p, 1, m].astype(F32)).astype(BF)
            out[128:, lanes] = (center[p, m, 128:] + rim_r[p, 0, m].astype(F32)).astype(BF)

    r0, fin, gt, gg, gsend, grecv = scratch[0], scratch[9], scratch[10], scratch[11], scratch[16], scratch[17]
    for_other, half = scratch[18:20]
    refs = (nt, ct, gq, gk, gv, masked)
    for c in range(3):
        def put(at, v, c=c):
            for_other[(c,) + at] = v.astype(BF)
        weight_terms(refs, scratch, 1 - me.core, c, put)
        core_hop(me, scratch, c).start()
    stages = reduce_stages(me, half, scratch)
    sum_gain = GainSum(me, gt, gg, gsend, grecv)
    for c in range(3):
        core_hop(me, scratch, c).wait_recv()

        def put(at, v, c=c):
            half[(c,) + at] = v + r0[(c,) + at].astype(F32)
        weight_terms(refs, scratch, me.core, c, put)
        stages[c][0].start()
    grad_normed(w, gq, gk, gv, center)
    for c in range(3):
        stages[c][0].relay()
    norm_backward(frames, cotangent, gain, center, grad_frames, gt)
    stores = [
        pltpu.make_async_copy(grad_frames, grad_frames_hbm, local.at[11]),
        pltpu.make_async_copy(frames_out, frames_out_hbm, local.at[12]),
    ]
    stores[0].start()
    sum_gain.start(0)
    project_out(w, ctx, frames, length, frames_out)
    stores[1].start()
    for n in range(3):
        for c in range(3):
            stages[c][n].finish()
            if n < 2:
                stages[c][n + 1].start()
        sum_gain.finish(n)
        sum_gain.start(n + 1)
        if n < 2:
            for c in range(3):
                stages[c][n + 1].relay()

    def last(core):
        return pltpu.make_async_remote_copy(
            src_ref=fin.at[core], dst_ref=fin.at[core], send_sem=gsend.at[10], recv_sem=grecv.at[10],
            device_id=me.device(), device_id_type=MESH)

    last(me.core).start()
    sum_gain.finish(3)
    gain_out[...] = gt[4]
    for c in range(3):
        core_hop(me, scratch, c).wait_send()
        for n in range(3):
            stages[c][n].drain()
    sum_gain.drain()
    last(me.core).wait_send()
    last(1 - me.core).wait_recv()
    total[...] = fin[...]
    for p in range(6):
        for right in range(2):
            halo(p, right).wait_send()
            rim(p, right).wait_send()
    for row in rows:
        for stage in row:
            stage.drain()
    for copy in stores:
        copy.wait()


def block(wq, wk, wv, wo, *args):
    vm, hbm = pl.BlockSpec(memory_space=pltpu.VMEM), pl.BlockSpec(memory_space=pltpu.HBM)
    sds, sem = jax.ShapeDtypeStruct, pltpu.SemaphoreType.DMA
    return pl.pallas_call(
        block_kernel,
        out_shape=(sds((2, 3, 96, 128), F32), sds((16, 128), F32), sds((256, 1536), BF), sds((256, 1536), BF)),
        in_specs=[hbm] * 7 + [pl.BlockSpec(memory_space=pltpu.SMEM)] + [hbm] * 2,
        out_specs=(vm, vm, hbm, hbm),
        scratch_shapes=[
            pltpu.VMEM((1536, 256), BF), pltpu.VMEM((768, 256), BF), pltpu.VMEM((256, 768), BF),
            pltpu.VMEM((256, 768), BF), pltpu.VMEM((256, 768), BF), pltpu.VMEM((256, 768), BF),
            pltpu.VMEM((256, 1536), BF), pltpu.VMEM((256, 1536), BF), pltpu.VMEM((256, 1536), BF),
            pltpu.VMEM((1, 1536), F32), pltpu.VMEM((1, 256), jnp.int32), pltpu.VMEM((1, 256), jnp.int32),
            pltpu.VMEM((256, 1536), BF), pltpu.VMEM((256, 1536), BF),
            pltpu.VMEM((48, 16, 768), BF),
            pltpu.VMEM((2, 4, 2, 3, 2, 4, 16, 768), BF),
            pltpu.VMEM((256, 1536), BF),
            pltpu.VMEM((6, 256, 128), BF), pltpu.VMEM((6, 256, 128), BF),
            pltpu.VMEM((6, 2, 512, 128), BF),
            pltpu.VMEM((6, 2, 256, 128), F32),
            pltpu.VMEM((2, 384, 128), F32),
            pltpu.VMEM((6, 2, 2, 128, 128), BF), pltpu.VMEM((6, 2, 2, 128, 128), BF),
            sem((GATHER_SEMS,)), sem((GATHER_SEMS,)), sem((13,)), sem((24,)), sem((24,)),
        ] + reduce_scratch(),
        compiler_params=pltpu.CompilerParams(collective_id=0, has_side_effects=True, vmem_limit_bytes=67043328),
        name="block",
    )(wq.reshape(12, 16, 768), wk.reshape(12, 16, 768), wv.reshape(12, 16, 768), wo.reshape(6, 16, 1536), *args)


def outputs_kernel(total, gain, grad_in, frames_in, out_q, out_k, out_v, out_o, out_gain, grad_frames, frames_out):
    me = Place()
    frames_out[...] = frames_in[...]
    grad_frames[...] = grad_in[...]
    odd = lax.rem(me.x, 2)
    for h in range(2):
        for c in range(3):
            lanes = pl.ds(384 * h + 128 * c, 128)
            for n, out in enumerate((out_q, out_k, out_v)):
                t = total[h, c, pl.ds(24 * n, 24)]
                out[:, lanes] = jnp.where(me.core == 0, t[:12], t[12:])
            for b in range(2):
                lanes = pl.ds(768 * h + 256 * c + 128 * b, 128)
                for r in range(6):
                    even0, even1 = 8 * b + r, 8 * b + 6 + r if r < 2 else 14 + 4 * b + r
                    odd0, odd1 = 16 + 4 * b + r if r < 4 else 8 * b + r - 4, 8 * b + 2 + r
                    row = 72 + jnp.where(
                        odd == 0, jnp.where(me.core == 0, even0, even1), jnp.where(me.core == 0, odd0, odd1))
                    out_o[r:r + 1, lanes] = total[h, c, pl.ds(row, 1)]
    at = (lax.axis_index("dp") * 16 + lax.axis_index("tm")) * 12
    row, lane = at // 128, lax.rem(at, 128)
    both = jnp.concatenate([gain[pl.ds(row, 1)], gain[pl.ds(row + 1, 1)]], 1)
    both = jnp.broadcast_to(both, (8, 256))
    out_gain[...] = pltpu.roll(both, lax.rem(256 - lane, 256), 1)[:1, :12]


def write_outputs(*args):
    vm = pl.BlockSpec(memory_space=pltpu.VMEM)
    sds = jax.ShapeDtypeStruct
    return pl.pallas_call(
        outputs_kernel,
        out_shape=(sds((12, 768), F32),) * 3 + (
            sds((6, 1536), F32), sds((1, 12), F32), sds((256, 1536), BF), sds((256, 1536), BF)),
        in_specs=[vm] * 4,
        out_specs=(vm,) * 7,
        name="write_outputs",
    )(*args)


def per_device(
    frames, cotangent, layer_norm_gain, w_query, w_key, w_value, w_out, lengths, win_lo, win_hi
):
    gain = layer_norm_gain[None]
    sums = block(
        w_query, w_key, w_value, w_out, frames[0], cotangent[0], gain, lengths, win_lo, win_hi)
    grad_wq, grad_wk, grad_wv, grad_wo, grad_gain, grad_frames, frames_out = write_outputs(*sums)
    return (frames_out[None], grad_frames[None], grad_wq, grad_wk, grad_wv, grad_wo, grad_gain.reshape(12))


def solution(mesh):
    in_specs = (
        P("dp", "tm", None),
        P("dp", "tm", None),
        P(),
        P("dp", None),
        P("dp", None),
        P("dp", None),
        P("dp", None),
        P("dp"),
        P("dp", "tm"),
        P("dp", "tm"),
    )
    out_specs = (
        P("dp", "tm", None),
        P("dp", "tm", None),
        P(("dp", "tm"), None),
        P(("dp", "tm"), None),
        P(("dp", "tm"), None),
        P(("dp", "tm"), None),
        P(("dp", "tm")),
    )
    return jax.shard_map(
        per_device, mesh=mesh, in_specs=in_specs, out_specs=out_specs, check_vma=False
    )
```

```python
import jax
import jax.numpy as jnp
from jax import lax
from jax.experimental import pallas as pl
from jax.experimental.pallas import tpu as pltpu

from jax.sharding import PartitionSpec as P

MESH = pl.DeviceIdType.MESH
BF = jnp.bfloat16
F32 = jnp.float32


class Place:
    def __init__(self):
        dp, tm = lax.axis_index("dp"), lax.axis_index("tm")
        self.yh, self.z = dp // 4, lax.rem(dp, 4)
        self.yl, self.x, self.core = tm // 8, lax.rem(tm // 2, 4), lax.rem(tm, 2)
        self.y = self.yh * 2 + self.yl

    def at(self, axis):
        return {"x": self.x, "y": self.y, "z": self.z}[axis]

    def device(self, axis=None, j=None):
        y, z, x, core = self.y, self.z, self.x, self.core
        if axis == "x":
            x = j
        elif axis == "y":
            y = j
        elif axis == "z":
            z = j
        else:
            core = 1 - core
        return ((y // 2) * 4 + z, (lax.rem(y, 2) * 4 + x) * 2 + core)

    def along(self, by):
        return (lax.axis_index("dp"), lax.rem(lax.axis_index("tm") + by, 16))

    def right(self, axis):
        return lax.rem(self.at(axis) + 1, 4)

    def left(self, axis):
        return lax.rem(self.at(axis) + 3, 4)

    def over(self, axis):
        return lax.rem(self.at(axis) + 2, 4)


def greet(me, far=False, ring=False):
    barrier = pltpu.get_barrier_semaphore()
    for axis in "xyz":
        for j in (me.left(axis), me.right(axis)) + ((me.over(axis),) if far else ()):
            pl.semaphore_signal(barrier, inc=1, device_id=me.device(axis, j), device_id_type=MESH)
    pl.semaphore_signal(barrier, inc=1, device_id=me.device(), device_id_type=MESH)
    if ring:
        for by in (1, 15):
            pl.semaphore_signal(barrier, inc=1, device_id=me.along(by), device_id_type=MESH)
    pl.semaphore_wait(barrier, 7 + 3 * far + 2 * ring)


def gather_regions(me, w, h):
    return (
        (
            ("y", lambda j, p: w.at[j // 2, me.z, h, 0, lax.rem(j, 2), pl.ds(2 * p, 2)]),
            ("z", lambda j, p: w.at[p, j, h, 0]),
        ),
        (
            ("z", lambda j, p: w.at[me.yh, j, h, 1, me.yl, pl.ds(2 * p, 2)]),
            ("y", lambda j, p: w.at[j // 2, pl.ds(2 * p, 2), h, 1, lax.rem(j, 2)]),
        ),
        (
            ("z", lambda j, p: w.at[me.yh, j, h, 2, me.yl, me.x, :, pl.ds(384 * p, 384)]),
            ("y", lambda j, p: w.at[j // 2, pl.ds(2 * p, 2), h, 2, lax.rem(j, 2), me.x]),
            ("x", lambda j, p: w.at[p, :, h, 2, :, j]),
        ),
    )


class GatherStage:
    def __init__(self, me, axis, region, other, send, recv, base):
        self.me, self.axis, self.region, self.other = me, axis, region, other
        self.send, self.recv, self.base = send, recv, base

    def hop(self, k, j, p, right):
        me, n = self.me, self.base + k
        to = me.right(self.axis) if right else me.left(self.axis)
        part = self.region(j, p)
        return pltpu.make_async_remote_copy(
            src_ref=part, dst_ref=part, send_sem=self.send.at[n], recv_sem=self.recv.at[n],
            device_id=me.device(self.axis, to), device_id_type=MESH)

    def share(self, k, j, p, region=None):
        n = self.base + 6 + k
        part = (region or self.region)(j, p)
        return pltpu.make_async_remote_copy(
            src_ref=part, dst_ref=part, send_sem=self.send.at[n], recv_sem=self.recv.at[n],
            device_id=self.me.device(), device_id_type=MESH)

    def start(self):
        i = self.me.at(self.axis)
        self.hop(0, i, 0, True).start()
        self.hop(1, i, 1, False).start()
        self.hop(2, i, 1, True).start()
        self.hop(3, i, 0, False).start()

    def relay(self):
        me = self.me
        l, r = me.left(self.axis), me.right(self.axis)
        self.hop(0, l, 0, True).wait_recv()
        self.hop(4, l, 0, True).start()
        self.share(0, l, 0).start()
        self.hop(1, r, 1, False).wait_recv()
        self.hop(5, r, 1, False).start()
        self.share(1, r, 1).start()

    def finish(self):
        me = self.me
        l, r, o = me.left(self.axis), me.right(self.axis), me.over(self.axis)
        self.hop(2, l, 1, True).wait_recv()
        self.share(2, l, 1).start()
        self.hop(3, r, 0, False).wait_recv()
        self.share(3, r, 0).start()
        self.hop(4, o, 0, True).wait_recv()
        self.share(4, o, 0).start()
        self.hop(5, o, 1, False).wait_recv()
        self.share(5, o, 1).start()

    def arrive(self):
        me = self.me
        l, r, o = me.left(self.axis), me.right(self.axis), me.over(self.axis)
        for k, (j, p) in enumerate(((l, 0), (r, 1), (l, 1), (r, 0), (o, 0), (o, 1))):
            self.share(k, j, p, self.other).wait_recv()

    def drain(self):
        me = self.me
        i, l, r, o = me.at(self.axis), me.left(self.axis), me.right(self.axis), me.over(self.axis)
        for k, (j, p, right) in enumerate(((i, 0, True), (i, 1, False), (i, 1, True), (i, 0, False), (l, 0, True), (r, 1, False))):
            self.hop(k, j, p, right).wait_send()
        for k, (j, p) in enumerate(((l, 0), (r, 1), (l, 1), (r, 0), (o, 0), (o, 1))):
            self.share(k, j, p).wait_send()


def gather_stages(me, w, send, recv):
    mine, theirs = gather_regions(me, w, me.core), gather_regions(me, w, 1 - me.core)
    stages, base = [], 0
    for colour, other in zip(mine, theirs):
        row = []
        for (axis, region), (_, other_region) in zip(colour, other):
            row.append(GatherStage(me, axis, region, other_region, send, recv, base))
            base += 12
        stages.append(row)
    return stages


GATHER_SEMS = 84


def start_gather(me, shards, held, w, send, recv, local):
    wq, wk, wv, wo = shards
    loads = [pltpu.make_async_copy(part, held.at[pl.ds(12 * n, 12)], local.at[n]) for n, part in enumerate((wq, wk, wv))]
    for n in range(2):
        loads.append(pltpu.make_async_copy(wo.at[:, :, pl.ds(768 * n, 768)], held.at[pl.ds(36 + 6 * n, 6)], local.at[3 + n]))
    for copy in loads:
        copy.start()
    for copy in loads:
        copy.wait()
    own = []
    for h in range(2):
        for c in range(2):
            own.append((held.at[pl.ds(24 * h + 8 * c + 4 * me.yl, 4)], w.at[me.yh, me.z, h, c, me.yl]))
        own.append((held.at[24 * h + 16 + 4 * me.yl + me.x], w.at[me.yh, me.z, h, 2, me.yl, me.x]))
    own = [pltpu.make_async_copy(src, dst, local.at[n]) for n, (src, dst) in enumerate(own)]
    for copy in own:
        copy.start()
    greet(me, ring=True)
    for copy in own:
        copy.wait()
    rows = gather_stages(me, w, send, recv)
    for row in (rows[2], rows[0], rows[1]):
        row[0].start()
    return rows


def finish_gather(rows, first, second):
    a, b, c = rows
    c[0].relay()
    a[0].relay()
    b[0].relay()
    c[0].finish()
    c[1].start()
    a[0].finish()
    a[1].start()
    b[0].finish()
    c[1].relay()
    b[1].start()
    c[1].finish()
    c[2].start()
    first()
    a[1].relay()
    b[1].relay()
    second()
    c[2].relay()
    a[1].finish()
    b[1].finish()
    c[2].finish()
    for row in rows:
        for stage in row:
            stage.arrive()


def weight_rows(w, s, n):
    parts = []
    for k in range(3 * n, 3 * n + 3):
        parts.append(w[s // 4, s % 4, k // 6, k % 6 // 2, k % 2].reshape(64, 768))
    return jnp.concatenate(parts, 0)


def pair_rows(w, i, n):
    return jnp.concatenate([weight_rows(w, 2 * i, n), weight_rows(w, 2 * i + 1, n)], 0)


def out_rows(w, yh, b):
    parts = []
    for z in range(4):
        parts.append(w[yh, z, 1, 2, b].reshape(64, 768) if b else w[yh, z, 1, 1, 1].reshape(64, 768))
        middle = w[yh, z, 1, 2, 0, 2 * b:2 * b + 2].reshape(32, 768)
        parts.insert(len(parts) - 1 if b else len(parts), middle)
    return jnp.concatenate(parts, 0)


def norm(frames):
    xf = frames.astype(F32)
    mean = jnp.mean(xf, -1, keepdims=True)
    centered = xf - mean
    var = jnp.mean(centered * centered, -1, keepdims=True)
    inverse = lax.rsqrt(var + 1e-05)
    return centered * inverse, inverse


ROWS, COLS = (((1,), (1,)), ((), ())), (((1,), (0,)), ((), ()))


def dot(a, b, dims=COLS):
    return lax.dot_general(a, b, dims, preferred_element_type=F32)


ORDERS = (("x", "y", "z"), ("y", "z", "x"), ("z", "x", "y"))
DIMS = {"y": 0, "z": 1, "x": 2}


class ReduceStage:
    def __init__(self, me, axis, load, count, out, bufs, sems, base):
        self.me, self.axis, self.load, self.count, self.out = me, axis, load, count, out
        self.sent, self.got = bufs
        self.send, self.recv = sems
        self.base = base

    def hop(self, k):
        me = self.me
        to = me.right(self.axis) if k % 2 == 0 else me.left(self.axis)
        return pltpu.make_async_remote_copy(
            src_ref=self.sent.at[k], dst_ref=self.got.at[k],
            send_sem=self.send.at[self.base + k], recv_sem=self.recv.at[self.base + k],
            device_id=me.device(self.axis, to), device_id_type=MESH)

    def each(self, body):
        if self.count == 1:
            body(0)
        else:
            @pl.loop(0, self.count)
            def _(m):
                body(m)

    def fill(self, k, j, p, extra=None):
        def body(m):
            v = self.load(j, p, m)
            if extra is not None:
                v = v + self.got[extra, m].astype(F32)
            self.sent[k, m] = v.astype(self.sent.dtype)
        self.each(body)
        self.hop(k).start()

    def start(self):
        me = self.me
        l, r, o = me.left(self.axis), me.right(self.axis), me.over(self.axis)
        self.fill(0, o, 0)
        self.fill(1, o, 1)
        self.fill(2, r, 1)
        self.fill(3, l, 0)

    def relay(self):
        me = self.me
        self.hop(0).wait_recv()
        self.fill(4, me.right(self.axis), 0, 0)
        self.hop(1).wait_recv()
        self.fill(5, me.left(self.axis), 1, 1)

    def finish(self):
        me = self.me
        i = me.at(self.axis)
        for k in (2, 3, 4, 5):
            self.hop(k).wait_recv()

        for p, a, b in ((0, 4, 3), (1, 2, 5)):
            def body(m, p=p, a=a, b=b):
                v = self.load(i, p, m) + self.got[a, m].astype(F32) + self.got[b, m].astype(F32)
                self.out(p, m, v)
            self.each(body)

    def drain(self):
        for k in range(6):
            self.hop(k).wait_send()


class LastStage:
    def __init__(self, me, axis, terms, got, out, sems, base):
        self.me, self.axis, self.terms, self.got, self.out = me, axis, terms, got, out
        self.send, self.recv = sems
        self.base = base

    def hops(self):
        me = self.me
        to = (me.over(self.axis), me.right(self.axis), me.left(self.axis))
        return [
            pltpu.make_async_remote_copy(
                src_ref=self.terms.at[j], dst_ref=self.got.at[n], send_sem=self.send.at[self.base + n],
                recv_sem=self.recv.at[self.base + n], device_id=me.device(self.axis, j), device_id_type=MESH)
            for n, j in enumerate(to)
        ]

    def start(self):
        for hop in self.hops():
            hop.start()

    def relay(self):
        pass

    def finish(self):
        v = self.terms[self.me.at(self.axis)]
        for n, hop in enumerate(self.hops()):
            hop.wait_recv()
            v = v + self.got[n]
        self.out[...] = v

    def drain(self):
        for hop in self.hops():
            hop.wait_send()


class GainSum:
    def __init__(self, me, total, got, send, recv):
        self.me, self.total, self.got, self.send, self.recv = me, total, got, send, recv

    def hops(self, s):
        me = self.me
        if s == 3:
            devices = (me.device(),)
        else:
            axis = "xyz"[s]
            devices = tuple(me.device(axis, j) for j in (me.right(axis), me.left(axis), me.over(axis)))
        return [
            pltpu.make_async_remote_copy(
                src_ref=self.total.at[s], dst_ref=self.got.at[3 * s + n], send_sem=self.send.at[3 * s + n],
                recv_sem=self.recv.at[3 * s + n], device_id=device, device_id_type=MESH)
            for n, device in enumerate(devices)
        ]

    def start(self, s):
        for hop in self.hops(s):
            hop.start()

    def finish(self, s):
        v = self.total[s]
        for n, hop in enumerate(self.hops(s)):
            hop.wait_recv()
            v = v + self.got[3 * s + n]
        self.total[s + 1] = v

    def drain(self):
        for s in range(4):
            for hop in self.hops(s):
                hop.wait_send()


def reduce_scratch():
    sem = pltpu.SemaphoreType.DMA
    return [
        pltpu.VMEM((3, 4, 4, 4, 96, 128), BF),
        pltpu.VMEM((3, 6, 8, 96, 128), BF), pltpu.VMEM((3, 6, 8, 96, 128), BF),
        pltpu.VMEM((3, 6, 2, 96, 128), BF), pltpu.VMEM((3, 6, 2, 96, 128), BF),
        pltpu.VMEM((8, 128), F32), pltpu.VMEM((3, 3, 96, 128), F32),
        pltpu.VMEM((3, 4, 4, 96, 128), F32),
        pltpu.VMEM((3, 4, 96, 128), F32),
        pltpu.VMEM((2, 3, 96, 128), F32),
        pltpu.VMEM((5, 16, 128), F32), pltpu.VMEM((10, 16, 128), F32),
        sem((54,)), sem((54,)), sem((3,)), sem((3,)), sem((11,)), sem((11,)),
        pltpu.VMEM((3, 4, 4, 4, 96, 128), BF),
        pltpu.VMEM((3, 4, 4, 4, 96, 128), F32),
        pltpu.VMEM((1536, 384), F32), pltpu.VMEM((768, 256), F32),
    ]


def reduce_stages(me, half, scratch):
    (r0, s1, d1, s2, d2, s3, d3, t1, t2, fin, gt, gg, send, recv, csend, crecv, gsend, grecv) = scratch[:18]

    def load1(c):
        axis = ORDERS[c][0]

        def load(j, p, m):
            a, b = 2 * p + m // 4, lax.rem(m, 4)
            at = {"x": (a, b, j), "y": (j, a, b), "z": (a, j, b)}[axis]
            return half[(c,) + at]
        return load

    def out1(c):
        def out(p, m, v):
            t1[c, 2 * p + m // 4, lax.rem(m, 4)] = v
        return out

    def load2(c):
        def load(j, p, m):
            return t1[c, 2 * p + m, j] if c == 2 else t1[c, j, 2 * p + m]
        return load

    def out2(c):
        def out(p, m, v):
            t2[c, 2 * p + m] = v
        return out

    stages, base = [], 0
    for c in range(3):
        row = []
        for n, (load, out, bufs, count) in enumerate(
            ((load1, out1, (s1, d1), 8), (load2, out2, (s2, d2), 2))
        ):
            row.append(ReduceStage(me, ORDERS[c][n], load(c), count, out(c), (bufs[0].at[c], bufs[1].at[c]), (send, recv), base))
            base += 6
        row.append(LastStage(me, ORDERS[c][2], t2.at[c], d3.at[c], fin.at[me.core, c], (send, recv), base))
        base += 6
        stages.append(row)
    return stages


def core_hop(me, scratch, c):
    r0, csend, crecv, g = scratch[0], scratch[14], scratch[15], scratch[18]
    return pltpu.make_async_remote_copy(
        src_ref=g.at[c], dst_ref=r0.at[c], send_sem=csend.at[c], recv_sem=crecv.at[c],
        device_id=me.device(), device_id_type=MESH)


def weight_terms(refs, scratch, h, c, put):
    nt, ct, gq, gk, gv, masked = refs
    prod, prod_o = scratch[20:22]
    columns = pl.ds(pl.multiple_of(h * 384 + c * 128, 128), 128)
    rhs = jnp.concatenate([gq[:, columns], gk[:, columns], gv[:, columns]], 1)
    prod[...] = jnp.dot(nt[...], rhs, preferred_element_type=F32)
    columns = pl.ds(pl.multiple_of(h * 768 + c * 256, 128), 256)
    prod_o[...] = jnp.dot(ct[...], masked[:, columns], preferred_element_type=F32)

    @pl.loop(0, 32)
    def _(pair):
        upper = lax.broadcasted_iota(jnp.int32, (8, 128), 0) < 4
        at = pl.multiple_of(pair * 24, 8)
        tiles = [[prod_o[pl.ds(at + 8 * n, 8), pl.ds(128 * b, 128)] for b in range(2)] for n in range(3)]
        mixed = (
            jnp.where(upper, tiles[1][0], pltpu.roll(tiles[1][1], 4, 0)),
            jnp.where(upper, pltpu.roll(tiles[1][0], 4, 0), tiles[1][1]),
        )
        yh, z, yl, xh = pair // 16, lax.rem(pair // 4, 4), lax.rem(pair // 2, 2), lax.rem(pair, 2)
        for odd in range(2):
            rows = pl.ds(pl.multiple_of(pair * 48 + 24 * odd, 8), 24)
            parts = [prod[rows, pl.ds(128 * n, 128)] for n in range(3)]
            parts += [tiles[2 * odd][0], tiles[2 * odd][1], mixed[odd]]
            put((yh * 2 + yl, z, xh * 2 + odd), jnp.concatenate(parts, 0))


def grad_normed(w, gq, gk, gv, out):
    for s in range(4):
        total = None
        for n, g in enumerate((gq, gk, gv)):
            term = dot(g[...], pair_rows(w, s, n), ROWS)
            total = term if total is None else total + term
        for b in range(3 * s, 3 * s + 3):
            out[b // 2, b % 2] = total[:, 128 * (b - 3 * s):128 * (b - 3 * s) + 128]


def norm_backward(frames, cotangent, gain, gn, grad_frames, gain_total):
    gain_total[0] = jnp.zeros((16, 128), F32)

    @pl.loop(0, 8)
    def _(n):
        rows = pl.ds(pl.multiple_of(n * 32, 32), 32)
        xhat, inverse = norm(frames[rows])
        grad = jnp.concatenate([gn[b // 2, b % 2, rows] for b in range(12)], 1)
        gx = grad * xhat
        for b in range(12):
            gain_total[0, b:b + 1] += jnp.sum(gx[:, 128 * b: 128 * b + 128], 0, keepdims=True)
        g = grad * gain[...]
        first = jnp.mean(g, -1, keepdims=True)
        second = jnp.mean(gx * gain[...], -1, keepdims=True)
        back = inverse * (g - first - xhat * second)
        grad_frames[rows] = (cotangent[rows].astype(F32) + back).astype(BF)


def project_out(w, ctx, frames, length, out):
    base = lax.axis_index("tm") * 256
    for b in range(2):
        attn = dot(ctx[:, :384], out_rows(w, 0, b)) + dot(ctx[:, 384:], out_rows(w, 1, b))
        lanes = pl.ds(768 * b, 768)
        frame = base + lax.broadcasted_iota(jnp.int32, (256, 768), 0)
        out[:, lanes] = (frames[:, lanes].astype(F32) + jnp.where(frame < length, attn, 0.0)).astype(BF)


def block_kernel(
    wq, wk, wv, wo, frames_hbm, cotangent_hbm, gain_hbm, lengths, lo_hbm, hi_hbm,
    total, gain_out, grad_frames_hbm, frames_out_hbm,
    nt, ct, ctx, gq, gk, gv, masked, frames, cotangent, gain, lo, hi, grad_frames, frames_out,
    held, w, nm, q6, gc6, kv, center, bias, rim_s, rim_r, send, recv, local, ring_send, ring_recv, *scratch
):
    me = Place()
    length = lengths[0]
    base = lax.axis_index("tm") * 256
    loads = ((frames_hbm, frames), (gain_hbm, gain), (cotangent_hbm, cotangent), (lo_hbm, lo), (hi_hbm, hi))
    loads = [pltpu.make_async_copy(src, dst, local.at[6 + n]) for n, (src, dst) in enumerate(loads)]
    for copy in loads:
        copy.start()
    rows = start_gather(me, (wq, wk, wv, wo), held, w, send, recv, local)

    def normalize():
        for copy in loads:
            copy.wait()

        @pl.loop(0, 8)
        def _(n):
            at = pl.ds(pl.multiple_of(n * 32, 32), 32)
            xhat, _ = norm(frames[at])
            nm[at] = (xhat * gain[...]).astype(BF)

    def prepare():
        nt[...] = nm[...].T

        @pl.loop(0, 8)
        def _(n):
            at = pl.ds(pl.multiple_of(n * 32, 32), 32)
            frame = base + n * 32 + lax.broadcasted_iota(jnp.int32, (32, 1536), 0)
            masked[at] = jnp.where(frame < length, cotangent[at].astype(F32), 0.0).astype(BF)

        for b in range(2):
            kp = base + 128 * (b - 1) + lax.broadcasted_iota(jnp.int32, (384, 128), 0)
            qp = base + 128 * b + lax.broadcasted_iota(jnp.int32, (384, 128), 1)
            cols = pl.ds(128 * b, 128)
            seen = (kp >= lo[:, cols]) & (kp < hi[:, cols]) & (kp < length)
            bias[b] = jnp.where(seen | (kp == qp), 0.0, -1e30)

    finish_gather(rows, normalize, prepare)

    def project(n):
        total = None
        for i in range(4):
            term = dot(nm[:, 384 * i:384 * i + 384], pair_rows(w, i, n))
            total = term if total is None else total + term
        return total.astype(BF)

    def halo(p, right):
        src, dst, by = (256, 0, 1) if right else (128, 384, 15)
        n = 2 * p + right
        return pltpu.make_async_remote_copy(
            src_ref=kv.at[p, :, pl.ds(src, 128)], dst_ref=kv.at[p, :, pl.ds(dst, 128)],
            send_sem=ring_send.at[n], recv_sem=ring_recv.at[n], device_id=me.along(by), device_id_type=MESH)

    def rim(p, right):
        n = 12 + 2 * p + right
        return pltpu.make_async_remote_copy(
            src_ref=rim_s.at[p, right], dst_ref=rim_r.at[p, right],
            send_sem=ring_send.at[n], recv_sem=ring_recv.at[n], device_id=me.along(1 if right else 15), device_id_type=MESH)

    for m in range(2):
        k = project(1 + m)
        for p in range(6):
            kv[p, m, 128:384] = k[:, 128 * p:128 * p + 128]
    for p in range(6):
        for right in range(2):
            halo(p, right).start()
    q = project(0)
    for p in range(6):
        q6[p] = q[:, 128 * p:128 * p + 128]
    for yh in range(2):
        g = (dot(masked[:, :768], out_rows(w, yh, 0), ROWS) + dot(masked[:, 768:], out_rows(w, yh, 1), ROWS)).astype(BF)
        for n in range(3):
            gc6[3 * yh + n] = g[:, 128 * n:128 * n + 128]

    @pl.loop(0, 6)
    def _(p):
        for right in range(2):
            halo(p, right).wait_recv()
        first = (lax.broadcasted_iota(jnp.int32, (128, 128), 1) < 64).astype(F32)
        even, odd = first.astype(BF), (1.0 - first).astype(BF)
        lanes = pl.ds(pl.multiple_of(128 * p, 128), 128)
        grads = []
        for b in range(2):
            at = pl.ds(128 * b, 128)
            q = q6[p, at]
            g = gc6[p, at]
            qm = jnp.concatenate([q * even, q * odd], 0)
            gm = jnp.concatenate([g * even, g * odd], 0)
            key = kv[p, 0, pl.ds(128 * b, 384)]
            value = kv[p, 1, pl.ds(128 * b, 384)]
            s = dot(key, qm, ROWS) * 0.125 + jnp.concatenate([bias[b], bias[b]], 1)
            e = jnp.exp(s - jnp.max(s, 0, keepdims=True))
            probs = e * (1.0 / jnp.sum(e, 0, keepdims=True))
            low = probs.astype(BF)
            grad = dot(value, gm, ROWS)
            delta = jnp.sum(probs * grad, 0, keepdims=True)
            ds = (probs * (grad - delta)).astype(BF)
            c = dot(value.T, low)
            c = jnp.concatenate([c[:64, :128], c[64:, 128:]], 0)
            ct[lanes, at] = c.astype(BF)
            ctx[at, lanes] = c.T.astype(BF)
            d = dot(key.T, ds)
            d = jnp.concatenate([d[:64, :128], d[64:, 128:]], 0) * 0.125
            gq[at, lanes] = d.T.astype(BF)
            grads.append((dot(ds, qm) * 0.125, dot(low, gm)))
        for m in range(2):
            here, there = grads[0][m], grads[1][m]
            rim_s[p, 0, m] = here[:128].astype(BF)
            rim_s[p, 1, m] = there[256:].astype(BF)
            center[p, m] = here[128:] + there[:256]
        for right in range(2):
            rim(p, right).start()

    for p in range(6):
        for right in range(2):
            rim(p, right).wait_recv()
        for m, out in enumerate((gk, gv)):
            lanes = pl.ds(128 * p, 128)
            out[:128, lanes] = (center[p, m, :128] + rim_r[p, 1, m].astype(F32)).astype(BF)
            out[128:, lanes] = (center[p, m, 128:] + rim_r[p, 0, m].astype(F32)).astype(BF)

    r0, fin, gt, gg, gsend, grecv = scratch[0], scratch[9], scratch[10], scratch[11], scratch[16], scratch[17]
    for_other, half = scratch[18:20]
    refs = (nt, ct, gq, gk, gv, masked)
    stages = reduce_stages(me, half, scratch)
    sum_gain = GainSum(me, gt, gg, gsend, grecv)

    def send_other(c):
        def put(at, v):
            for_other[(c,) + at] = v.astype(BF)
        weight_terms(refs, scratch, 1 - me.core, c, put)
        core_hop(me, scratch, c).start()

    def start_own(c):
        core_hop(me, scratch, c).wait_recv()

        def put(at, v):
            half[(c,) + at] = v + r0[(c,) + at].astype(F32)
        weight_terms(refs, scratch, me.core, c, put)
        stages[c][0].start()

    for c in range(3):
        send_other(c)
    for c in range(3):
        start_own(c)
    stages[0][0].relay()
    grad_normed(w, gq, gk, gv, center)
    stages[1][0].relay()
    stages[2][0].relay()
    norm_backward(frames, cotangent, gain, center, grad_frames, gt)
    stores = [
        pltpu.make_async_copy(grad_frames, grad_frames_hbm, local.at[11]),
        pltpu.make_async_copy(frames_out, frames_out_hbm, local.at[12]),
    ]
    stores[0].start()
    sum_gain.start(0)
    project_out(w, ctx, frames, length, frames_out)
    stores[1].start()
    for n in range(3):
        for c in range(3):
            stages[c][n].finish()
            if n < 2:
                stages[c][n + 1].start()
        sum_gain.finish(n)
        sum_gain.start(n + 1)
        if n < 2:
            for c in range(3):
                stages[c][n + 1].relay()

    def last(core):
        return pltpu.make_async_remote_copy(
            src_ref=fin.at[core], dst_ref=fin.at[core], send_sem=gsend.at[10], recv_sem=grecv.at[10],
            device_id=me.device(), device_id_type=MESH)

    last(me.core).start()
    sum_gain.finish(3)
    gain_out[...] = gt[4]
    for c in range(3):
        core_hop(me, scratch, c).wait_send()
        for n in range(3):
            stages[c][n].drain()
    sum_gain.drain()
    last(me.core).wait_send()
    last(1 - me.core).wait_recv()
    total[...] = fin[...]
    for p in range(6):
        for right in range(2):
            halo(p, right).wait_send()
            rim(p, right).wait_send()
    for row in rows:
        for stage in row:
            stage.drain()
    for copy in stores:
        copy.wait()


def block(wq, wk, wv, wo, *args):
    vm, hbm = pl.BlockSpec(memory_space=pltpu.VMEM), pl.BlockSpec(memory_space=pltpu.HBM)
    sds, sem = jax.ShapeDtypeStruct, pltpu.SemaphoreType.DMA
    return pl.pallas_call(
        block_kernel,
        out_shape=(sds((2, 3, 96, 128), F32), sds((16, 128), F32), sds((256, 1536), BF), sds((256, 1536), BF)),
        in_specs=[hbm] * 7 + [pl.BlockSpec(memory_space=pltpu.SMEM)] + [hbm] * 2,
        out_specs=(vm, vm, hbm, hbm),
        scratch_shapes=[
            pltpu.VMEM((1536, 256), BF), pltpu.VMEM((768, 256), BF), pltpu.VMEM((256, 768), BF),
            pltpu.VMEM((256, 768), BF), pltpu.VMEM((256, 768), BF), pltpu.VMEM((256, 768), BF),
            pltpu.VMEM((256, 1536), BF), pltpu.VMEM((256, 1536), BF), pltpu.VMEM((256, 1536), BF),
            pltpu.VMEM((1, 1536), F32), pltpu.VMEM((1, 256), jnp.int32), pltpu.VMEM((1, 256), jnp.int32),
            pltpu.VMEM((256, 1536), BF), pltpu.VMEM((256, 1536), BF),
            pltpu.VMEM((48, 16, 768), BF),
            pltpu.VMEM((2, 4, 2, 3, 2, 4, 16, 768), BF),
            pltpu.VMEM((256, 1536), BF),
            pltpu.VMEM((6, 256, 128), BF), pltpu.VMEM((6, 256, 128), BF),
            pltpu.VMEM((6, 2, 512, 128), BF),
            pltpu.VMEM((6, 2, 256, 128), F32),
            pltpu.VMEM((2, 384, 128), F32),
            pltpu.VMEM((6, 2, 2, 128, 128), BF), pltpu.VMEM((6, 2, 2, 128, 128), BF),
            sem((GATHER_SEMS,)), sem((GATHER_SEMS,)), sem((13,)), sem((24,)), sem((24,)),
        ] + reduce_scratch(),
        compiler_params=pltpu.CompilerParams(collective_id=0, has_side_effects=True, vmem_limit_bytes=67043328),
        name="block",
    )(wq.reshape(12, 16, 768), wk.reshape(12, 16, 768), wv.reshape(12, 16, 768), wo.reshape(6, 16, 1536), *args)


def outputs_kernel(total, gain, grad_in, frames_in, out_q, out_k, out_v, out_o, out_gain, grad_frames, frames_out):
    me = Place()
    frames_out[...] = frames_in[...]
    grad_frames[...] = grad_in[...]
    odd = lax.rem(me.x, 2)
    for h in range(2):
        for c in range(3):
            lanes = pl.ds(384 * h + 128 * c, 128)
            for n, out in enumerate((out_q, out_k, out_v)):
                t = total[h, c, pl.ds(24 * n, 24)]
                out[:, lanes] = jnp.where(me.core == 0, t[:12], t[12:])
            for b in range(2):
                lanes = pl.ds(768 * h + 256 * c + 128 * b, 128)
                for r in range(6):
                    even0, even1 = 8 * b + r, 8 * b + 6 + r if r < 2 else 14 + 4 * b + r
                    odd0, odd1 = 16 + 4 * b + r if r < 4 else 8 * b + r - 4, 8 * b + 2 + r
                    row = 72 + jnp.where(
                        odd == 0, jnp.where(me.core == 0, even0, even1), jnp.where(me.core == 0, odd0, odd1))
                    out_o[r:r + 1, lanes] = total[h, c, pl.ds(row, 1)]
    at = (lax.axis_index("dp") * 16 + lax.axis_index("tm")) * 12
    row, lane = at // 128, lax.rem(at, 128)
    both = jnp.concatenate([gain[pl.ds(row, 1)], gain[pl.ds(row + 1, 1)]], 1)
    both = jnp.broadcast_to(both, (8, 256))
    out_gain[...] = pltpu.roll(both, lax.rem(256 - lane, 256), 1)[:1, :12]


def write_outputs(*args):
    vm = pl.BlockSpec(memory_space=pltpu.VMEM)
    sds = jax.ShapeDtypeStruct
    return pl.pallas_call(
        outputs_kernel,
        out_shape=(sds((12, 768), F32),) * 3 + (
            sds((6, 1536), F32), sds((1, 12), F32), sds((256, 1536), BF), sds((256, 1536), BF)),
        in_specs=[vm] * 4,
        out_specs=(vm,) * 7,
        name="write_outputs",
    )(*args)


def per_device(
    frames, cotangent, layer_norm_gain, w_query, w_key, w_value, w_out, lengths, win_lo, win_hi
):
    gain = layer_norm_gain[None]
    sums = block(
        w_query, w_key, w_value, w_out, frames[0], cotangent[0], gain, lengths, win_lo, win_hi)
    grad_wq, grad_wk, grad_wv, grad_wo, grad_gain, grad_frames, frames_out = write_outputs(*sums)
    return (frames_out[None], grad_frames[None], grad_wq, grad_wk, grad_wv, grad_wo, grad_gain.reshape(12))


def solution(mesh):
    in_specs = (
        P("dp", "tm", None),
        P("dp", "tm", None),
        P(),
        P("dp", None),
        P("dp", None),
        P("dp", None),
        P("dp", None),
        P("dp"),
        P("dp", "tm"),
        P("dp", "tm"),
    )
    out_specs = (
        P("dp", "tm", None),
        P("dp", "tm", None),
        P(("dp", "tm"), None),
        P(("dp", "tm"), None),
        P(("dp", "tm"), None),
        P(("dp", "tm"), None),
        P(("dp", "tm")),
    )
    return jax.shard_map(
        per_device, mesh=mesh, in_specs=in_specs, out_specs=out_specs, check_vma=False
    )
```

```python
import jax
import jax.numpy as jnp
from jax import lax
from jax.experimental import pallas as pl
from jax.experimental.pallas import tpu as pltpu

from jax.sharding import PartitionSpec as P

MESH = pl.DeviceIdType.MESH
BF = jnp.bfloat16
F32 = jnp.float32


class Place:
    def __init__(self):
        dp, tm = lax.axis_index("dp"), lax.axis_index("tm")
        self.yh, self.z = dp // 4, lax.rem(dp, 4)
        self.yl, self.x, self.core = tm // 8, lax.rem(tm // 2, 4), lax.rem(tm, 2)
        self.y = self.yh * 2 + self.yl

    def at(self, axis):
        return {"x": self.x, "y": self.y, "z": self.z}[axis]

    def device(self, axis=None, j=None):
        y, z, x, core = self.y, self.z, self.x, self.core
        if axis == "x":
            x = j
        elif axis == "y":
            y = j
        elif axis == "z":
            z = j
        else:
            core = 1 - core
        return ((y // 2) * 4 + z, (lax.rem(y, 2) * 4 + x) * 2 + core)

    def along(self, by):
        return (lax.axis_index("dp"), lax.rem(lax.axis_index("tm") + by, 16))

    def right(self, axis):
        return lax.rem(self.at(axis) + 1, 4)

    def left(self, axis):
        return lax.rem(self.at(axis) + 3, 4)

    def over(self, axis):
        return lax.rem(self.at(axis) + 2, 4)


def greet(me, far=False, ring=False):
    barrier = pltpu.get_barrier_semaphore()
    for axis in "xyz":
        for j in (me.left(axis), me.right(axis)) + ((me.over(axis),) if far else ()):
            pl.semaphore_signal(barrier, inc=1, device_id=me.device(axis, j), device_id_type=MESH)
    pl.semaphore_signal(barrier, inc=1, device_id=me.device(), device_id_type=MESH)
    if ring:
        for by in (1, 15):
            pl.semaphore_signal(barrier, inc=1, device_id=me.along(by), device_id_type=MESH)
    pl.semaphore_wait(barrier, 7 + 3 * far + 2 * ring)


def gather_regions(me, w, h):
    return (
        (
            ("y", lambda j, p: w.at[j // 2, me.z, h, 0, lax.rem(j, 2), pl.ds(2 * p, 2)]),
            ("z", lambda j, p: w.at[p, j, h, 0]),
        ),
        (
            ("z", lambda j, p: w.at[me.yh, j, h, 1, me.yl, pl.ds(2 * p, 2)]),
            ("y", lambda j, p: w.at[j // 2, pl.ds(2 * p, 2), h, 1, lax.rem(j, 2)]),
        ),
        (
            ("z", lambda j, p: w.at[me.yh, j, h, 2, me.yl, me.x, :, pl.ds(384 * p, 384)]),
            ("y", lambda j, p: w.at[j // 2, pl.ds(2 * p, 2), h, 2, lax.rem(j, 2), me.x]),
            ("x", lambda j, p: w.at[p, :, h, 2, :, j]),
        ),
    )


class GatherStage:
    def __init__(self, me, axis, region, other, send, recv, base):
        self.me, self.axis, self.region, self.other = me, axis, region, other
        self.send, self.recv, self.base = send, recv, base

    def hop(self, k, j, p, right):
        me, n = self.me, self.base + k
        to = me.right(self.axis) if right else me.left(self.axis)
        part = self.region(j, p)
        return pltpu.make_async_remote_copy(
            src_ref=part, dst_ref=part, send_sem=self.send.at[n], recv_sem=self.recv.at[n],
            device_id=me.device(self.axis, to), device_id_type=MESH)

    def share(self, k, j, p, region=None):
        n = self.base + 6 + k
        part = (region or self.region)(j, p)
        return pltpu.make_async_remote_copy(
            src_ref=part, dst_ref=part, send_sem=self.send.at[n], recv_sem=self.recv.at[n],
            device_id=self.me.device(), device_id_type=MESH)

    def start(self):
        i = self.me.at(self.axis)
        self.hop(0, i, 0, True).start()
        self.hop(1, i, 1, False).start()
        self.hop(2, i, 1, True).start()
        self.hop(3, i, 0, False).start()

    def relay(self):
        me = self.me
        l, r = me.left(self.axis), me.right(self.axis)
        self.hop(0, l, 0, True).wait_recv()
        self.hop(4, l, 0, True).start()
        self.share(0, l, 0).start()
        self.hop(1, r, 1, False).wait_recv()
        self.hop(5, r, 1, False).start()
        self.share(1, r, 1).start()

    def finish(self):
        me = self.me
        l, r, o = me.left(self.axis), me.right(self.axis), me.over(self.axis)
        self.hop(2, l, 1, True).wait_recv()
        self.share(2, l, 1).start()
        self.hop(3, r, 0, False).wait_recv()
        self.share(3, r, 0).start()
        self.hop(4, o, 0, True).wait_recv()
        self.share(4, o, 0).start()
        self.hop(5, o, 1, False).wait_recv()
        self.share(5, o, 1).start()

    def arrive(self):
        me = self.me
        l, r, o = me.left(self.axis), me.right(self.axis), me.over(self.axis)
        for k, (j, p) in enumerate(((l, 0), (r, 1), (l, 1), (r, 0), (o, 0), (o, 1))):
            self.share(k, j, p, self.other).wait_recv()

    def drain(self):
        me = self.me
        i, l, r, o = me.at(self.axis), me.left(self.axis), me.right(self.axis), me.over(self.axis)
        for k, (j, p, right) in enumerate(((i, 0, True), (i, 1, False), (i, 1, True), (i, 0, False), (l, 0, True), (r, 1, False))):
            self.hop(k, j, p, right).wait_send()
        for k, (j, p) in enumerate(((l, 0), (r, 1), (l, 1), (r, 0), (o, 0), (o, 1))):
            self.share(k, j, p).wait_send()


def gather_stages(me, w, send, recv):
    mine, theirs = gather_regions(me, w, me.core), gather_regions(me, w, 1 - me.core)
    stages, base = [], 0
    for colour, other in zip(mine, theirs):
        row = []
        for (axis, region), (_, other_region) in zip(colour, other):
            row.append(GatherStage(me, axis, region, other_region, send, recv, base))
            base += 12
        stages.append(row)
    return stages


GATHER_SEMS = 84


def start_gather(me, shards, held, w, send, recv, local):
    wq, wk, wv, wo = shards
    loads = [pltpu.make_async_copy(part, held.at[pl.ds(12 * n, 12)], local.at[n]) for n, part in enumerate((wq, wk, wv))]
    for n in range(2):
        loads.append(pltpu.make_async_copy(wo.at[:, :, pl.ds(768 * n, 768)], held.at[pl.ds(36 + 6 * n, 6)], local.at[3 + n]))
    for copy in loads:
        copy.start()
    for copy in loads:
        copy.wait()
    own = []
    for h in range(2):
        for c in range(2):
            own.append((held.at[pl.ds(24 * h + 8 * c + 4 * me.yl, 4)], w.at[me.yh, me.z, h, c, me.yl]))
        own.append((held.at[24 * h + 16 + 4 * me.yl + me.x], w.at[me.yh, me.z, h, 2, me.yl, me.x]))
    own = [pltpu.make_async_copy(src, dst, local.at[n]) for n, (src, dst) in enumerate(own)]
    for copy in own:
        copy.start()
    greet(me, ring=True)
    for copy in own:
        copy.wait()
    rows = gather_stages(me, w, send, recv)
    for row in (rows[2], rows[0], rows[1]):
        row[0].start()
    return rows


def finish_gather(rows, first, second):
    a, b, c = rows
    c[0].relay()
    a[0].relay()
    b[0].relay()
    c[0].finish()
    c[1].start()
    a[0].finish()
    a[1].start()
    b[0].finish()
    c[1].relay()
    b[1].start()
    c[1].finish()
    c[2].start()
    first()
    a[1].relay()
    b[1].relay()
    second()
    c[2].relay()
    a[1].finish()
    b[1].finish()
    c[2].finish()
    for row in rows:
        for stage in row:
            stage.arrive()


def weight_rows(w, s, n):
    parts = []
    for k in range(3 * n, 3 * n + 3):
        parts.append(w[s // 4, s % 4, k // 6, k % 6 // 2, k % 2].reshape(64, 768))
    return jnp.concatenate(parts, 0)


def pair_rows(w, i, n):
    return jnp.concatenate([weight_rows(w, 2 * i, n), weight_rows(w, 2 * i + 1, n)], 0)


def out_rows(w, yh, b):
    parts = []
    for z in range(4):
        parts.append(w[yh, z, 1, 2, b].reshape(64, 768) if b else w[yh, z, 1, 1, 1].reshape(64, 768))
        middle = w[yh, z, 1, 2, 0, 2 * b:2 * b + 2].reshape(32, 768)
        parts.insert(len(parts) - 1 if b else len(parts), middle)
    return jnp.concatenate(parts, 0)


def norm(frames):
    xf = frames.astype(F32)
    mean = jnp.mean(xf, -1, keepdims=True)
    centered = xf - mean
    var = jnp.mean(centered * centered, -1, keepdims=True)
    inverse = lax.rsqrt(var + 1e-05)
    return centered * inverse, inverse


ROWS, COLS = (((1,), (1,)), ((), ())), (((1,), (0,)), ((), ()))


def dot(a, b, dims=COLS):
    return lax.dot_general(a, b, dims, preferred_element_type=F32)


ORDERS = (("x", "y", "z"), ("y", "z", "x"), ("z", "x", "y"))
DIMS = {"y": 0, "z": 1, "x": 2}


class ReduceStage:
    def __init__(self, me, axis, load, count, out, bufs, sems, base):
        self.me, self.axis, self.load, self.count, self.out = me, axis, load, count, out
        self.sent, self.got = bufs
        self.send, self.recv = sems
        self.base = base

    def hop(self, k):
        me = self.me
        to = me.right(self.axis) if k % 2 == 0 else me.left(self.axis)
        return pltpu.make_async_remote_copy(
            src_ref=self.sent.at[k], dst_ref=self.got.at[k],
            send_sem=self.send.at[self.base + k], recv_sem=self.recv.at[self.base + k],
            device_id=me.device(self.axis, to), device_id_type=MESH)

    def each(self, body):
        if self.count == 1:
            body(0)
        else:
            @pl.loop(0, self.count)
            def _(m):
                body(m)

    def fill(self, k, j, p, extra=None):
        def body(m):
            v = self.load(j, p, m)
            if extra is not None:
                v = v + self.got[extra, m].astype(F32)
            self.sent[k, m] = v.astype(self.sent.dtype)
        self.each(body)
        self.hop(k).start()

    def start(self):
        me = self.me
        l, r, o = me.left(self.axis), me.right(self.axis), me.over(self.axis)
        self.fill(0, o, 0)
        self.fill(1, o, 1)
        self.fill(2, r, 1)
        self.fill(3, l, 0)

    def relay(self):
        me = self.me
        self.hop(0).wait_recv()
        self.fill(4, me.right(self.axis), 0, 0)
        self.hop(1).wait_recv()
        self.fill(5, me.left(self.axis), 1, 1)

    def finish(self):
        me = self.me
        i = me.at(self.axis)
        for k in (2, 3, 4, 5):
            self.hop(k).wait_recv()

        for p, a, b in ((0, 4, 3), (1, 2, 5)):
            def body(m, p=p, a=a, b=b):
                v = self.load(i, p, m) + self.got[a, m].astype(F32) + self.got[b, m].astype(F32)
                self.out(p, m, v)
            self.each(body)

    def drain(self):
        for k in range(6):
            self.hop(k).wait_send()


class LastStage:
    def __init__(self, me, axis, terms, got, out, sems, base):
        self.me, self.axis, self.terms, self.got, self.out = me, axis, terms, got, out
        self.send, self.recv = sems
        self.base = base

    def hops(self):
        me = self.me
        to = (me.over(self.axis), me.right(self.axis), me.left(self.axis))
        return [
            pltpu.make_async_remote_copy(
                src_ref=self.terms.at[j], dst_ref=self.got.at[n], send_sem=self.send.at[self.base + n],
                recv_sem=self.recv.at[self.base + n], device_id=me.device(self.axis, j), device_id_type=MESH)
            for n, j in enumerate(to)
        ]

    def start(self):
        for hop in self.hops():
            hop.start()

    def relay(self):
        pass

    def finish(self):
        v = self.terms[self.me.at(self.axis)]
        for n, hop in enumerate(self.hops()):
            hop.wait_recv()
            v = v + self.got[n]
        self.out[...] = v

    def drain(self):
        for hop in self.hops():
            hop.wait_send()


class GainSum:
    def __init__(self, me, total, got, send, recv):
        self.me, self.total, self.got, self.send, self.recv = me, total, got, send, recv

    def hops(self, s):
        me = self.me
        if s == 3:
            devices = (me.device(),)
        else:
            axis = "xyz"[s]
            devices = tuple(me.device(axis, j) for j in (me.right(axis), me.left(axis), me.over(axis)))
        return [
            pltpu.make_async_remote_copy(
                src_ref=self.total.at[s], dst_ref=self.got.at[3 * s + n], send_sem=self.send.at[3 * s + n],
                recv_sem=self.recv.at[3 * s + n], device_id=device, device_id_type=MESH)
            for n, device in enumerate(devices)
        ]

    def start(self, s):
        for hop in self.hops(s):
            hop.start()

    def finish(self, s):
        v = self.total[s]
        for n, hop in enumerate(self.hops(s)):
            hop.wait_recv()
            v = v + self.got[3 * s + n]
        self.total[s + 1] = v

    def drain(self):
        for s in range(4):
            for hop in self.hops(s):
                hop.wait_send()


def reduce_scratch():
    sem = pltpu.SemaphoreType.DMA
    return [
        pltpu.VMEM((3, 6, 8, 96, 128), BF), pltpu.VMEM((3, 6, 8, 96, 128), BF),
        pltpu.VMEM((3, 6, 2, 96, 128), BF), pltpu.VMEM((3, 6, 2, 96, 128), BF),
        pltpu.VMEM((3, 3, 96, 128), F32),
        pltpu.VMEM((3, 4, 4, 96, 128), F32),
        pltpu.VMEM((3, 4, 96, 128), F32),
        pltpu.VMEM((2, 3, 96, 128), F32),
        pltpu.VMEM((5, 16, 128), F32), pltpu.VMEM((10, 16, 128), F32),
        sem((54,)), sem((54,)), sem((11,)), sem((11,)),
        pltpu.VMEM((3, 4, 4, 4, 96, 128), F32),
        pltpu.VMEM((1536, 384), F32), pltpu.VMEM((3, 768, 256), F32),
    ]


def reduce_stages(me, half, scratch):
    s1, d1, s2, d2, d3, t1, t2, fin, gt, gg, send, recv = scratch[:12]

    def load1(c):
        axis = ORDERS[c][0]

        def load(j, p, m):
            a, b = 2 * p + m // 4, lax.rem(m, 4)
            at = {"x": (a, b, j), "y": (j, a, b), "z": (a, j, b)}[axis]
            return half[(c,) + at]
        return load

    def out1(c):
        def out(p, m, v):
            t1[c, 2 * p + m // 4, lax.rem(m, 4)] = v
        return out

    def load2(c):
        def load(j, p, m):
            return t1[c, 2 * p + m, j] if c == 2 else t1[c, j, 2 * p + m]
        return load

    def out2(c):
        def out(p, m, v):
            t2[c, 2 * p + m] = v
        return out

    stages, base = [], 0
    for c in range(3):
        row = []
        for n, (load, out, bufs, count) in enumerate(
            ((load1, out1, (s1, d1), 8), (load2, out2, (s2, d2), 2))
        ):
            row.append(ReduceStage(me, ORDERS[c][n], load(c), count, out(c), (bufs[0].at[c], bufs[1].at[c]), (send, recv), base))
            base += 6
        row.append(LastStage(me, ORDERS[c][2], t2.at[c], d3.at[c], fin.at[me.core, c], (send, recv), base))
        base += 6
        stages.append(row)
    return stages


def out_terms(refs, scratch, core, c):
    ct, masked, prod_o = refs[1], refs[5], scratch[16]
    columns = pl.ds(pl.multiple_of(core * 768 + c * 256, 128), 256)
    prod_o[c] = dot(ct[...], masked[:, columns])


def weight_terms(refs, scratch, core, c):
    nt, _, gq, gk, gv, _ = refs
    half, prod, prod_o = scratch[14:17]
    columns = pl.ds(pl.multiple_of(core * 384 + c * 128, 128), 128)
    rhs = jnp.concatenate([gq[:, columns], gk[:, columns], gv[:, columns]], 1)
    prod[...] = dot(nt[...], rhs)

    @pl.loop(0, 32)
    def _(pair):
        upper = lax.broadcasted_iota(jnp.int32, (8, 128), 0) < 4
        at = pl.multiple_of(pair * 24, 8)
        tiles = [[prod_o[c, pl.ds(at + 8 * n, 8), pl.ds(128 * b, 128)] for b in range(2)] for n in range(3)]
        mixed = (
            jnp.where(upper, tiles[1][0], pltpu.roll(tiles[1][1], 4, 0)),
            jnp.where(upper, pltpu.roll(tiles[1][0], 4, 0), tiles[1][1]),
        )
        yh, z, yl, xh = pair // 16, lax.rem(pair // 4, 4), lax.rem(pair // 2, 2), lax.rem(pair, 2)
        for odd in range(2):
            rows = pl.ds(pl.multiple_of(pair * 48 + 24 * odd, 8), 24)
            parts = [prod[rows, pl.ds(128 * n, 128)] for n in range(3)]
            parts += [tiles[2 * odd][0], tiles[2 * odd][1], mixed[odd]]
            half[c, yh * 2 + yl, z, xh * 2 + odd] = jnp.concatenate(parts, 0)


def grad_normed(w, gq, gk, gv, out):
    for s in range(4):
        total = None
        for n, g in enumerate((gq, gk, gv)):
            term = dot(g[:256], pair_rows(w, s, n), ROWS)
            total = term if total is None else total + term
        for b in range(3 * s, 3 * s + 3):
            out[b // 2, b % 2] = total[:, 128 * (b - 3 * s):128 * (b - 3 * s) + 128]


def norm_backward(frames, cotangent, gain, gn, grad_frames, gain_total):
    gain_total[0] = jnp.zeros((16, 128), F32)

    @pl.loop(0, 8)
    def _(n):
        rows = pl.ds(pl.multiple_of(n * 32, 32), 32)
        xhat, inverse = norm(frames[rows])
        grad = jnp.concatenate([gn[b // 2, b % 2, rows] for b in range(12)], 1)
        gx = grad * xhat
        for b in range(12):
            gain_total[0, b:b + 1] += jnp.sum(gx[:, 128 * b: 128 * b + 128], 0, keepdims=True)
        g = grad * gain[...]
        first = jnp.mean(g, -1, keepdims=True)
        second = jnp.mean(gx * gain[...], -1, keepdims=True)
        back = inverse * (g - first - xhat * second)
        grad_frames[rows] = (cotangent[rows].astype(F32) + back).astype(BF)


def project_out(w, ctx, frames, length, out):
    base = lax.axis_index("tm") * 256
    for b in range(2):
        attn = dot(ctx[:, :384], out_rows(w, 0, b)) + dot(ctx[:, 384:], out_rows(w, 1, b))
        lanes = pl.ds(768 * b, 768)
        frame = base + lax.broadcasted_iota(jnp.int32, (256, 768), 0)
        out[:, lanes] = (frames[:, lanes].astype(F32) + jnp.where(frame < length, attn, 0.0)).astype(BF)


def block_kernel(
    wq, wk, wv, wo, frames_hbm, cotangent_hbm, gain_hbm, lengths, lo_hbm, hi_hbm,
    total, gain_out, grad_frames_hbm, frames_out_hbm,
    nt, ct, ctx, gq, gk, gv, masked, frames, cotangent, gain, lo, hi, grad_frames, frames_out,
    held, w, nm, q6, gc6, kv, center, bias, rim_s, rim_r, send, recv, local, ring_send, ring_recv, twin_send, twin_recv, *scratch
):
    me = Place()
    length = lengths[0]
    base = lax.axis_index("tm") * 256
    loads = ((frames_hbm, frames), (gain_hbm, gain), (cotangent_hbm, cotangent), (lo_hbm, lo), (hi_hbm, hi))
    loads = [pltpu.make_async_copy(src, dst, local.at[6 + n]) for n, (src, dst) in enumerate(loads)]
    for copy in loads:
        copy.start()
    rows = start_gather(me, (wq, wk, wv, wo), held, w, send, recv, local)

    def twin(n):
        across = lambda width: pl.ds(pl.multiple_of((1 - me.core) * width, 128), width)
        ref = (nt, masked, ct, gq, gk, gv)[n]
        if n in (0, 2):
            src, dst = ref.at[:, pl.ds(0, 256)], ref.at[:, pl.ds(256, 256)]
        else:
            lanes = across(768 if n == 1 else 384)
            src, dst = ref.at[pl.ds(0, 256), lanes], ref.at[pl.ds(256, 256), lanes]
        return pltpu.make_async_remote_copy(
            src_ref=src, dst_ref=dst, send_sem=twin_send.at[n], recv_sem=twin_recv.at[n],
            device_id=me.device(), device_id_type=MESH)

    def normalize():
        for copy in loads:
            copy.wait()

        @pl.loop(0, 8)
        def _(n):
            at = pl.ds(pl.multiple_of(n * 32, 32), 32)
            xhat, _ = norm(frames[at])
            nm[at] = (xhat * gain[...]).astype(BF)

    def prepare():
        nt[:, :256] = nm[...].T
        twin(0).start()

        @pl.loop(0, 8)
        def _(n):
            at = pl.ds(pl.multiple_of(n * 32, 32), 32)
            frame = base + n * 32 + lax.broadcasted_iota(jnp.int32, (32, 1536), 0)
            masked[at] = jnp.where(frame < length, cotangent[at].astype(F32), 0.0).astype(BF)
        twin(1).start()

        for b in range(2):
            kp = base + 128 * (b - 1) + lax.broadcasted_iota(jnp.int32, (384, 128), 0)
            qp = base + 128 * b + lax.broadcasted_iota(jnp.int32, (384, 128), 1)
            cols = pl.ds(128 * b, 128)
            seen = (kp >= lo[:, cols]) & (kp < hi[:, cols]) & (kp < length)
            bias[b] = jnp.where(seen | (kp == qp), 0.0, -1e30)

    finish_gather(rows, normalize, prepare)

    def project(n):
        total = None
        for i in range(4):
            term = dot(nm[:, 384 * i:384 * i + 384], pair_rows(w, i, n))
            total = term if total is None else total + term
        return total.astype(BF)

    def halo(p, right):
        src, dst, by = (256, 0, 1) if right else (128, 384, 15)
        n = 2 * p + right
        return pltpu.make_async_remote_copy(
            src_ref=kv.at[p, :, pl.ds(src, 128)], dst_ref=kv.at[p, :, pl.ds(dst, 128)],
            send_sem=ring_send.at[n], recv_sem=ring_recv.at[n], device_id=me.along(by), device_id_type=MESH)

    def rim(p, right):
        n = 12 + 2 * p + right
        return pltpu.make_async_remote_copy(
            src_ref=rim_s.at[p, right], dst_ref=rim_r.at[p, right],
            send_sem=ring_send.at[n], recv_sem=ring_recv.at[n], device_id=me.along(1 if right else 15), device_id_type=MESH)

    for m in range(2):
        k = project(1 + m)
        for p in range(6):
            kv[p, m, 128:384] = k[:, 128 * p:128 * p + 128]
    for p in range(6):
        for right in range(2):
            halo(p, right).start()
    q = project(0)
    for p in range(6):
        q6[p] = q[:, 128 * p:128 * p + 128]
    for yh in range(2):
        g = (dot(masked[:256, :768], out_rows(w, yh, 0), ROWS) + dot(masked[:256, 768:], out_rows(w, yh, 1), ROWS)).astype(BF)
        for n in range(3):
            gc6[3 * yh + n] = g[:, 128 * n:128 * n + 128]

    @pl.loop(0, 6)
    def _(p):
        for right in range(2):
            halo(p, right).wait_recv()
        first = (lax.broadcasted_iota(jnp.int32, (128, 128), 1) < 64).astype(F32)
        even, odd = first.astype(BF), (1.0 - first).astype(BF)
        lanes = pl.ds(pl.multiple_of(128 * p, 128), 128)
        grads = []
        for b in range(2):
            at = pl.ds(128 * b, 128)
            q = q6[p, at]
            g = gc6[p, at]
            qm = jnp.concatenate([q * even, q * odd], 0)
            gm = jnp.concatenate([g * even, g * odd], 0)
            key = kv[p, 0, pl.ds(128 * b, 384)]
            value = kv[p, 1, pl.ds(128 * b, 384)]
            s = dot(key, qm, ROWS) * 0.125 + jnp.concatenate([bias[b], bias[b]], 1)
            e = jnp.exp(s - jnp.max(s, 0, keepdims=True))
            probs = e * (1.0 / jnp.sum(e, 0, keepdims=True))
            low = probs.astype(BF)
            grad = dot(value, gm, ROWS)
            delta = jnp.sum(probs * grad, 0, keepdims=True)
            ds = (probs * (grad - delta)).astype(BF)
            c = dot(value.T, low)
            c = jnp.concatenate([c[:64, :128], c[64:, 128:]], 0)
            ct[lanes, at] = c.astype(BF)
            ctx[at, lanes] = c.T.astype(BF)
            d = dot(key.T, ds)
            d = jnp.concatenate([d[:64, :128], d[64:, 128:]], 0) * 0.125
            gq[at, lanes] = d.T.astype(BF)
            grads.append((dot(ds, qm) * 0.125, dot(low, gm)))
        for m in range(2):
            here, there = grads[0][m], grads[1][m]
            rim_s[p, 0, m] = here[:128].astype(BF)
            rim_s[p, 1, m] = there[256:].astype(BF)
            center[p, m] = here[128:] + there[:256]
        for right in range(2):
            rim(p, right).start()

    twin(2).start()
    twin(3).start()
    for p in range(6):
        for right in range(2):
            rim(p, right).wait_recv()
        for m, out in enumerate((gk, gv)):
            lanes = pl.ds(128 * p, 128)
            out[:128, lanes] = (center[p, m, :128] + rim_r[p, 1, m].astype(F32)).astype(BF)
            out[128:256, lanes] = (center[p, m, 128:] + rim_r[p, 0, m].astype(F32)).astype(BF)

    twin(4).start()
    twin(5).start()
    fin, gt, gg = scratch[7:10]
    gsend, grecv, half = scratch[12:15]
    refs = (nt, ct, gq, gk, gv, masked)
    stages = reduce_stages(me, half, scratch)
    sum_gain = GainSum(me, gt, gg, gsend, grecv)

    for n in range(3):
        twin(n).wait_recv()
    for c in range(3):
        out_terms(refs, scratch, me.core, c)
    for n in range(3, 6):
        twin(n).wait_recv()
    for c in range(3):
        weight_terms(refs, scratch, me.core, c)
        stages[c][0].start()
    grad_normed(w, gq, gk, gv, center)
    for c in range(3):
        stages[c][0].relay()
    norm_backward(frames, cotangent, gain, center, grad_frames, gt)
    stores = [
        pltpu.make_async_copy(grad_frames, grad_frames_hbm, local.at[11]),
        pltpu.make_async_copy(frames_out, frames_out_hbm, local.at[12]),
    ]
    stores[0].start()
    sum_gain.start(0)
    project_out(w, ctx, frames, length, frames_out)
    stores[1].start()
    for n in range(3):
        for c in range(3):
            stages[c][n].finish()
            if n < 2:
                stages[c][n + 1].start()
        sum_gain.finish(n)
        sum_gain.start(n + 1)
        if n < 2:
            for c in range(3):
                stages[c][n + 1].relay()

    def last(core):
        return pltpu.make_async_remote_copy(
            src_ref=fin.at[core], dst_ref=fin.at[core], send_sem=gsend.at[10], recv_sem=grecv.at[10],
            device_id=me.device(), device_id_type=MESH)

    last(me.core).start()
    sum_gain.finish(3)
    gain_out[...] = gt[4]
    for c in range(3):
        for n in range(3):
            stages[c][n].drain()
    sum_gain.drain()
    for n in range(6):
        twin(n).wait_send()
    last(me.core).wait_send()
    last(1 - me.core).wait_recv()
    total[...] = fin[...]
    for p in range(6):
        for right in range(2):
            halo(p, right).wait_send()
            rim(p, right).wait_send()
    for row in rows:
        for stage in row:
            stage.drain()
    for copy in stores:
        copy.wait()


def block(wq, wk, wv, wo, *args):
    vm, hbm = pl.BlockSpec(memory_space=pltpu.VMEM), pl.BlockSpec(memory_space=pltpu.HBM)
    sds, sem = jax.ShapeDtypeStruct, pltpu.SemaphoreType.DMA
    return pl.pallas_call(
        block_kernel,
        out_shape=(sds((2, 3, 96, 128), F32), sds((16, 128), F32), sds((256, 1536), BF), sds((256, 1536), BF)),
        in_specs=[hbm] * 7 + [pl.BlockSpec(memory_space=pltpu.SMEM)] + [hbm] * 2,
        out_specs=(vm, vm, hbm, hbm),
        scratch_shapes=[
            pltpu.VMEM((1536, 512), BF), pltpu.VMEM((768, 512), BF), pltpu.VMEM((256, 768), BF),
            pltpu.VMEM((512, 768), BF), pltpu.VMEM((512, 768), BF), pltpu.VMEM((512, 768), BF),
            pltpu.VMEM((512, 1536), BF), pltpu.VMEM((256, 1536), BF), pltpu.VMEM((256, 1536), BF),
            pltpu.VMEM((1, 1536), F32), pltpu.VMEM((1, 256), jnp.int32), pltpu.VMEM((1, 256), jnp.int32),
            pltpu.VMEM((256, 1536), BF), pltpu.VMEM((256, 1536), BF),
            pltpu.VMEM((48, 16, 768), BF),
            pltpu.VMEM((2, 4, 2, 3, 2, 4, 16, 768), BF),
            pltpu.VMEM((256, 1536), BF),
            pltpu.VMEM((6, 256, 128), BF), pltpu.VMEM((6, 256, 128), BF),
            pltpu.VMEM((6, 2, 512, 128), BF),
            pltpu.VMEM((6, 2, 256, 128), F32),
            pltpu.VMEM((2, 384, 128), F32),
            pltpu.VMEM((6, 2, 2, 128, 128), BF), pltpu.VMEM((6, 2, 2, 128, 128), BF),
            sem((GATHER_SEMS,)), sem((GATHER_SEMS,)), sem((13,)), sem((24,)), sem((24,)), sem((6,)), sem((6,)),
        ] + reduce_scratch(),
        compiler_params=pltpu.CompilerParams(collective_id=0, has_side_effects=True, vmem_limit_bytes=67043328),
        name="block",
    )(wq.reshape(12, 16, 768), wk.reshape(12, 16, 768), wv.reshape(12, 16, 768), wo.reshape(6, 16, 1536), *args)


def outputs_kernel(total, gain, grad_in, frames_in, out_q, out_k, out_v, out_o, out_gain, grad_frames, frames_out):
    me = Place()
    frames_out[...] = frames_in[...]
    grad_frames[...] = grad_in[...]
    odd = lax.rem(me.x, 2)
    for h in range(2):
        for c in range(3):
            lanes = pl.ds(384 * h + 128 * c, 128)
            for n, out in enumerate((out_q, out_k, out_v)):
                t = total[h, c, pl.ds(24 * n, 24)]
                out[:, lanes] = jnp.where(me.core == 0, t[:12], t[12:])
            for b in range(2):
                lanes = pl.ds(768 * h + 256 * c + 128 * b, 128)
                for r in range(6):
                    even0, even1 = 8 * b + r, 8 * b + 6 + r if r < 2 else 14 + 4 * b + r
                    odd0, odd1 = 16 + 4 * b + r if r < 4 else 8 * b + r - 4, 8 * b + 2 + r
                    row = 72 + jnp.where(
                        odd == 0, jnp.where(me.core == 0, even0, even1), jnp.where(me.core == 0, odd0, odd1))
                    out_o[r:r + 1, lanes] = total[h, c, pl.ds(row, 1)]
    at = (lax.axis_index("dp") * 16 + lax.axis_index("tm")) * 12
    row, lane = at // 128, lax.rem(at, 128)
    both = jnp.concatenate([gain[pl.ds(row, 1)], gain[pl.ds(row + 1, 1)]], 1)
    both = jnp.broadcast_to(both, (8, 256))
    out_gain[...] = pltpu.roll(both, lax.rem(256 - lane, 256), 1)[:1, :12]


def write_outputs(*args):
    vm = pl.BlockSpec(memory_space=pltpu.VMEM)
    sds = jax.ShapeDtypeStruct
    return pl.pallas_call(
        outputs_kernel,
        out_shape=(sds((12, 768), F32),) * 3 + (
            sds((6, 1536), F32), sds((1, 12), F32), sds((256, 1536), BF), sds((256, 1536), BF)),
        in_specs=[vm] * 4,
        out_specs=(vm,) * 7,
        name="write_outputs",
    )(*args)


def per_device(
    frames, cotangent, layer_norm_gain, w_query, w_key, w_value, w_out, lengths, win_lo, win_hi
):
    gain = layer_norm_gain[None]
    sums = block(
        w_query, w_key, w_value, w_out, frames[0], cotangent[0], gain, lengths, win_lo, win_hi)
    grad_wq, grad_wk, grad_wv, grad_wo, grad_gain, grad_frames, frames_out = write_outputs(*sums)
    return (frames_out[None], grad_frames[None], grad_wq, grad_wk, grad_wv, grad_wo, grad_gain.reshape(12))


def solution(mesh):
    in_specs = (
        P("dp", "tm", None),
        P("dp", "tm", None),
        P(),
        P("dp", None),
        P("dp", None),
        P("dp", None),
        P("dp", None),
        P("dp"),
        P("dp", "tm"),
        P("dp", "tm"),
    )
    out_specs = (
        P("dp", "tm", None),
        P("dp", "tm", None),
        P(("dp", "tm"), None),
        P(("dp", "tm"), None),
        P(("dp", "tm"), None),
        P(("dp", "tm"), None),
        P(("dp", "tm")),
    )
    return jax.shard_map(
        per_device, mesh=mesh, in_specs=in_specs, out_specs=out_specs, check_vma=False
    )
```

```python
import jax
import jax.numpy as jnp
from jax import lax
from jax.experimental import pallas as pl
from jax.experimental.pallas import tpu as pltpu

from jax.sharding import PartitionSpec as P

MESH = pl.DeviceIdType.MESH
BF = jnp.bfloat16
F32 = jnp.float32


class Place:
    def __init__(self):
        dp, tm = lax.axis_index("dp"), lax.axis_index("tm")
        self.yh, self.z = dp // 4, lax.rem(dp, 4)
        self.yl, self.x, self.core = tm // 8, lax.rem(tm // 2, 4), lax.rem(tm, 2)
        self.y = self.yh * 2 + self.yl

    def at(self, axis):
        return {"x": self.x, "y": self.y, "z": self.z}[axis]

    def device(self, axis=None, j=None):
        y, z, x, core = self.y, self.z, self.x, self.core
        if axis == "x":
            x = j
        elif axis == "y":
            y = j
        elif axis == "z":
            z = j
        else:
            core = 1 - core
        return ((y // 2) * 4 + z, (lax.rem(y, 2) * 4 + x) * 2 + core)

    def along(self, by):
        return (lax.axis_index("dp"), lax.rem(lax.axis_index("tm") + by, 16))

    def right(self, axis):
        return lax.rem(self.at(axis) + 1, 4)

    def left(self, axis):
        return lax.rem(self.at(axis) + 3, 4)

    def over(self, axis):
        return lax.rem(self.at(axis) + 2, 4)


def greet(me, far=False, ring=False):
    barrier = pltpu.get_barrier_semaphore()
    for axis in "xyz":
        for j in (me.left(axis), me.right(axis)) + ((me.over(axis),) if far else ()):
            pl.semaphore_signal(barrier, inc=1, device_id=me.device(axis, j), device_id_type=MESH)
    pl.semaphore_signal(barrier, inc=1, device_id=me.device(), device_id_type=MESH)
    if ring:
        for by in (1, 15):
            pl.semaphore_signal(barrier, inc=1, device_id=me.along(by), device_id_type=MESH)
    pl.semaphore_wait(barrier, 7 + 3 * far + 2 * ring)


def gather_regions(me, w, h):
    return (
        (
            ("y", lambda j, p: w.at[j // 2, me.z, h, 0, lax.rem(j, 2), pl.ds(2 * p, 2)]),
            ("z", lambda j, p: w.at[p, j, h, 0]),
        ),
        (
            ("z", lambda j, p: w.at[me.yh, j, h, 1, me.yl, pl.ds(2 * p, 2)]),
            ("y", lambda j, p: w.at[j // 2, pl.ds(2 * p, 2), h, 1, lax.rem(j, 2)]),
        ),
        (
            ("z", lambda j, p: w.at[me.yh, j, h, 2, p, me.x]),
            ("cross", lambda j, p: w.at[j, pl.ds(2 * p, 2), h, 2, :, me.x]),
            ("x", lambda j, p: w.at[1 - me.yh if p else me.yh, :, h, 2, :, j]),
        ),
    )


class GatherStage:
    def __init__(self, me, axis, region, other, send, recv, base):
        self.me, self.axis, self.region, self.other = me, axis, region, other
        self.send, self.recv, self.base = send, recv, base

    def hop(self, k, j, p, right):
        me, n = self.me, self.base + k
        to = me.right(self.axis) if right else me.left(self.axis)
        part = self.region(j, p)
        return pltpu.make_async_remote_copy(
            src_ref=part, dst_ref=part, send_sem=self.send.at[n], recv_sem=self.recv.at[n],
            device_id=me.device(self.axis, to), device_id_type=MESH)

    def share(self, k, j, p, region=None):
        n = self.base + 6 + k
        part = (region or self.region)(j, p)
        return pltpu.make_async_remote_copy(
            src_ref=part, dst_ref=part, send_sem=self.send.at[n], recv_sem=self.recv.at[n],
            device_id=self.me.device(), device_id_type=MESH)

    def start(self):
        i = self.me.at(self.axis)
        self.hop(0, i, 0, True).start()
        self.hop(1, i, 1, False).start()
        self.hop(2, i, 1, True).start()
        self.hop(3, i, 0, False).start()

    def start_half(self, p):
        i = self.me.at(self.axis)
        for k, right in ((1, False), (2, True)) if p else ((0, True), (3, False)):
            self.hop(k, i, p, right).start()

    def relay(self):
        me = self.me
        l, r = me.left(self.axis), me.right(self.axis)
        self.hop(0, l, 0, True).wait_recv()
        self.hop(4, l, 0, True).start()
        self.share(0, l, 0).start()
        self.hop(1, r, 1, False).wait_recv()
        self.hop(5, r, 1, False).start()
        self.share(1, r, 1).start()

    def finish(self):
        me = self.me
        l, r, o = me.left(self.axis), me.right(self.axis), me.over(self.axis)
        self.hop(2, l, 1, True).wait_recv()
        self.share(2, l, 1).start()
        self.hop(3, r, 0, False).wait_recv()
        self.share(3, r, 0).start()
        self.hop(4, o, 0, True).wait_recv()
        self.share(4, o, 0).start()
        self.hop(5, o, 1, False).wait_recv()
        self.share(5, o, 1).start()

    def arrive(self):
        me = self.me
        l, r, o = me.left(self.axis), me.right(self.axis), me.over(self.axis)
        for k, (j, p) in enumerate(((l, 0), (r, 1), (l, 1), (r, 0), (o, 0), (o, 1))):
            self.share(k, j, p, self.other).wait_recv()

    def drain(self):
        me = self.me
        i, l, r, o = me.at(self.axis), me.left(self.axis), me.right(self.axis), me.over(self.axis)
        for k, (j, p, right) in enumerate(((i, 0, True), (i, 1, False), (i, 1, True), (i, 0, False), (l, 0, True), (r, 1, False))):
            self.hop(k, j, p, right).wait_send()
        for k, (j, p) in enumerate(((l, 0), (r, 1), (l, 1), (r, 0), (o, 0), (o, 1))):
            self.share(k, j, p).wait_send()


class CrossStage(GatherStage):
    def hop(self, k):
        me, n = self.me, self.base + k
        part = self.region(me.yh, k)
        return pltpu.make_async_remote_copy(
            src_ref=part, dst_ref=part, send_sem=self.send.at[n], recv_sem=self.recv.at[n],
            device_id=me.device("y", 3 - me.y), device_id_type=MESH)

    def start(self):
        for k in range(2):
            self.hop(k).start()

    def finish(self):
        for k in range(2):
            self.hop(k).wait_recv()
            self.share(k, 1 - self.me.yh, k).start()

    def arrive(self):
        for k in range(2):
            self.share(k, 1 - self.me.yh, k, self.other).wait_recv()

    def drain(self):
        for k in range(2):
            self.hop(k).wait_send()
            self.share(k, 1 - self.me.yh, k).wait_send()


def gather_stages(me, w, send, recv):
    mine, theirs = gather_regions(me, w, me.core), gather_regions(me, w, 1 - me.core)
    stages, base = [], 0
    for colour, other in zip(mine, theirs):
        row = []
        for (axis, region), (_, other_region) in zip(colour, other):
            kind = CrossStage if axis == "cross" else GatherStage
            row.append(kind(me, axis, region, other_region, send, recv, base))
            base += 12
        stages.append(row)
    return stages


GATHER_SEMS = 84


def start_gather(me, shards, held, w, send, recv, local):
    wq, wk, wv, wo = shards
    loads = [pltpu.make_async_copy(part, held.at[pl.ds(12 * n, 12)], local.at[n]) for n, part in enumerate((wq, wk, wv))]
    for n in range(2):
        loads.append(pltpu.make_async_copy(wo.at[:, :, pl.ds(768 * n, 768)], held.at[pl.ds(36 + 6 * n, 6)], local.at[3 + n]))
    for copy in loads:
        copy.start()
    for copy in loads:
        copy.wait()
    own = []
    for h in range(2):
        for c in range(2):
            own.append((held.at[pl.ds(24 * h + 8 * c + 4 * me.yl, 4)], w.at[me.yh, me.z, h, c, me.yl]))
        for yl in range(2):
            own.append((held.at[24 * h + 16 + 4 * yl + me.x], w.at[me.yh, me.z, h, 2, yl, me.x]))
    own = [pltpu.make_async_copy(src, dst, local.at[n if n < 6 else 7 + n]) for n, (src, dst) in enumerate(own)]
    for copy in own:
        copy.start()
    greet(me, ring=True)
    for copy in own:
        copy.wait()
    rows = gather_stages(me, w, send, recv)
    for row in (rows[2], rows[0], rows[1]):
        row[0].start()
    return rows


def finish_gather(rows, first, second):
    a, b, c = rows
    c[0].relay()
    a[0].relay()
    b[0].relay()
    c[0].finish()
    c[1].start()
    c[2].start_half(0)
    a[0].finish()
    a[1].start()
    b[0].finish()
    b[1].start()
    first()
    c[1].finish()
    c[2].start_half(1)
    a[1].relay()
    second()
    b[1].relay()
    c[2].relay()
    a[1].finish()
    b[1].finish()
    c[2].finish()
    for row in rows:
        for stage in row:
            stage.arrive()


def weight_rows(w, s, n):
    parts = []
    for k in range(3 * n, 3 * n + 3):
        parts.append(w[s // 4, s % 4, k // 6, k % 6 // 2, k % 2].reshape(64, 768))
    return jnp.concatenate(parts, 0)


def pair_rows(w, i, n):
    return jnp.concatenate([weight_rows(w, 2 * i, n), weight_rows(w, 2 * i + 1, n)], 0)


def out_rows(w, yh, b):
    parts = []
    for z in range(4):
        parts.append(w[yh, z, 1, 2, b].reshape(64, 768) if b else w[yh, z, 1, 1, 1].reshape(64, 768))
        middle = w[yh, z, 1, 2, 0, 2 * b:2 * b + 2].reshape(32, 768)
        parts.insert(len(parts) - 1 if b else len(parts), middle)
    return jnp.concatenate(parts, 0)


def norm(frames):
    xf = frames.astype(F32)
    mean = jnp.mean(xf, -1, keepdims=True)
    centered = xf - mean
    var = jnp.mean(centered * centered, -1, keepdims=True)
    inverse = lax.rsqrt(var + 1e-05)
    return centered * inverse, inverse


ROWS, COLS = (((1,), (1,)), ((), ())), (((1,), (0,)), ((), ()))


def dot(a, b, dims=COLS):
    return lax.dot_general(a, b, dims, preferred_element_type=F32)


ORDERS = (("x", "y", "z"), ("y", "z", "x"), ("z", "x", "y"))
DIMS = {"y": 0, "z": 1, "x": 2}


class ReduceStage:
    def __init__(self, me, axis, load, count, out, bufs, sems, base):
        self.me, self.axis, self.load, self.count, self.out = me, axis, load, count, out
        self.sent, self.got = bufs
        self.send, self.recv = sems
        self.base = base

    def hop(self, k):
        me = self.me
        to = me.right(self.axis) if k % 2 == 0 else me.left(self.axis)
        return pltpu.make_async_remote_copy(
            src_ref=self.sent.at[k], dst_ref=self.got.at[k],
            send_sem=self.send.at[self.base + k], recv_sem=self.recv.at[self.base + k],
            device_id=me.device(self.axis, to), device_id_type=MESH)

    def each(self, body):
        if self.count == 1:
            body(0)
        else:
            @pl.loop(0, self.count)
            def _(m):
                body(m)

    def fill(self, k, j, p, extra=None):
        def body(m):
            v = self.load(j, p, m)
            if extra is not None:
                v = v + self.got[extra, m].astype(F32)
            self.sent[k, m] = v.astype(self.sent.dtype)
        self.each(body)
        self.hop(k).start()

    def start(self):
        me = self.me
        l, r, o = me.left(self.axis), me.right(self.axis), me.over(self.axis)
        self.fill(0, o, 0)
        self.fill(1, o, 1)
        self.fill(2, r, 1)
        self.fill(3, l, 0)

    def relay(self):
        me = self.me
        self.hop(0).wait_recv()
        self.fill(4, me.right(self.axis), 0, 0)
        self.hop(1).wait_recv()
        self.fill(5, me.left(self.axis), 1, 1)

    def finish(self):
        me = self.me
        i = me.at(self.axis)
        for k in (2, 3, 4, 5):
            self.hop(k).wait_recv()

        for p, a, b in ((0, 4, 3), (1, 2, 5)):
            def body(m, p=p, a=a, b=b):
                v = self.load(i, p, m) + self.got[a, m].astype(F32) + self.got[b, m].astype(F32)
                self.out(p, m, v)
            self.each(body)

    def drain(self):
        for k in range(6):
            self.hop(k).wait_send()


class LastStage:
    def __init__(self, me, axis, terms, got, out, sems, base):
        self.me, self.axis, self.terms, self.got, self.out = me, axis, terms, got, out
        self.send, self.recv = sems
        self.base = base

    def hops(self):
        me = self.me
        to = (me.over(self.axis), me.right(self.axis), me.left(self.axis))
        return [
            pltpu.make_async_remote_copy(
                src_ref=self.terms.at[j], dst_ref=self.got.at[n], send_sem=self.send.at[self.base + n],
                recv_sem=self.recv.at[self.base + n], device_id=me.device(self.axis, j), device_id_type=MESH)
            for n, j in enumerate(to)
        ]

    def start(self):
        for hop in self.hops():
            hop.start()

    def relay(self):
        pass

    def finish(self):
        v = self.terms[self.me.at(self.axis)]
        for n, hop in enumerate(self.hops()):
            hop.wait_recv()
            v = v + self.got[n]
        self.out[...] = v

    def drain(self):
        for hop in self.hops():
            hop.wait_send()


class GainSum:
    def __init__(self, me, total, got, send, recv):
        self.me, self.total, self.got, self.send, self.recv = me, total, got, send, recv

    def hops(self, s):
        me = self.me
        if s == 3:
            devices = (me.device(),)
        else:
            axis = "xyz"[s]
            devices = tuple(me.device(axis, j) for j in (me.right(axis), me.left(axis), me.over(axis)))
        return [
            pltpu.make_async_remote_copy(
                src_ref=self.total.at[s], dst_ref=self.got.at[3 * s + n], send_sem=self.send.at[3 * s + n],
                recv_sem=self.recv.at[3 * s + n], device_id=device, device_id_type=MESH)
            for n, device in enumerate(devices)
        ]

    def start(self, s):
        for hop in self.hops(s):
            hop.start()

    def finish(self, s):
        v = self.total[s]
        for n, hop in enumerate(self.hops(s)):
            hop.wait_recv()
            v = v + self.got[3 * s + n]
        self.total[s + 1] = v

    def drain(self):
        for s in range(4):
            for hop in self.hops(s):
                hop.wait_send()


def reduce_scratch():
    sem = pltpu.SemaphoreType.DMA
    return [
        pltpu.VMEM((3, 6, 8, 96, 128), BF), pltpu.VMEM((3, 6, 8, 96, 128), BF),
        pltpu.VMEM((3, 6, 2, 96, 128), BF), pltpu.VMEM((3, 6, 2, 96, 128), BF),
        pltpu.VMEM((3, 3, 96, 128), F32),
        pltpu.VMEM((3, 4, 4, 96, 128), F32),
        pltpu.VMEM((3, 4, 96, 128), F32),
        pltpu.VMEM((2, 3, 96, 128), F32),
        pltpu.VMEM((5, 16, 128), F32), pltpu.VMEM((10, 16, 128), F32),
        sem((54,)), sem((54,)), sem((11,)), sem((11,)),
        pltpu.VMEM((3, 4, 4, 4, 96, 128), F32),
        pltpu.VMEM((1536, 384), F32), pltpu.VMEM((3, 768, 256), F32),
    ]


def reduce_stages(me, half, scratch):
    s1, d1, s2, d2, d3, t1, t2, fin, gt, gg, send, recv = scratch[:12]

    def load1(c):
        axis = ORDERS[c][0]

        def load(j, p, m):
            a, b = 2 * p + m // 4, lax.rem(m, 4)
            at = {"x": (a, b, j), "y": (j, a, b), "z": (a, j, b)}[axis]
            return half[(c,) + at]
        return load

    def out1(c):
        def out(p, m, v):
            t1[c, 2 * p + m // 4, lax.rem(m, 4)] = v
        return out

    def load2(c):
        def load(j, p, m):
            return t1[c, 2 * p + m, j] if c == 2 else t1[c, j, 2 * p + m]
        return load

    def out2(c):
        def out(p, m, v):
            t2[c, 2 * p + m] = v
        return out

    stages, base = [], 0
    for c in range(3):
        row = []
        for n, (load, out, bufs, count) in enumerate(
            ((load1, out1, (s1, d1), 8), (load2, out2, (s2, d2), 2))
        ):
            row.append(ReduceStage(me, ORDERS[c][n], load(c), count, out(c), (bufs[0].at[c], bufs[1].at[c]), (send, recv), base))
            base += 6
        row.append(LastStage(me, ORDERS[c][2], t2.at[c], d3.at[c], fin.at[me.core, c], (send, recv), base))
        base += 6
        stages.append(row)
    return stages


def out_terms(refs, scratch, core, c):
    ct, masked, prod_o = refs[1], refs[5], scratch[16]
    columns = pl.ds(pl.multiple_of(core * 768 + c * 256, 128), 256)
    prod_o[c] = dot(ct[...], masked[:, columns])


def weight_terms(refs, scratch, core, c):
    nt, _, gq, gk, gv, _ = refs
    half, prod, prod_o = scratch[14:17]
    columns = pl.ds(pl.multiple_of(core * 384 + c * 128, 128), 128)
    rhs = jnp.concatenate([gq[:, columns], gk[:, columns], gv[:, columns]], 1)
    prod[...] = dot(nt[...], rhs)

    @pl.loop(0, 32)
    def _(pair):
        upper = lax.broadcasted_iota(jnp.int32, (8, 128), 0) < 4
        at = pl.multiple_of(pair * 24, 8)
        tiles = [[prod_o[c, pl.ds(at + 8 * n, 8), pl.ds(128 * b, 128)] for b in range(2)] for n in range(3)]
        mixed = (
            jnp.where(upper, tiles[1][0], pltpu.roll(tiles[1][1], 4, 0)),
            jnp.where(upper, pltpu.roll(tiles[1][0], 4, 0), tiles[1][1]),
        )
        yh, z, yl, xh = pair // 16, lax.rem(pair // 4, 4), lax.rem(pair // 2, 2), lax.rem(pair, 2)
        for odd in range(2):
            rows = pl.ds(pl.multiple_of(pair * 48 + 24 * odd, 8), 24)
            parts = [prod[rows, pl.ds(128 * n, 128)] for n in range(3)]
            parts += [tiles[2 * odd][0], tiles[2 * odd][1], mixed[odd]]
            half[c, yh * 2 + yl, z, xh * 2 + odd] = jnp.concatenate(parts, 0)


def grad_normed(w, gq, gk, gv, out):
    for s in range(4):
        total = None
        for n, g in enumerate((gq, gk, gv)):
            term = dot(g[:256], pair_rows(w, s, n), ROWS)
            total = term if total is None else total + term
        for b in range(3 * s, 3 * s + 3):
            out[b // 2, b % 2] = total[:, 128 * (b - 3 * s):128 * (b - 3 * s) + 128]


def norm_backward(frames, cotangent, gain, gn, grad_frames, gain_total):
    gain_total[0] = jnp.zeros((16, 128), F32)

    @pl.loop(0, 8)
    def _(n):
        rows = pl.ds(pl.multiple_of(n * 32, 32), 32)
        xhat, inverse = norm(frames[rows])
        grad = jnp.concatenate([gn[b // 2, b % 2, rows] for b in range(12)], 1)
        gx = grad * xhat
        for b in range(12):
            gain_total[0, b:b + 1] += jnp.sum(gx[:, 128 * b: 128 * b + 128], 0, keepdims=True)
        g = grad * gain[...]
        first = jnp.mean(g, -1, keepdims=True)
        second = jnp.mean(gx * gain[...], -1, keepdims=True)
        back = inverse * (g - first - xhat * second)
        grad_frames[rows] = (cotangent[rows].astype(F32) + back).astype(BF)


def project_out(w, ctx, frames, length, out):
    base = lax.axis_index("tm") * 256
    for b in range(2):
        attn = dot(ctx[:, :384], out_rows(w, 0, b)) + dot(ctx[:, 384:], out_rows(w, 1, b))
        lanes = pl.ds(768 * b, 768)
        frame = base + lax.broadcasted_iota(jnp.int32, (256, 768), 0)
        out[:, lanes] = (frames[:, lanes].astype(F32) + jnp.where(frame < length, attn, 0.0)).astype(BF)


def block_kernel(
    wq, wk, wv, wo, frames_hbm, cotangent_hbm, gain_hbm, lengths, lo_hbm, hi_hbm,
    total, gain_out, grad_frames_hbm, frames_out_hbm,
    nt, ct, ctx, gq, gk, gv, masked, frames, cotangent, gain, lo, hi, grad_frames, frames_out,
    held, w, nm, q6, gc6, kv, center, bias, rim_s, rim_r, send, recv, local, ring_send, ring_recv, twin_send, twin_recv, *scratch
):
    me = Place()
    length = lengths[0]
    base = lax.axis_index("tm") * 256
    loads = ((frames_hbm, frames), (gain_hbm, gain), (cotangent_hbm, cotangent), (lo_hbm, lo), (hi_hbm, hi))
    loads = [pltpu.make_async_copy(src, dst, local.at[6 + n]) for n, (src, dst) in enumerate(loads)]
    for copy in loads:
        copy.start()
    rows = start_gather(me, (wq, wk, wv, wo), held, w, send, recv, local)

    def twin(n):
        across = lambda width: pl.ds(pl.multiple_of((1 - me.core) * width, 128), width)
        ref = (nt, masked, ct, gq, gk, gv)[n]
        if n in (0, 2):
            src, dst = ref.at[:, pl.ds(0, 256)], ref.at[:, pl.ds(256, 256)]
        else:
            lanes = across(768 if n == 1 else 384)
            src, dst = ref.at[pl.ds(0, 256), lanes], ref.at[pl.ds(256, 256), lanes]
        return pltpu.make_async_remote_copy(
            src_ref=src, dst_ref=dst, send_sem=twin_send.at[n], recv_sem=twin_recv.at[n],
            device_id=me.device(), device_id_type=MESH)

    def normalize():
        for copy in loads:
            copy.wait()

        @pl.loop(0, 8)
        def _(n):
            at = pl.ds(pl.multiple_of(n * 32, 32), 32)
            xhat, _ = norm(frames[at])
            nm[at] = (xhat * gain[...]).astype(BF)

    def prepare():
        nt[:, :256] = nm[...].T
        twin(0).start()

        @pl.loop(0, 8)
        def _(n):
            at = pl.ds(pl.multiple_of(n * 32, 32), 32)
            frame = base + n * 32 + lax.broadcasted_iota(jnp.int32, (32, 1536), 0)
            masked[at] = jnp.where(frame < length, cotangent[at].astype(F32), 0.0).astype(BF)
        twin(1).start()

        for b in range(2):
            kp = base + 128 * (b - 1) + lax.broadcasted_iota(jnp.int32, (384, 128), 0)
            qp = base + 128 * b + lax.broadcasted_iota(jnp.int32, (384, 128), 1)
            cols = pl.ds(128 * b, 128)
            seen = (kp >= lo[:, cols]) & (kp < hi[:, cols]) & (kp < length)
            bias[b] = jnp.where(seen | (kp == qp), 0.0, -1e30)

    finish_gather(rows, normalize, prepare)

    def project(n):
        total = None
        for i in range(4):
            term = dot(nm[:, 384 * i:384 * i + 384], pair_rows(w, i, n))
            total = term if total is None else total + term
        return total.astype(BF)

    def halo(p, right):
        src, dst, by = (256, 0, 1) if right else (128, 384, 15)
        n = 2 * p + right
        return pltpu.make_async_remote_copy(
            src_ref=kv.at[p, :, pl.ds(src, 128)], dst_ref=kv.at[p, :, pl.ds(dst, 128)],
            send_sem=ring_send.at[n], recv_sem=ring_recv.at[n], device_id=me.along(by), device_id_type=MESH)

    def rim(p, right):
        n = 12 + 2 * p + right
        return pltpu.make_async_remote_copy(
            src_ref=rim_s.at[p, right], dst_ref=rim_r.at[p, right],
            send_sem=ring_send.at[n], recv_sem=ring_recv.at[n], device_id=me.along(1 if right else 15), device_id_type=MESH)

    for m in range(2):
        k = project(1 + m)
        for p in range(6):
            kv[p, m, 128:384] = k[:, 128 * p:128 * p + 128]
    for p in range(6):
        for right in range(2):
            halo(p, right).start()
    q = project(0)
    for p in range(6):
        q6[p] = q[:, 128 * p:128 * p + 128]
    for yh in range(2):
        g = (dot(masked[:256, :768], out_rows(w, yh, 0), ROWS) + dot(masked[:256, 768:], out_rows(w, yh, 1), ROWS)).astype(BF)
        for n in range(3):
            gc6[3 * yh + n] = g[:, 128 * n:128 * n + 128]

    @pl.loop(0, 6)
    def _(p):
        for right in range(2):
            halo(p, right).wait_recv()
        first = (lax.broadcasted_iota(jnp.int32, (128, 128), 1) < 64).astype(F32)
        even, odd = first.astype(BF), (1.0 - first).astype(BF)
        lanes = pl.ds(pl.multiple_of(128 * p, 128), 128)
        grads = []
        for b in range(2):
            at = pl.ds(128 * b, 128)
            q = q6[p, at]
            g = gc6[p, at]
            qm = jnp.concatenate([q * even, q * odd], 0)
            gm = jnp.concatenate([g * even, g * odd], 0)
            key = kv[p, 0, pl.ds(128 * b, 384)]
            value = kv[p, 1, pl.ds(128 * b, 384)]
            s = dot(key, qm, ROWS) * 0.125 + jnp.concatenate([bias[b], bias[b]], 1)
            e = jnp.exp(s - jnp.max(s, 0, keepdims=True))
            probs = e * (1.0 / jnp.sum(e, 0, keepdims=True))
            low = probs.astype(BF)
            grad = dot(value, gm, ROWS)
            delta = jnp.sum(probs * grad, 0, keepdims=True)
            ds = (probs * (grad - delta)).astype(BF)
            c = dot(value.T, low)
            c = jnp.concatenate([c[:64, :128], c[64:, 128:]], 0)
            ct[lanes, at] = c.astype(BF)
            ctx[at, lanes] = c.T.astype(BF)
            d = dot(key.T, ds)
            d = jnp.concatenate([d[:64, :128], d[64:, 128:]], 0) * 0.125
            gq[at, lanes] = d.T.astype(BF)
            grads.append((dot(ds, qm) * 0.125, dot(low, gm)))
        for m in range(2):
            here, there = grads[0][m], grads[1][m]
            rim_s[p, 0, m] = here[:128].astype(BF)
            rim_s[p, 1, m] = there[256:].astype(BF)
            center[p, m] = here[128:] + there[:256]
        for right in range(2):
            rim(p, right).start()

    twin(2).start()
    twin(3).start()
    for p in range(6):
        for right in range(2):
            rim(p, right).wait_recv()
        for m, out in enumerate((gk, gv)):
            lanes = pl.ds(128 * p, 128)
            out[:128, lanes] = (center[p, m, :128] + rim_r[p, 1, m].astype(F32)).astype(BF)
            out[128:256, lanes] = (center[p, m, 128:] + rim_r[p, 0, m].astype(F32)).astype(BF)

    twin(4).start()
    twin(5).start()
    fin, gt, gg = scratch[7:10]
    gsend, grecv, half = scratch[12:15]
    refs = (nt, ct, gq, gk, gv, masked)
    stages = reduce_stages(me, half, scratch)
    sum_gain = GainSum(me, gt, gg, gsend, grecv)

    for n in range(3):
        twin(n).wait_recv()
    for c in range(3):
        out_terms(refs, scratch, me.core, c)
    for n in range(3, 6):
        twin(n).wait_recv()
    for c in range(3):
        weight_terms(refs, scratch, me.core, c)
        stages[c][0].start()
    grad_normed(w, gq, gk, gv, center)
    for c in range(3):
        stages[c][0].relay()
    norm_backward(frames, cotangent, gain, center, grad_frames, gt)
    stores = [
        pltpu.make_async_copy(grad_frames, grad_frames_hbm, local.at[11]),
        pltpu.make_async_copy(frames_out, frames_out_hbm, local.at[12]),
    ]
    stores[0].start()
    sum_gain.start(0)
    project_out(w, ctx, frames, length, frames_out)
    stores[1].start()
    for n in range(3):
        for c in range(3):
            stages[c][n].finish()
            if n < 2:
                stages[c][n + 1].start()
        sum_gain.finish(n)
        sum_gain.start(n + 1)
        if n < 2:
            for c in range(3):
                stages[c][n + 1].relay()

    def last(core):
        return pltpu.make_async_remote_copy(
            src_ref=fin.at[core], dst_ref=fin.at[core], send_sem=gsend.at[10], recv_sem=grecv.at[10],
            device_id=me.device(), device_id_type=MESH)

    last(me.core).start()
    sum_gain.finish(3)
    gain_out[...] = gt[4]
    for c in range(3):
        for n in range(3):
            stages[c][n].drain()
    sum_gain.drain()
    for n in range(6):
        twin(n).wait_send()
    last(me.core).wait_send()
    last(1 - me.core).wait_recv()
    total[...] = fin[...]
    for p in range(6):
        for right in range(2):
            halo(p, right).wait_send()
            rim(p, right).wait_send()
    for row in rows:
        for stage in row:
            stage.drain()
    for copy in stores:
        copy.wait()


def block(wq, wk, wv, wo, *args):
    vm, hbm = pl.BlockSpec(memory_space=pltpu.VMEM), pl.BlockSpec(memory_space=pltpu.HBM)
    sds, sem = jax.ShapeDtypeStruct, pltpu.SemaphoreType.DMA
    return pl.pallas_call(
        block_kernel,
        out_shape=(sds((2, 3, 96, 128), F32), sds((16, 128), F32), sds((256, 1536), BF), sds((256, 1536), BF)),
        in_specs=[hbm] * 7 + [pl.BlockSpec(memory_space=pltpu.SMEM)] + [hbm] * 2,
        out_specs=(vm, vm, hbm, hbm),
        scratch_shapes=[
            pltpu.VMEM((1536, 512), BF), pltpu.VMEM((768, 512), BF), pltpu.VMEM((256, 768), BF),
            pltpu.VMEM((512, 768), BF), pltpu.VMEM((512, 768), BF), pltpu.VMEM((512, 768), BF),
            pltpu.VMEM((512, 1536), BF), pltpu.VMEM((256, 1536), BF), pltpu.VMEM((256, 1536), BF),
            pltpu.VMEM((1, 1536), F32), pltpu.VMEM((1, 256), jnp.int32), pltpu.VMEM((1, 256), jnp.int32),
            pltpu.VMEM((256, 1536), BF), pltpu.VMEM((256, 1536), BF),
            pltpu.VMEM((48, 16, 768), BF),
            pltpu.VMEM((2, 4, 2, 3, 2, 4, 16, 768), BF),
            pltpu.VMEM((256, 1536), BF),
            pltpu.VMEM((6, 256, 128), BF), pltpu.VMEM((6, 256, 128), BF),
            pltpu.VMEM((6, 2, 512, 128), BF),
            pltpu.VMEM((6, 2, 256, 128), F32),
            pltpu.VMEM((2, 384, 128), F32),
            pltpu.VMEM((6, 2, 2, 128, 128), BF), pltpu.VMEM((6, 2, 2, 128, 128), BF),
            sem((GATHER_SEMS,)), sem((GATHER_SEMS,)), sem((15,)), sem((24,)), sem((24,)), sem((6,)), sem((6,)),
        ] + reduce_scratch(),
        compiler_params=pltpu.CompilerParams(collective_id=0, has_side_effects=True, vmem_limit_bytes=67043328),
        name="block",
    )(wq.reshape(12, 16, 768), wk.reshape(12, 16, 768), wv.reshape(12, 16, 768), wo.reshape(6, 16, 1536), *args)


def outputs_kernel(total, gain, grad_in, frames_in, out_q, out_k, out_v, out_o, out_gain, grad_frames, frames_out):
    me = Place()
    frames_out[...] = frames_in[...]
    grad_frames[...] = grad_in[...]
    odd = lax.rem(me.x, 2)
    for h in range(2):
        for c in range(3):
            lanes = pl.ds(384 * h + 128 * c, 128)
            for n, out in enumerate((out_q, out_k, out_v)):
                t = total[h, c, pl.ds(24 * n, 24)]
                out[:, lanes] = jnp.where(me.core == 0, t[:12], t[12:])
            for b in range(2):
                lanes = pl.ds(768 * h + 256 * c + 128 * b, 128)
                for r in range(6):
                    even0, even1 = 8 * b + r, 8 * b + 6 + r if r < 2 else 14 + 4 * b + r
                    odd0, odd1 = 16 + 4 * b + r if r < 4 else 8 * b + r - 4, 8 * b + 2 + r
                    row = 72 + jnp.where(
                        odd == 0, jnp.where(me.core == 0, even0, even1), jnp.where(me.core == 0, odd0, odd1))
                    out_o[r:r + 1, lanes] = total[h, c, pl.ds(row, 1)]
    at = (lax.axis_index("dp") * 16 + lax.axis_index("tm")) * 12
    row, lane = at // 128, lax.rem(at, 128)
    both = jnp.concatenate([gain[pl.ds(row, 1)], gain[pl.ds(row + 1, 1)]], 1)
    both = jnp.broadcast_to(both, (8, 256))
    out_gain[...] = pltpu.roll(both, lax.rem(256 - lane, 256), 1)[:1, :12]


def write_outputs(*args):
    vm = pl.BlockSpec(memory_space=pltpu.VMEM)
    sds = jax.ShapeDtypeStruct
    return pl.pallas_call(
        outputs_kernel,
        out_shape=(sds((12, 768), F32),) * 3 + (
            sds((6, 1536), F32), sds((1, 12), F32), sds((256, 1536), BF), sds((256, 1536), BF)),
        in_specs=[vm] * 4,
        out_specs=(vm,) * 7,
        name="write_outputs",
    )(*args)


def per_device(
    frames, cotangent, layer_norm_gain, w_query, w_key, w_value, w_out, lengths, win_lo, win_hi
):
    gain = layer_norm_gain[None]
    sums = block(
        w_query, w_key, w_value, w_out, frames[0], cotangent[0], gain, lengths, win_lo, win_hi)
    grad_wq, grad_wk, grad_wv, grad_wo, grad_gain, grad_frames, frames_out = write_outputs(*sums)
    return (frames_out[None], grad_frames[None], grad_wq, grad_wk, grad_wv, grad_wo, grad_gain.reshape(12))


def solution(mesh):
    in_specs = (
        P("dp", "tm", None),
        P("dp", "tm", None),
        P(),
        P("dp", None),
        P("dp", None),
        P("dp", None),
        P("dp", None),
        P("dp"),
        P("dp", "tm"),
        P("dp", "tm"),
    )
    out_specs = (
        P("dp", "tm", None),
        P("dp", "tm", None),
        P(("dp", "tm"), None),
        P(("dp", "tm"), None),
        P(("dp", "tm"), None),
        P(("dp", "tm"), None),
        P(("dp", "tm")),
    )
    return jax.shard_map(
        per_device, mesh=mesh, in_specs=in_specs, out_specs=out_specs, check_vma=False
    )
```
